256 devices in a mesh: slab: 64 (over y, x, z_lo, core), atom: 4 (over z_hi).
Axes of the slice: x: 4, y: 4, z: 8 (z_hi: 4, z_lo: 2; z = z_hi * 2 + z_lo), core: 2. Of those that a mesh axis runs over, the one named last changes fastest.
Arguments:
- cells: int32 [3, 4096, 512], P(None, 'slab', 'atom'), may hold values from 0 to 255, as said below
- fractions: float32 [3, 4096, 512], P(None, 'slab', 'atom'), may hold values from 0 to 1
- charges: float32 [4096, 512], P('slab', 'atom'), may hold values from -3 to 3
- counts: int32 [4096, 4], P('slab', 'atom'), may hold values from 1 to 128, as said below
- box: float32 [3], replicated, may hold values from 192 to 243.2
Outputs:
- kfield: float32 [2, 256, 256, 256], P(None, 'slab', 'atom')
- totals: float32 [7], replicated
The draws below stay inside these ranges and needn't reach their ends.
Inputs may be any that keep to these rules, and one draw needn't show every extreme that they name: `cells`: for row r (tile r mod 64 of slab r div 64) every slot's z cell lies in the 4 planes from (r div 64) * 4 and its y cell in the 4 rows from (r mod 64) * 4; x anywhere. `counts`: live slots are the first ones of a tile's 128; some tile is full in every draw.
All inputs are finite; a program needn't handle non-finite values.
Results may differ from the reference program's by a relative error of at most 0.000078.
Values sent between devices are 32-bit elements; how exact they have to be, the bound alone decides.
A program may use at most 64 MiB of HBM per device.

```python
import math
import jax
import jax.numpy as jnp
from jax import lax

K = 256
TILES = 64
SLOTS = 128
DZ = 4
TY = 4
ROWS = 4096
COLS = 512


def draw_cells(key, part):
    keys = jax.random.split(jax.random.fold_in(key, 11), 3)
    row_ids = jnp.arange(ROWS, dtype=jnp.int32)[:, None]
    zcell = row_ids // TILES * DZ + jax.random.randint(keys[0], (ROWS, COLS), 0, DZ)
    ycell = row_ids % TILES * TY + jax.random.randint(keys[1], (ROWS, COLS), 0, TY)
    xcell = jax.random.randint(keys[2], (ROWS, COLS), 0, K)
    return jnp.stack([zcell, ycell, xcell]).astype(jnp.int32)


def draw_counts(key, part):
    first, second = jax.random.split(jax.random.fold_in(key, 23))
    shards = COLS // SLOTS
    filled = jax.random.randint(first, (ROWS * shards,), 1, SLOTS + 1)
    where = jax.random.randint(second, (), 0, ROWS * shards)
    filled = filled.at[where].set(SLOTS)
    return filled.reshape(ROWS, shards).astype(jnp.int32)


def block_levels(stream_key, shape, cuts, smallest, top_value):
    factor_of = 1.0
    for axis_at, parts in cuts:
        heights = jax.random.uniform(jax.random.fold_in(jax.random.fold_in(stream_key, 6), axis_at), (parts,), jnp.float32, smallest / len(cuts), top_value / len(cuts))
        factor_of = factor_of * jnp.repeat(jnp.exp(heights), shape[axis_at] // parts).reshape((-1,) + (1,) * (len(shape) - 1 - axis_at))
    return factor_of


def scatter_about(key, extent, spread, most, cuts=(), kind=jnp.bfloat16):
    loudness = block_levels(key, extent, cuts, -0.22, 0.18) if cuts else 1.0
    entries = jax.random.normal(key, extent, jnp.float32) * spread * loudness
    return jnp.minimum(jnp.maximum(entries, -most), most).astype(kind)


def setup_inputs(seed: int = 0) -> dict:
    arg_keys = jax.random.split(jax.random.key(seed), 6)
    cells = draw_cells(jax.random.fold_in(arg_keys[5], 71), 0)
    fractions = jnp.clip(1.0 * jax.random.uniform(arg_keys[1], (3, ROWS, COLS), jnp.float32) ** block_levels(arg_keys[1], (3, ROWS, COLS), ((1, 64), (2, 4)), -0.2, 0.2), 0.0, 1.0)
    charges = scatter_about(arg_keys[2], (ROWS, COLS), 0.5, 3.0, ((0, 64), (1, 4)), jnp.float32)
    counts = draw_counts(jax.random.fold_in(arg_keys[5], 71), 0)
    box = jnp.clip(jax.random.uniform(arg_keys[4], (3,), jnp.float32, 192.0, 243.2), 192.0, 243.2)
    return dict(cells=cells, fractions=fractions, charges=charges, counts=counts, box=box)


ewald_beta = 1.25


def spline_weights(frac):
    prior = [jnp.ones_like(frac)]
    for order in range(2, 7):
        nxt = []
        for i in range(order):
            point = frac + i
            here = prior[i] if i < order - 1 else jnp.zeros_like(frac)
            lower = prior[i - 1] if i > 0 else jnp.zeros_like(frac)
            nxt.append((point * here + (order - point) * lower) / (order - 1))
        prior = nxt
    return prior


def moduli(index):
    angle = (index % K).astype(jnp.float32) * (2.0 * math.pi / K)
    denom = 66.0 + 52.0 * jnp.cos(angle) + 2.0 * jnp.cos(2.0 * angle)
    return (120.0 / denom) ** 2


def reference(cells, fractions, charges, counts, box):
    rows, cols = charges.shape
    column = jnp.arange(cols, dtype=jnp.int32)
    limit = counts[:, column // SLOTS]
    live = ((column % SLOTS)[None, :] < limit).astype(jnp.float32)
    weight = charges * live
    along_z = jnp.stack(spline_weights(fractions[0]))
    along_y = jnp.stack(spline_weights(fractions[1]))
    along_x = spline_weights(fractions[2])

    def add_pair(pair, flat):
        first = pair // 6
        second = pair % 6
        zcell = (cells[0] + 3 - first) % K
        ycell = (cells[1] + 3 - second) % K
        base = weight * along_z[first] * along_y[second]
        for third in range(6):
            xcell = (cells[2] + 3 - third) % K
            flat = flat.at[(zcell * K + ycell) * K + xcell].add(base * along_x[third])
        return flat

    flat = lax.fori_loop(0, 36, add_pair, jnp.zeros((K * K * K,), jnp.float32))
    spectrum = jnp.fft.fftn(flat.reshape(K, K, K))
    real_part = jnp.transpose(jnp.real(spectrum), (1, 2, 0)).astype(jnp.float32)
    imag_part = jnp.transpose(jnp.imag(spectrum), (1, 2, 0)).astype(jnp.float32)
    index = jnp.arange(K, dtype=jnp.int32)
    folded = jnp.where(index < K // 2, index, index - K).astype(jnp.float32)
    m_z = (folded / box[0])[None, None, :]
    m_y = (folded / box[1])[:, None, None]
    m_x = (folded / box[2])[None, :, None]
    msq = m_z * m_z + m_y * m_y + m_x * m_x
    anchor = (index[:, None, None] == 0) & (index[None, :, None] == 0) & (index[None, None, :] == 0)
    safe = jnp.where(anchor, 1.0, msq)
    volume = box[0] * box[1] * box[2]
    spline_part = moduli(index)[None, None, :] * moduli(index)[:, None, None] * moduli(index)[None, :, None]
    theta = jnp.exp(-(math.pi ** 2) * safe / ewald_beta ** 2) * spline_part / (math.pi * volume * safe)
    theta = jnp.where(anchor, 0.0, theta)
    kfield = jnp.stack([theta * real_part, theta * imag_part])
    half = 0.5 * theta * (real_part * real_part + imag_part * imag_part)
    factor = 2.0 * (1.0 + (math.pi ** 2) * safe / ewald_beta ** 2) / safe
    count = rows * cols
    totals = jnp.stack([
        jnp.sum(half),
        jnp.sum(half * (1.0 - factor * m_z * m_z)),
        jnp.sum(half * (1.0 - factor * m_y * m_y)),
        jnp.sum(half * (1.0 - factor * m_x * m_x)),
        jnp.sum(half * (-factor * m_z * m_y)),
        jnp.sum(half * (-factor * m_z * m_x)),
        jnp.sum(half * (-factor * m_y * m_x)),
    ]) / count
    return kfield, totals
```

```python
import functools
import math

import jax
import jax.numpy as jnp
import numpy as np
from jax import lax
from jax.experimental import pallas as pl
from jax.experimental.pallas import tpu as pltpu
from jax.sharding import PartitionSpec as P

K = 256
TILES = 64
SLOTS = 128
SLABS = 64
SHARDS = 4
DZ = 4
QUARTER = 64
MAIN = 16
PLANES = 9
ROWS = 88
SHIFT = 10
LANES = SHARDS * SLOTS
beta = 1.25
F32 = jnp.float32
BF16 = jnp.bfloat16
MESH = pl.DeviceIdType.MESH


def tables():
    index = np.arange(K)
    angle = (index[:, None] * index[None, :] % K) * (2.0 * np.pi / K)
    cosine, sine = np.cos(angle), np.sin(angle)
    plain = np.concatenate([cosine, sine], axis=1)
    blocks = []
    for shard in range(SHARDS):
        cols = slice(shard * QUARTER, (shard + 1) * QUARTER)
        blocks += [cosine[:, cols], -sine[:, cols]]
    ordered = np.concatenate(blocks, axis=1)

    def halves(x):
        high = x.astype(np.float32).astype(jnp.bfloat16)
        low = (x - high.astype(np.float64)).astype(np.float32).astype(jnp.bfloat16)
        return np.stack([high, low])

    turn = 2.0 * np.pi * index / K
    modulus = (120.0 / (66.0 + 52.0 * np.cos(turn) + 2.0 * np.cos(2.0 * turn))) ** 2
    folded = np.where(index < K // 2, index, index - K)
    along_rows = np.zeros((K, 128), np.float32)
    along_rows[:, 0] = modulus
    along_rows[:, 1] = folded
    along_lanes = np.zeros((8, K), np.float32)
    along_lanes[0] = modulus
    along_lanes[1] = folded
    return halves(ordered), halves(plain), along_rows, along_lanes


def spline_weights(frac):
    prior = [jnp.ones_like(frac)]
    for order in range(2, 7):
        nxt = []
        for i in range(order):
            point = frac + i
            if i == 0:
                value = point * prior[0]
            elif i == order - 1:
                value = (order - point) * prior[i - 1]
            else:
                value = point * prior[i] + (order - point) * prior[i - 1]
            nxt.append(value * (1.0 / (order - 1)))
        prior = nxt
    return prior


def halved(x):
    high = x.astype(BF16)
    low = (x - high.astype(F32)).astype(BF16)
    return high, low


def dot(a, b):
    return jnp.dot(a, b, preferred_element_type=F32)


def dot_lanes(a, b):
    return lax.dot_general(a, b, (((1,), (1,)), ((), ())), preferred_element_type=F32)


def kernel(
    cells, fractions, charges, counts, box, tx_hbm, t_hbm, rows_const, lanes_const,
    kfield, totals,
    tx, t, send_atoms, atoms, splines, window, x_high, x_low, grid, planes, from_below, from_above,
    x_out, x_in, y_out, z_in, result, part, parts, middle, middles,
    table_sem, atom_send, atom_recv, halo_send, halo_recv, x_send, x_recv,
    y_send, y_recv, out_sem, sum_send, sum_recv, mid_send, mid_recv,
):
    slab = lax.axis_index("slab")
    atom = lax.axis_index("atom")

    barrier = pltpu.get_barrier_semaphore()
    for step in range(1, SHARDS):
        pl.semaphore_signal(barrier, inc=1, device_id=(slab, lax.rem(atom + step, SHARDS)), device_id_type=MESH)

    def greet(step, carry):
        pl.semaphore_signal(barrier, inc=1, device_id=(lax.rem(slab + step, SLABS), atom), device_id_type=MESH)
        return carry

    lax.fori_loop(1, SLABS, greet, 0)
    load_tx = pltpu.make_async_copy(tx_hbm, tx, table_sem.at[0])
    load_t = pltpu.make_async_copy(t_hbm, t, table_sem.at[1])
    load_tx.start()
    load_t.start()

    slot = lax.broadcasted_iota(jnp.int32, (TILES, SLOTS), 1)
    weight = jnp.where(slot < counts[...], charges[...], 0.0)
    fields = [cells[d].astype(F32) for d in range(3)] + [fractions[d] for d in range(3)] + [weight]
    for shard in range(SHARDS):
        edge = []
        for number, field in enumerate(fields):
            first = shard * MAIN
            send_atoms[shard, number] = field[first : first + MAIN]
            after = (first + MAIN) % TILES
            before = (first - 1) % TILES
            edge += [field[after : after + 1], field[before : before + 1]]
        edge += [jnp.zeros((2, SLOTS), F32)]
        send_atoms[shard, 7] = jnp.concatenate(edge, axis=0)
    pl.semaphore_wait(barrier, SHARDS - 1 + SLABS - 1)

    def atom_copy(step):
        peer = lax.rem(atom + step, SHARDS)
        return pltpu.make_async_remote_copy(
            src_ref=send_atoms.at[peer], dst_ref=atoms.at[atom],
            send_sem=atom_send.at[step], recv_sem=atom_recv.at[SHARDS - step],
            device_id=(slab, peer), device_id_type=MESH,
        )

    for step in (2, 1, 3):
        atom_copy(step).start()
    atoms[atom] = send_atoms[atom]
    grid[...] = jnp.zeros_like(grid)
    for step in (1, 3, 2):
        atom_copy(step).wait_recv()

    def gathered(number):
        main = jnp.concatenate([atoms[shard, number] for shard in range(SHARDS)], axis=1)
        edge = jnp.concatenate([atoms[shard, 7, 2 * number : 2 * number + 2] for shard in range(SHARDS)], axis=1)
        return jnp.concatenate([main, edge, jnp.zeros((6, LANES), F32)], axis=0)

    weights = gathered(6)
    for d in range(3):
        for i, value in enumerate(spline_weights(gathered(3 + d))):
            splines[6 * d + i] = value * weights if d == 0 else value
    for d in range(2):
        cell = gathered(d)
        splines[18 + d] = cell - 4.0 * jnp.floor(cell * 0.25) + 5.0
    first = gathered(2) - 2.0
    first = jnp.where(first < 0.0, first + K, first)
    block = jnp.floor(first * (1.0 / 16.0))
    splines[20] = block
    splines[21] = first - 16.0 * block

    row16 = lax.broadcasted_iota(jnp.int32, (16, LANES), 0).astype(F32)
    row24 = lax.broadcasted_iota(jnp.int32, (24, LANES), 0).astype(F32)

    def spread(step, carry):
        tile = step - 1
        at = lax.rem(step + 17, 18)
        base = pl.multiple_of(((step + 1) // 2) * 8, 8)
        offset = (4 * lax.rem(step + 1, 2)).astype(F32)

        def row(number):
            return splines[number, pl.ds(at, 1), :]

        near_z = row(18) - row16
        near_y = (row(19) + offset) - row16
        table_z = jnp.zeros((16, LANES), F32)
        table_y = jnp.zeros((16, LANES), F32)
        for i in range(6):
            table_z = jnp.where(near_z == i, row(i), table_z)
            table_y = jnp.where(near_y == i, row(6 + i), table_y)
        for p in range(PLANES):
            high, low = halved(table_z[p : p + 1] * table_y)
            window[p * 16 : (p + 1) * 16] = high
            window[PLANES * 16 + p * 16 : PLANES * 16 + (p + 1) * 16] = low
        past = row24 - row(21)
        small = jnp.zeros((24, LANES), F32)
        for j in range(6):
            small = jnp.where(past == j, row(12 + 5 - j), small)
        high = small.astype(BF16).astype(F32)
        low = small - high
        where_block = row(20)
        for b in range(16):
            here = where_block == b
            prior = where_block == (b - 1) % 16
            for source, target in ((high, x_high), (low, x_low)):
                top = jnp.where(here, source[0:8], jnp.where(prior, source[16:24], 0.0))
                bottom = jnp.where(here, source[8:16], 0.0)
                target[b * 16 : (b + 1) * 16] = jnp.concatenate([top, bottom], axis=0).astype(BF16)
        double = dot_lanes(window[...], x_high[...])
        single = dot_lanes(window[0 : PLANES * 16], x_low[...])
        out = double[0 : PLANES * 16] + double[PLANES * 16 :] + single
        out = out.reshape(PLANES, 16, K)
        grid[:, pl.ds(base, 16), :] += out
        return carry

    lax.fori_loop(0, 18, spread, 0)

    planes[...] = grid[:, SHIFT : SHIFT + QUARTER, :]
    above = lax.rem(slab + 1, SLABS)
    below = lax.rem(slab + SLABS - 1, SLABS)
    up = pltpu.make_async_remote_copy(
        src_ref=planes.at[pl.ds(6, 3)], dst_ref=from_below,
        send_sem=halo_send.at[0], recv_sem=halo_recv.at[0], device_id=(above, atom), device_id_type=MESH,
    )
    down = pltpu.make_async_remote_copy(
        src_ref=planes.at[pl.ds(0, 2)], dst_ref=from_above,
        send_sem=halo_send.at[1], recv_sem=halo_recv.at[1], device_id=(below, atom), device_id_type=MESH,
    )
    up.start()
    down.start()
    load_tx.wait()
    load_t.wait()

    def x_copy(half, step):
        peer = lax.rem(atom + step, SHARDS)
        return pltpu.make_async_remote_copy(
            src_ref=x_out.at[half, peer], dst_ref=x_in.at[half, atom],
            send_sem=x_send.at[half, step], recv_sem=x_recv.at[half, SHARDS - step],
            device_id=(slab, peer), device_id_type=MESH,
        )

    for half in range(2):
        if half == 0:
            up.wait_recv()
            real = jnp.concatenate([planes[2] + from_below[0], planes[3] + from_below[1]], axis=0)
        else:
            down.wait_recv()
            real = jnp.concatenate([planes[4] + from_below[2] + from_above[0], planes[5] + from_above[1]], axis=0)
        high, low = halved(real)
        out = dot(high, tx[0]) + dot(low, tx[0]) + dot(high, tx[1])
        for shard in range(SHARDS):
            x_out[half, shard] = out[:, shard * 128 : (shard + 1) * 128].reshape(2, QUARTER, 128)
        for step in (2, 1, 3):
            x_copy(half, step).start()
        x_in[half, atom] = x_out[half, atom]

    lane = lax.broadcasted_iota(jnp.int32, (K, 128), 1)
    row8 = lax.broadcasted_iota(jnp.int32, (32, 8, 128), 1)

    def y_copy(half, step):
        peer = lax.rem(slab + step, SLABS)
        return pltpu.make_async_remote_copy(
            src_ref=y_out.at[half, peer // 2, lax.rem(peer, 2)],
            dst_ref=z_in.at[pl.ds(pl.multiple_of(slab * 16 + half * 8, 8), 8)],
            send_sem=y_send.at[half], recv_sem=y_recv.at[half],
            device_id=(peer, atom), device_id_type=MESH,
        )

    for half in range(2):
        for step in (1, 3, 2):
            x_copy(half, step).wait_recv()
        plain, turned = [], []
        for p in range(2):
            f = jnp.concatenate([x_in[half, shard, p] for shard in range(SHARDS)], axis=0)
            g = pltpu.roll(f, 64, 1)
            plain.append(f)
            turned.append(jnp.where(lane < 64, g, -g))
        both = jnp.concatenate([jnp.concatenate(plain, axis=1), jnp.concatenate(turned, axis=1)], axis=0)
        high, low = halved(both)
        out = dot(t[0], high) + dot(t[0], low) + dot(t[1], high)
        y0 = out[:, 0:128].reshape(32, 8, 128)
        y1 = out[:, 128:256].reshape(32, 8, 128)
        y_out[half, :, 0] = jnp.where(row8 < 4, y0, pltpu.roll(y1, 4, 1))
        y_out[half, :, 1] = jnp.where(row8 < 4, pltpu.roll(y0, 4, 1), y1)

        def send(step, carry):
            y_copy(half, step).start()
            return carry

        lax.fori_loop(1, SLABS, send, 0)
        z_in[pl.ds(pl.multiple_of(slab * 16 + half * 8, 8), 8)] = y_out[half, slab // 2, lax.rem(slab, 2)]

    def y_all(half):
        return pltpu.make_async_remote_copy(
            src_ref=z_in.at[pl.ds(0, 8 * (SLABS - 1))], dst_ref=z_in.at[pl.ds(0, 8 * (SLABS - 1))],
            send_sem=y_send.at[half], recv_sem=y_recv.at[half],
            device_id=(above, atom), device_id_type=MESH,
        )

    span_z, span_y, span_x = box[0], box[1], box[2]
    decay = -(math.pi**2) / beta**2
    ones = jnp.ones((8, K), F32)
    m_z = lanes_const[1:2] / (ones[0:1] * span_z)
    part_z = jnp.exp(decay * m_z * m_z) * lanes_const[0:1]
    own_x = rows_const[pl.ds(pl.multiple_of(atom * QUARTER, QUARTER), QUARTER)]
    m_x = own_x[:, 1:2] / (ones[0, 0] * span_x * jnp.ones((QUARTER, 1), F32))
    scale = jnp.ones((QUARTER, 1), F32) / (math.pi * span_z * span_y * span_x * jnp.ones((QUARTER, 1), F32))
    part_x = jnp.exp(decay * m_x * m_x) * own_x[:, 0:1] * scale
    part_xz = part_x * part_z
    msq_xz = m_x * m_x + m_z * m_z
    own_y = rows_const[pl.ds(pl.multiple_of((slab // 2) * 8, 8), 8)]
    kx_at = lax.broadcasted_iota(jnp.int32, (QUARTER, K), 0) + atom * QUARTER
    kz_at = lax.broadcasted_iota(jnp.int32, (QUARTER, K), 1)
    zero_xz = kx_at + kz_at

    for half in range(2):
        y_all(half).wait_recv()

    sums = [jnp.zeros((1, K), F32) for _ in range(7)]
    for ky in range(DZ):
        f = z_in[pl.ds(ky, K, stride=4), :].T
        high, low = halved(f)
        out = dot(high, t[0]) + dot(low, t[0]) + dot(high, t[1])
        real = out[0:QUARTER, 0:K] + out[QUARTER:, K:]
        imag = out[QUARTER:, 0:K] - out[0:QUARTER, K:]
        y_row = jnp.where(lax.rem(slab, 2) == 0, own_y[ky : ky + 1], own_y[ky + 4 : ky + 5])
        m_y = y_row[:, 1:2] / (jnp.ones((1, 1), F32) * span_y)
        part_y = jnp.exp(decay * m_y * m_y) * y_row[:, 0:1]
        msq = msq_xz + m_y * m_y
        anchor = (zero_xz + (slab * DZ + ky)) == 0
        safe = jnp.where(anchor, 1.0, msq)
        theta = jnp.where(anchor, 0.0, part_xz * part_y / safe)
        result[0, ky] = theta * real
        result[1, ky] = theta * imag
        for c in range(2):
            pltpu.make_async_copy(result.at[c, ky], kfield.at[c, ky], out_sem.at[c, ky]).start()
        half_term = 0.5 * theta * (real * real + imag * imag)
        u = half_term * (2.0 * (1.0 - decay * safe) / safe)
        u_z = u * m_z
        down_x = lambda x: jnp.sum(x, axis=0, keepdims=True)
        s_half, s_u = down_x(half_term), down_x(u)
        s_ux, s_uxx = down_x(u * m_x), down_x(u * m_x * m_x)
        s_uz = s_u * m_z
        terms = [
            s_half,
            s_half - s_uz * m_z,
            s_half - s_u * (m_y * m_y),
            s_half - s_uxx,
            -s_uz * m_y,
            -s_ux * m_z,
            -s_ux * m_y,
        ]
        sums = [a + b for a, b in zip(sums, terms)]
    lane_row = lax.broadcasted_iota(jnp.int32, (1, 128), 1)
    packed = jnp.zeros((1, 128), F32)
    for i, value in enumerate(sums):
        packed = jnp.where(lane_row == i, jnp.sum(value, axis=1, keepdims=True), packed)
    part[0] = packed

    def sum_copy(step):
        peer = lax.rem(slab + step, SLABS)
        return pltpu.make_async_remote_copy(
            src_ref=part.at[0], dst_ref=parts.at[slab],
            send_sem=sum_send, recv_sem=sum_recv, device_id=(peer, atom), device_id_type=MESH,
        )

    def sum_start(step, carry):
        sum_copy(step).start()
        return carry

    lax.fori_loop(1, SLABS, sum_start, 0)
    parts[slab] = packed
    sum_all = pltpu.make_async_remote_copy(
        src_ref=parts.at[pl.ds(0, SLABS - 1)], dst_ref=parts.at[pl.ds(0, SLABS - 1)],
        send_sem=sum_send, recv_sem=sum_recv, device_id=(above, atom), device_id_type=MESH,
    )
    sum_all.wait_recv()
    level = jnp.sum(parts[...], axis=0)
    middle[0] = level

    def mid_copy(step):
        peer = lax.rem(atom + step, SHARDS)
        return pltpu.make_async_remote_copy(
            src_ref=middle.at[0], dst_ref=middles.at[atom],
            send_sem=mid_send.at[step], recv_sem=mid_recv.at[SHARDS - step],
            device_id=(slab, peer), device_id_type=MESH,
        )

    for step in (2, 1, 3):
        mid_copy(step).start()
    middles[atom] = level

    for step in range(1, SHARDS):
        atom_copy(step).wait_send()
        for half in range(2):
            x_copy(half, step).wait_send()
    up.wait_send()
    down.wait_send()
    for half in range(2):
        y_all(half).wait_send()
    sum_all.wait_send()
    for ky in range(DZ):
        for c in range(2):
            pltpu.make_async_copy(result.at[c, ky], kfield.at[c, ky], out_sem.at[c, ky]).wait()
    for step in (1, 3, 2):
        mid_copy(step).wait_recv()
    whole = (middles[0] + middles[1]) + (middles[2] + middles[3])
    totals[...] = whole[:, 0:7] * (1.0 / (TILES * SLABS * SLOTS * SHARDS))
    for step in range(1, SHARDS):
        mid_copy(step).wait_send()


def body(cells, fractions, charges, counts, box):
    tx, t, rows_const, lanes_const = tables()
    vmem = pl.BlockSpec(memory_space=pltpu.VMEM)
    smem = pl.BlockSpec(memory_space=pltpu.SMEM)
    anywhere = pl.BlockSpec(memory_space=pl.ANY)
    dma = pltpu.SemaphoreType.DMA
    scratch = [
        pltpu.VMEM((2, K, 2 * K), BF16),
        pltpu.VMEM((2, K, 2 * K), BF16),
        pltpu.VMEM((SHARDS, 8, MAIN, SLOTS), F32),
        pltpu.VMEM((SHARDS, 8, MAIN, SLOTS), F32),
        pltpu.VMEM((22, 24, LANES), F32),
        pltpu.VMEM((2 * PLANES * 16, LANES), BF16),
        pltpu.VMEM((K, LANES), BF16),
        pltpu.VMEM((K, LANES), BF16),
        pltpu.VMEM((PLANES, ROWS, K), F32),
        pltpu.VMEM((PLANES, QUARTER, K), F32),
        pltpu.VMEM((3, QUARTER, K), F32),
        pltpu.VMEM((2, QUARTER, K), F32),
        pltpu.VMEM((2, SHARDS, 2, QUARTER, 128), F32),
        pltpu.VMEM((2, SHARDS, 2, QUARTER, 128), F32),
        pltpu.VMEM((2, SLABS // 2, 2, 8, 128), F32),
        pltpu.VMEM((SLABS * 16, 128), F32),
        pltpu.VMEM((2, DZ, QUARTER, K), F32),
        pltpu.VMEM((1, 1, 128), F32),
        pltpu.VMEM((SLABS, 1, 128), F32),
        pltpu.VMEM((1, 1, 128), F32),
        pltpu.VMEM((SHARDS, 1, 128), F32),
        dma((2,)), dma((SHARDS,)), dma((SHARDS,)), dma((2,)), dma((2,)), dma((2, SHARDS)), dma((2, SHARDS)),
        dma((2,)), dma((2,)), dma((2, DZ)), dma, dma, dma((SHARDS,)), dma((SHARDS,)),
    ]
    kfield, totals = pl.pallas_call(
        kernel,
        name="ewald",
        out_shape=(
            jax.ShapeDtypeStruct((2, DZ, QUARTER, K), F32),
            jax.ShapeDtypeStruct((1, 7), F32),
        ),
        in_specs=[vmem, vmem, vmem, vmem, smem, anywhere, anywhere, vmem, vmem],
        out_specs=(anywhere, vmem),
        scratch_shapes=scratch,
        compiler_params=pltpu.CompilerParams(collective_id=0, has_side_effects=True, vmem_limit_bytes=48 << 20),
    )(cells, fractions, charges, counts, box, tx, t, rows_const, lanes_const)
    return kfield, totals.reshape(7)


def solution(mesh):
    placed = (P(None, "slab", "atom"), P(None, "slab", "atom"), P("slab", "atom"), P("slab", "atom"), P())
    return jax.shard_map(
        body,
        mesh=mesh,
        in_specs=placed,
        out_specs=(P(None, "slab", "atom", None), P()),
        check_vma=False,
    )
```

```python
import functools
import math

import jax
import jax.numpy as jnp
import numpy as np
from jax import lax
from jax.experimental import pallas as pl
from jax.experimental.pallas import tpu as pltpu
from jax.sharding import PartitionSpec as P

K = 256
TILES = 64
SLOTS = 128
SLABS = 64
SHARDS = 4
DZ = 4
QUARTER = 64
MAIN = 16
PLANES = 9
ROWS = 88
SHIFT = 10
LANES = SHARDS * SLOTS
PIECES = 4
BLOCKS = ((0, 5), (5, 4), (9, 4), (13, 5))
DONE = ((0, 8), (8, 16), (24, 16), (40, 24))
beta = 1.25
F32 = jnp.float32
BF16 = jnp.bfloat16
MESH = pl.DeviceIdType.MESH


def tables():
    index = np.arange(K)
    angle = (index[:, None] * index[None, :] % K) * (2.0 * np.pi / K)
    cosine, sine = np.cos(angle), np.sin(angle)
    plain = np.concatenate([cosine, sine], axis=1)
    blocks = []
    for shard in range(SHARDS):
        cols = slice(shard * QUARTER, (shard + 1) * QUARTER)
        blocks += [cosine[:, cols], -sine[:, cols]]
    ordered = np.concatenate(blocks, axis=1)

    def halves(x):
        high = x.astype(np.float32).astype(jnp.bfloat16)
        low = (x - high.astype(np.float64)).astype(np.float32).astype(jnp.bfloat16)
        return np.stack([high, low])

    turn = 2.0 * np.pi * index / K
    modulus = (120.0 / (66.0 + 52.0 * np.cos(turn) + 2.0 * np.cos(2.0 * turn))) ** 2
    folded = np.where(index < K // 2, index, index - K)
    along_rows = np.zeros((K, 128), np.float32)
    along_rows[:, 0] = modulus
    along_rows[:, 1] = folded
    along_lanes = np.zeros((8, K), np.float32)
    along_lanes[0] = modulus
    along_lanes[1] = folded
    return halves(ordered), halves(plain), along_rows, along_lanes


def spline_weights(frac):
    prior = [jnp.ones_like(frac)]
    for order in range(2, 7):
        nxt = []
        for i in range(order):
            point = frac + i
            if i == 0:
                value = point * prior[0]
            elif i == order - 1:
                value = (order - point) * prior[i - 1]
            else:
                value = point * prior[i] + (order - point) * prior[i - 1]
            nxt.append(value * (1.0 / (order - 1)))
        prior = nxt
    return prior


def halved(x):
    high = x.astype(BF16)
    low = (x - high.astype(F32)).astype(BF16)
    return high, low


def dot(a, b):
    return jnp.dot(a, b, preferred_element_type=F32)


def dot_lanes(a, b):
    return lax.dot_general(a, b, (((1,), (1,)), ((), ())), preferred_element_type=F32)


def kernel(
    cells_hbm, fractions_hbm, charges_hbm, counts_hbm, box, tx_hbm, t_hbm, rows_hbm, lanes_hbm,
    kfield, totals,
    cells, fractions, charges, counts, rows_const, lanes_const,
    tx, t, send_atoms, atoms, splines, window, x_high, x_low, grid, planes, from_below, from_above,
    x_out, x_in, y_out, z_in, result, part, parts, middle, middles,
    table_sem, atom_send, atom_recv, halo_send, halo_recv, x_send, x_recv,
    y_send, y_recv, out_sem, sum_send, sum_recv, mid_send, mid_recv,
):
    slab = lax.axis_index("slab")
    atom = lax.axis_index("atom")

    def around(place, step, count):
        peer = place + step
        return jnp.where(peer >= count, peer - count, peer)

    pairs = [
        (cells_hbm, cells), (charges_hbm, charges), (counts_hbm, counts), (fractions_hbm, fractions),
        (tx_hbm, tx), (t_hbm, t), (rows_hbm, rows_const), (lanes_hbm, lanes_const),
    ]
    loads = [pltpu.make_async_copy(a, b, table_sem.at[i]) for i, (a, b) in enumerate(pairs)]
    for load in loads[:4]:
        load.start()
    barrier = pltpu.get_barrier_semaphore()
    for step in range(1, SHARDS):
        pl.semaphore_signal(barrier, inc=1, device_id=(slab, around(atom, step, SHARDS)), device_id_type=MESH)

    def greet(step, carry):
        pl.semaphore_signal(barrier, inc=1, device_id=(around(slab, step, SLABS), atom), device_id_type=MESH)
        return carry

    lax.fori_loop(1, SLABS, greet, 0, unroll=9)
    for load in loads[4:]:
        load.start()
    pending = []
    for load in loads[:4]:
        load.wait()

    slot = lax.broadcasted_iota(jnp.int32, (TILES, SLOTS), 1)
    tile_row = lax.broadcasted_iota(jnp.int32, (TILES, TILES), 0)
    tile_col = lax.broadcasted_iota(jnp.int32, (TILES, TILES), 1)
    diagonal = jnp.where(tile_row == tile_col, counts[...].astype(F32), 0.0)
    limit = jnp.sum(diagonal, axis=1, keepdims=True)
    weight = jnp.where(slot.astype(F32) < limit, charges[...], 0.0)
    fields = [cells[d].astype(F32) for d in range(3)] + [fractions[d] for d in range(3)] + [weight]
    spare = jnp.zeros((4, SLOTS), F32)
    for shard in range(SHARDS):
        for piece, (start, size) in enumerate(BLOCKS):
            first = shard * MAIN + 4 * piece
            cuts = [field[first : first + 4] for field in fields] + [spare]
            for pair in range(4):
                send_atoms[shard, start + pair] = jnp.concatenate(cuts[2 * pair : 2 * pair + 2], axis=0)
            if size == 5:
                at = (first - 1 if piece == 0 else first + 4) % TILES
                edge = [field[at : at + 1] for field in fields] + [spare[0:1]]
                send_atoms[shard, start + 4] = jnp.concatenate(edge, axis=0)
    pl.semaphore_wait(barrier, SHARDS - 1 + SLABS - 1)

    def atom_copy(piece, step):
        start, size = BLOCKS[piece]
        peer = around(atom, step, SHARDS)
        return pltpu.make_async_remote_copy(
            src_ref=send_atoms.at[peer, pl.ds(start, size)], dst_ref=atoms.at[atom, pl.ds(start, size)],
            send_sem=atom_send.at[piece, step], recv_sem=atom_recv.at[piece, SHARDS - step],
            device_id=(slab, peer), device_id_type=MESH,
        )

    for piece in range(PIECES):
        for step in (2, 1, 3):
            atom_copy(piece, step).start()
            pending.append(atom_copy(piece, step).wait_send)
    atoms[atom] = send_atoms[atom]
    grid[...] = jnp.zeros_like(grid)

    def weigh(piece):
        start, size = BLOCKS[piece]

        def gathered(number):
            row = 4 * (number % 2)
            main = [atoms[shard, start + number // 2, row : row + 4] for shard in range(SHARDS)]
            parts_of = [jnp.concatenate(main, axis=1)]
            if size == 5:
                edge = [atoms[shard, start + 4, number : number + 1] for shard in range(SHARDS)]
                parts_of.append(jnp.concatenate(edge, axis=1))
            parts_of.append(jnp.zeros((8 - size, LANES), F32))
            return jnp.concatenate(parts_of, axis=0)

        rows = slice(8 * piece, 8 * piece + 8)
        weights = gathered(6)
        for d in range(3):
            for i, value in enumerate(spline_weights(gathered(3 + d))):
                splines[6 * d + i, rows] = value * weights if d == 0 else value
        for d in range(2):
            cell = gathered(d)
            splines[18 + d, rows] = cell - 4.0 * jnp.floor(cell * 0.25) + 5.0
        first = gathered(2) - 2.0
        first = jnp.where(first < 0.0, first + K, first)
        block = jnp.floor(first * (1.0 / 16.0))
        splines[20, rows] = block
        splines[21, rows] = first - 16.0 * block

    row16 = lax.broadcasted_iota(jnp.int32, (16, LANES), 0).astype(F32)
    row24 = lax.broadcasted_iota(jnp.int32, (24, LANES), 0).astype(F32)

    def spread(piece, step):
        tile = jnp.where(step == 4, 4 * piece - 1 if piece == 0 else 4 * piece + 4, 4 * piece + step)
        at = 8 * piece + step
        base = pl.multiple_of(((tile + 2) // 2) * 8, 8)
        offset = (4 * lax.rem(tile + 2, 2)).astype(F32)

        def row(number):
            return splines[number, pl.ds(at, 1), :]

        near_z = row(18) - row16
        near_y = (row(19) + offset) - row16
        table_z = jnp.zeros((16, LANES), F32)
        table_y = jnp.zeros((16, LANES), F32)
        for i in range(6):
            table_z = jnp.where(near_z == i, row(i), table_z)
            table_y = jnp.where(near_y == i, row(6 + i), table_y)
        for p in range(PLANES):
            high, low = halved(table_z[p : p + 1] * table_y)
            window[p * 16 : (p + 1) * 16] = high
            window[PLANES * 16 + p * 16 : PLANES * 16 + (p + 1) * 16] = low
        past = row24 - row(21)
        small = jnp.zeros((24, LANES), F32)
        for j in range(6):
            small = jnp.where(past == j, row(12 + 5 - j), small)
        high = small.astype(BF16).astype(F32)
        low = small - high
        where_block = row(20)
        for b in range(16):
            here = where_block == b
            prior = where_block == (b - 1) % 16
            for source, target in ((high, x_high), (low, x_low)):
                top = jnp.where(here, source[0:8], jnp.where(prior, source[16:24], 0.0))
                bottom = jnp.where(here, source[8:16], 0.0)
                target[b * 16 : (b + 1) * 16] = jnp.concatenate([top, bottom], axis=0).astype(BF16)
        double = dot_lanes(window[...], x_high[...])
        single = dot_lanes(window[0 : PLANES * 16], x_low[...])
        out = double[0 : PLANES * 16] + double[PLANES * 16 :] + single
        out = out.reshape(PLANES, 16, K)
        grid[:, pl.ds(base, 16), :] += out

    above = around(slab, 1, SLABS)
    below = jnp.where(slab == 0, SLABS - 1, slab - 1)

    def halo_copies(piece):
        rows = pl.ds(*DONE[piece])
        up = pltpu.make_async_remote_copy(
            src_ref=planes.at[pl.ds(6, 3), rows], dst_ref=from_below.at[:, rows],
            send_sem=halo_send.at[0, piece], recv_sem=halo_recv.at[0, piece],
            device_id=(above, atom), device_id_type=MESH,
        )
        down = pltpu.make_async_remote_copy(
            src_ref=planes.at[pl.ds(0, 2), rows], dst_ref=from_above.at[:, rows],
            send_sem=halo_send.at[1, piece], recv_sem=halo_recv.at[1, piece],
            device_id=(below, atom), device_id_type=MESH,
        )
        return up, down

    def spread_piece(piece):
        for step in (1, 3, 2):
            atom_copy(piece, step).wait_recv()
        weigh(piece)

        def one(step, carry):
            spread(piece, step)
            return carry

        lax.fori_loop(0, BLOCKS[piece][1], one, 0)
        start, size = DONE[piece]
        planes[:, start : start + size, :] = grid[:, SHIFT + start : SHIFT + start + size, :]
        for copy in halo_copies(piece):
            copy.start()
            pending.append(copy.wait_send)

    def x_copy(piece, half, step):
        rows = pl.ds(*DONE[piece])
        peer = around(atom, step, SHARDS)
        return pltpu.make_async_remote_copy(
            src_ref=x_out.at[half, peer, :, rows], dst_ref=x_in.at[half, atom, :, rows],
            send_sem=x_send.at[piece, half, step], recv_sem=x_recv.at[piece, half, SHARDS - step],
            device_id=(slab, peer), device_id_type=MESH,
        )

    def x_piece(piece):
        start, size = DONE[piece]
        rows = slice(start, start + size)
        for copy in halo_copies(piece):
            copy.wait_recv()
        real = jnp.concatenate(
            [
                planes[2, rows] + from_below[0, rows],
                planes[3, rows] + from_below[1, rows],
                planes[4, rows] + from_below[2, rows] + from_above[0, rows],
                planes[5, rows] + from_above[1, rows],
            ],
            axis=0,
        )
        high, low = halved(real)
        out = dot(high, tx[0]) + dot(low, tx[0]) + dot(high, tx[1])
        for half in range(2):
            for shard in range(SHARDS):
                block = out[2 * half * size : 2 * (half + 1) * size, shard * 128 : (shard + 1) * 128]
                x_out[half, shard, :, rows] = block.reshape(2, size, 128)
            for step in (2, 1, 3):
                x_copy(piece, half, step).start()
                pending.append(x_copy(piece, half, step).wait_send)
            x_in[half, atom, :, rows] = x_out[half, atom, :, rows]

    spread_piece(0)
    spread_piece(1)
    spread_piece(2)
    for load in loads[4:]:
        load.wait()
    x_piece(0)
    spread_piece(3)
    x_piece(1)
    x_piece(2)
    x_piece(3)

    lane = lax.broadcasted_iota(jnp.int32, (K, 128), 1)
    row8 = lax.broadcasted_iota(jnp.int32, (32, 8, 128), 1)

    def y_copy(half, step):
        peer = around(slab, step, SLABS)
        return pltpu.make_async_remote_copy(
            src_ref=y_out.at[half, peer // 2, lax.rem(peer, 2)],
            dst_ref=z_in.at[pl.ds(pl.multiple_of(slab * 16 + half * 8, 8), 8)],
            send_sem=y_send.at[half], recv_sem=y_recv.at[half],
            device_id=(peer, atom), device_id_type=MESH,
        )

    for half in range(2):
        for piece in range(PIECES):
            for step in (1, 3, 2):
                x_copy(piece, half, step).wait_recv()
        plain, turned = [], []
        for p in range(2):
            f = jnp.concatenate([x_in[half, shard, p] for shard in range(SHARDS)], axis=0)
            g = pltpu.roll(f, 64, 1)
            plain.append(f)
            turned.append(jnp.where(lane < 64, g, -g))
        both = jnp.concatenate([jnp.concatenate(plain, axis=1), jnp.concatenate(turned, axis=1)], axis=0)
        high, low = halved(both)
        out = dot(t[0], high) + dot(t[0], low) + dot(t[1], high)
        y0 = out[:, 0:128].reshape(32, 8, 128)
        y1 = out[:, 128:256].reshape(32, 8, 128)
        y_out[half, :, 0] = jnp.where(row8 < 4, y0, pltpu.roll(y1, 4, 1))
        y_out[half, :, 1] = jnp.where(row8 < 4, pltpu.roll(y0, 4, 1), y1)

        def send(step, carry):
            y_copy(half, step).start()
            return carry

        lax.fori_loop(1, SLABS, send, 0, unroll=9)
        z_in[pl.ds(pl.multiple_of(slab * 16 + half * 8, 8), 8)] = y_out[half, slab // 2, lax.rem(slab, 2)]

    def y_all(half):
        return pltpu.make_async_remote_copy(
            src_ref=z_in.at[pl.ds(0, 8 * (SLABS - 1))], dst_ref=z_in.at[pl.ds(0, 8 * (SLABS - 1))],
            send_sem=y_send.at[half], recv_sem=y_recv.at[half],
            device_id=(above, atom), device_id_type=MESH,
        )

    pending += [y_all(half).wait_send for half in range(2)]
    span_z, span_y, span_x = box[0], box[1], box[2]
    decay = -(math.pi**2) / beta**2
    ones = jnp.ones((8, K), F32)
    m_z = lanes_const[1:2] / (ones[0:1] * span_z)
    part_z = jnp.exp(decay * m_z * m_z) * lanes_const[0:1]
    own_x = rows_const[pl.ds(pl.multiple_of(atom * QUARTER, QUARTER), QUARTER)]
    m_x = own_x[:, 1:2] / (ones[0, 0] * span_x * jnp.ones((QUARTER, 1), F32))
    scale = jnp.ones((QUARTER, 1), F32) / (math.pi * span_z * span_y * span_x * jnp.ones((QUARTER, 1), F32))
    part_x = jnp.exp(decay * m_x * m_x) * own_x[:, 0:1] * scale
    part_xz = part_x * part_z
    msq_xz = m_x * m_x + m_z * m_z
    own_y = rows_const[pl.ds(pl.multiple_of((slab // 2) * 8, 8), 8)]
    kx_at = lax.broadcasted_iota(jnp.int32, (QUARTER, K), 0) + atom * QUARTER
    kz_at = lax.broadcasted_iota(jnp.int32, (QUARTER, K), 1)
    zero_xz = kx_at + kz_at

    for half in range(2):
        y_all(half).wait_recv()

    sums = [jnp.zeros((1, K), F32) for _ in range(7)]
    for ky in range(DZ):
        f = z_in[pl.ds(ky, K, stride=4), :].T
        high, low = halved(f)
        out = dot(high, t[0]) + dot(low, t[0]) + dot(high, t[1])
        real = out[0:QUARTER, 0:K] + out[QUARTER:, K:]
        imag = out[QUARTER:, 0:K] - out[0:QUARTER, K:]
        y_row = jnp.where(lax.rem(slab, 2) == 0, own_y[ky : ky + 1], own_y[ky + 4 : ky + 5])
        m_y = y_row[:, 1:2] / (jnp.ones((1, 1), F32) * span_y)
        part_y = jnp.exp(decay * m_y * m_y) * y_row[:, 0:1]
        msq = msq_xz + m_y * m_y
        anchor = (zero_xz + (slab * DZ + ky)) == 0
        safe = jnp.where(anchor, 1.0, msq)
        theta = jnp.where(anchor, 0.0, part_xz * part_y / safe)
        result[0, ky] = theta * real
        result[1, ky] = theta * imag
        for c in range(2):
            put = pltpu.make_async_copy(result.at[c, ky], kfield.at[c, ky], out_sem.at[c, ky])
            put.start()
            pending.append(put.wait)
        half_term = 0.5 * theta * (real * real + imag * imag)
        u = half_term * (2.0 * (1.0 - decay * safe) / safe)
        u_z = u * m_z
        down_x = lambda x: jnp.sum(x, axis=0, keepdims=True)
        s_half, s_u = down_x(half_term), down_x(u)
        s_ux, s_uxx = down_x(u * m_x), down_x(u * m_x * m_x)
        s_uz = s_u * m_z
        terms = [
            s_half,
            s_half - s_uz * m_z,
            s_half - s_u * (m_y * m_y),
            s_half - s_uxx,
            -s_uz * m_y,
            -s_ux * m_z,
            -s_ux * m_y,
        ]
        sums = [a + b for a, b in zip(sums, terms)]
    lane_row = lax.broadcasted_iota(jnp.int32, (1, 128), 1)
    packed = jnp.zeros((1, 128), F32)
    for i, value in enumerate(sums):
        packed = jnp.where(lane_row == i, jnp.sum(value, axis=1, keepdims=True), packed)
    part[0] = packed

    def sum_copy(step):
        peer = around(slab, step, SLABS)
        return pltpu.make_async_remote_copy(
            src_ref=part.at[0], dst_ref=parts.at[slab],
            send_sem=sum_send, recv_sem=sum_recv, device_id=(peer, atom), device_id_type=MESH,
        )

    def sum_start(step, carry):
        sum_copy(step).start()
        return carry

    lax.fori_loop(1, SLABS, sum_start, 0, unroll=9)
    parts[slab] = packed
    sum_all = pltpu.make_async_remote_copy(
        src_ref=parts.at[pl.ds(0, SLABS - 1)], dst_ref=parts.at[pl.ds(0, SLABS - 1)],
        send_sem=sum_send, recv_sem=sum_recv, device_id=(above, atom), device_id_type=MESH,
    )
    pending.append(sum_all.wait_send)
    sum_all.wait_recv()
    level = jnp.sum(parts[...], axis=0)
    middle[0] = level

    def mid_copy(step):
        peer = lax.rem(atom + step, SHARDS)
        return pltpu.make_async_remote_copy(
            src_ref=middle.at[0], dst_ref=middles.at[atom],
            send_sem=mid_send.at[step], recv_sem=mid_recv.at[SHARDS - step],
            device_id=(slab, peer), device_id_type=MESH,
        )

    for step in (2, 1, 3):
        mid_copy(step).start()
    middles[atom] = level

    for wait in pending:
        wait()
    for step in (1, 3, 2):
        mid_copy(step).wait_recv()
    whole = (middles[0] + middles[1]) + (middles[2] + middles[3])
    totals[...] = whole[:, 0:7] * (1.0 / (TILES * SLABS * SLOTS * SHARDS))
    for step in range(1, SHARDS):
        mid_copy(step).wait_send()


def body(cells, fractions, charges, counts, box):
    tx, t, rows_const, lanes_const = tables()
    vmem = pl.BlockSpec(memory_space=pltpu.VMEM)
    smem = pl.BlockSpec(memory_space=pltpu.SMEM)
    anywhere = pl.BlockSpec(memory_space=pl.ANY)
    hbm = pl.BlockSpec(memory_space=pltpu.HBM)
    dma = pltpu.SemaphoreType.DMA
    scratch = [
        pltpu.VMEM((3, TILES, SLOTS), jnp.int32),
        pltpu.VMEM((3, TILES, SLOTS), F32),
        pltpu.VMEM((TILES, SLOTS), F32),
        pltpu.VMEM((1, TILES), jnp.int32),
        pltpu.VMEM((K, 128), F32),
        pltpu.VMEM((8, K), F32),
        pltpu.VMEM((2, K, 2 * K), BF16),
        pltpu.VMEM((2, K, 2 * K), BF16),
        pltpu.VMEM((SHARDS, 18, 8, SLOTS), F32),
        pltpu.VMEM((SHARDS, 18, 8, SLOTS), F32),
        pltpu.VMEM((22, 8 * PIECES, LANES), F32),
        pltpu.VMEM((2 * PLANES * 16, LANES), BF16),
        pltpu.VMEM((K, LANES), BF16),
        pltpu.VMEM((K, LANES), BF16),
        pltpu.VMEM((PLANES, ROWS, K), F32),
        pltpu.VMEM((PLANES, QUARTER, K), F32),
        pltpu.VMEM((3, QUARTER, K), F32),
        pltpu.VMEM((2, QUARTER, K), F32),
        pltpu.VMEM((2, SHARDS, 2, QUARTER, 128), F32),
        pltpu.VMEM((2, SHARDS, 2, QUARTER, 128), F32),
        pltpu.VMEM((2, SLABS // 2, 2, 8, 128), F32),
        pltpu.VMEM((SLABS * 16, 128), F32),
        pltpu.VMEM((2, DZ, QUARTER, K), F32),
        pltpu.VMEM((1, 1, 128), F32),
        pltpu.VMEM((SLABS, 1, 128), F32),
        pltpu.VMEM((1, 1, 128), F32),
        pltpu.VMEM((SHARDS, 1, 128), F32),
        dma((8,)), dma((PIECES, SHARDS)), dma((PIECES, SHARDS)), dma((2, PIECES)), dma((2, PIECES)),
        dma((PIECES, 2, SHARDS)), dma((PIECES, 2, SHARDS)),
        dma((2,)), dma((2,)), dma((2, DZ)), dma, dma, dma((SHARDS,)), dma((SHARDS,)),
    ]
    kfield, totals = pl.pallas_call(
        kernel,
        name="ewald",
        out_shape=(
            jax.ShapeDtypeStruct((2, DZ, QUARTER, K), F32),
            jax.ShapeDtypeStruct((1, 7), F32),
        ),
        in_specs=[hbm, hbm, hbm, hbm, smem, hbm, hbm, hbm, hbm],
        out_specs=(anywhere, vmem),
        scratch_shapes=scratch,
        compiler_params=pltpu.CompilerParams(collective_id=0, has_side_effects=True),
    )(cells, fractions, charges, counts.reshape(1, TILES), box, tx, t, rows_const, lanes_const)
    return kfield, totals.reshape(7)


def solution(mesh):
    placed = (P(None, "slab", "atom"), P(None, "slab", "atom"), P("slab", "atom"), P("slab", "atom"), P())
    return jax.shard_map(
        body,
        mesh=mesh,
        in_specs=placed,
        out_specs=(P(None, "slab", "atom", None), P()),
        check_vma=False,
    )
```

```python
import functools
import math

import jax
import jax.numpy as jnp
import numpy as np
from jax import lax
from jax.experimental import pallas as pl
from jax.experimental.pallas import tpu as pltpu
from jax.sharding import PartitionSpec as P

K = 256
TILES = 64
SLOTS = 128
SLABS = 64
SHARDS = 4
DZ = 4
QUARTER = 64
MAIN = 16
PLANES = 9
ROWS = 88
SHIFT = 10
LANES = SHARDS * SLOTS
PIECES = 4
BLOCKS = ((0, 5), (5, 4), (9, 4), (13, 5))
SPREAD = (range(-1, 3), range(3, 7), range(7, 11), range(11, 17))
DONE = ((0, 8), (8, 16), (24, 16), (40, 24))


def distance(mask):
    return sum((0, 1, 2, 1)[(mask >> low) & 3] for low in (2, 4)) + ((mask >> 1) & 1)


FLIPS = sorted(range(1, SLABS), key=lambda mask: -distance(mask))
beta = 1.25
F32 = jnp.float32
BF16 = jnp.bfloat16
MESH = pl.DeviceIdType.MESH


def tables():
    index = np.arange(K)
    angle = (index[:, None] * index[None, :] % K) * (2.0 * np.pi / K)
    cosine, sine = np.cos(angle), np.sin(angle)
    plain = np.concatenate([cosine, sine], axis=1)
    blocks = []
    for shard in range(SHARDS):
        cols = slice(shard * QUARTER, (shard + 1) * QUARTER)
        blocks += [cosine[:, cols], -sine[:, cols]]
    ordered = np.concatenate(blocks, axis=1)

    def halves(x):
        high = x.astype(np.float32).astype(jnp.bfloat16)
        low = (x - high.astype(np.float64)).astype(np.float32).astype(jnp.bfloat16)
        return np.stack([high, low])

    turn = 2.0 * np.pi * index / K
    modulus = (120.0 / (66.0 + 52.0 * np.cos(turn) + 2.0 * np.cos(2.0 * turn))) ** 2
    folded = np.where(index < K // 2, index, index - K)
    along_rows = np.zeros((K, 128), np.float32)
    along_rows[:, 0] = modulus
    along_rows[:, 1] = folded
    along_lanes = np.zeros((8, K), np.float32)
    along_lanes[0] = modulus
    along_lanes[1] = folded
    return halves(ordered), halves(plain), along_rows, along_lanes


def spline_weights(frac):
    prior = [jnp.ones_like(frac)]
    for order in range(2, 7):
        nxt = []
        for i in range(order):
            point = frac + i
            if i == 0:
                value = point * prior[0]
            elif i == order - 1:
                value = (order - point) * prior[i - 1]
            else:
                value = point * prior[i] + (order - point) * prior[i - 1]
            nxt.append(value * (1.0 / (order - 1)))
        prior = nxt
    return prior


def halved(x):
    high = x.astype(BF16)
    low = (x - high.astype(F32)).astype(BF16)
    return high, low


def dot(a, b):
    return jnp.dot(a, b, preferred_element_type=F32)


def dot_lanes(a, b):
    return lax.dot_general(a, b, (((1,), (1,)), ((), ())), preferred_element_type=F32)


def kernel(
    cells_hbm, fractions_hbm, charges_hbm, counts_hbm, box, tx_hbm, t_hbm, rows_hbm, lanes_hbm,
    kfield, totals,
    cells, fractions, charges, counts, rows_const, lanes_const,
    tx, t, send_atoms, atoms, splines, windows, x_highs, x_lows, grid, planes, from_below, from_above,
    x_out, x_in, y_out, z_in, result, part, parts, middle, middles,
    table_sem, atom_send, atom_recv, halo_send, halo_recv, x_send, x_recv,
    y_send, y_recv, out_sem, sum_send, sum_recv, mid_send, mid_recv,
):
    slab = lax.axis_index("slab")
    atom = lax.axis_index("atom")

    def around(place, step, count):
        peer = place + step
        return jnp.where(peer >= count, peer - count, peer)

    pairs = [
        (cells_hbm, cells), (charges_hbm, charges), (counts_hbm, counts), (fractions_hbm, fractions),
        (tx_hbm, tx), (t_hbm, t), (rows_hbm, rows_const), (lanes_hbm, lanes_const),
    ]
    loads = [pltpu.make_async_copy(a, b, table_sem.at[i]) for i, (a, b) in enumerate(pairs)]
    for load in loads[:4]:
        load.start()
    barrier = pltpu.get_barrier_semaphore()
    for step in range(1, SHARDS):
        pl.semaphore_signal(barrier, inc=1, device_id=(slab, around(atom, step, SHARDS)), device_id_type=MESH)

    bits = [(1 - 2 * lax.rem(slab // (1 << b), 2)) * (1 << b) for b in range(6)]
    lower = [sum((bits[b] for b in range(3) if m >> b & 1), slab) for m in range(8)]
    upper = [sum((bits[b + 3] for b in range(3) if m >> b & 1), 0) for m in range(8)]

    def across(mask):
        return lower[mask % 8] + upper[mask // 8]

    for mask in FLIPS:
        pl.semaphore_signal(barrier, inc=1, device_id=(across(mask), atom), device_id_type=MESH)
    for load in loads[4:]:
        load.start()
    pending = []
    for load in loads[:4]:
        load.wait()

    slot = lax.broadcasted_iota(jnp.int32, (TILES, SLOTS), 1)
    tile_row = lax.broadcasted_iota(jnp.int32, (TILES, TILES), 0)
    tile_col = lax.broadcasted_iota(jnp.int32, (TILES, TILES), 1)
    diagonal = jnp.where(tile_row == tile_col, counts[...].astype(F32), 0.0)
    limit = jnp.sum(diagonal, axis=1, keepdims=True)
    weight = jnp.where(slot.astype(F32) < limit, charges[...], 0.0)
    fields = [cells[d].astype(F32) for d in range(3)] + [fractions[d] for d in range(3)] + [weight]
    spare = jnp.zeros((4, SLOTS), F32)
    for shard in range(SHARDS):
        for piece, (start, size) in enumerate(BLOCKS):
            first = shard * MAIN + 4 * piece
            cuts = [field[first : first + 4] for field in fields] + [spare]
            for pair in range(4):
                send_atoms[shard, start + pair] = jnp.concatenate(cuts[2 * pair : 2 * pair + 2], axis=0)
            if size == 5:
                at = (first - 1 if piece == 0 else first + 4) % TILES
                edge = [field[at : at + 1] for field in fields] + [spare[0:1]]
                send_atoms[shard, start + 4] = jnp.concatenate(edge, axis=0)
    pl.semaphore_wait(barrier, SHARDS - 1 + SLABS - 1)

    def atom_copy(piece, step):
        start, size = BLOCKS[piece]
        peer = around(atom, step, SHARDS)
        return pltpu.make_async_remote_copy(
            src_ref=send_atoms.at[peer, pl.ds(start, size)], dst_ref=atoms.at[atom, pl.ds(start, size)],
            send_sem=atom_send.at[piece, step], recv_sem=atom_recv.at[piece, SHARDS - step],
            device_id=(slab, peer), device_id_type=MESH,
        )

    for piece in range(PIECES):
        for step in (2, 1, 3):
            atom_copy(piece, step).start()
            pending.append(atom_copy(piece, step).wait_send)
    atoms[atom] = send_atoms[atom]
    grid[...] = jnp.zeros_like(grid)

    def weigh(piece):
        start, size = BLOCKS[piece]

        def gathered(number):
            row = 4 * (number % 2)
            main = [atoms[shard, start + number // 2, row : row + 4] for shard in range(SHARDS)]
            parts_of = [jnp.concatenate(main, axis=1)]
            if size == 5:
                edge = [atoms[shard, start + 4, number : number + 1] for shard in range(SHARDS)]
                parts_of.append(jnp.concatenate(edge, axis=1))
            parts_of.append(jnp.zeros((8 - size, LANES), F32))
            return jnp.concatenate(parts_of, axis=0)

        rows = slice(8 * piece, 8 * piece + 8)
        def within(cell):
            return cell - DZ * jnp.floor(cell * (1.0 / DZ))

        weights = gathered(6)
        along_z = [value * weights for value in spline_weights(gathered(3))]
        place = within(gathered(0))
        is_at = [place == c for c in range(DZ)]
        for p in range(PLANES):
            value = jnp.zeros((8, LANES), F32)
            for c in range(DZ):
                if 0 <= c + 5 - p <= 5:
                    value = jnp.where(is_at[c], along_z[c + 5 - p], value)
            splines[p, rows] = value
        for d in range(2):
            for i, value in enumerate(spline_weights(gathered(4 + d))):
                splines[PLANES + 6 * d + i, rows] = value
        splines[21, rows] = within(gathered(1)) + 5.0
        first = gathered(2) - 2.0
        first = jnp.where(first < 0.0, first + K, first)
        block = jnp.floor(first * (1.0 / 16.0))
        splines[22, rows] = block
        splines[23, rows] = first - 16.0 * block

    row16 = lax.broadcasted_iota(jnp.int32, (16, LANES), 0).astype(F32)
    row24 = lax.broadcasted_iota(jnp.int32, (24, LANES), 0).astype(F32)

    def spread(tile):
        at = {-1: 4, MAIN: 28}.get(tile, 8 * (tile // 4) + tile % 4)
        base = ((tile + 2) // 2) * 8
        offset = 4.0 * (tile % 2)
        window, x_high, x_low = windows.at[tile % 2], x_highs.at[tile % 2], x_lows.at[tile % 2]

        def row(number):
            return splines[number, at : at + 1, :]

        near_y = (row(21) + offset) - row16
        table_y = jnp.zeros((16, LANES), F32)
        for i in range(6):
            table_y = jnp.where(near_y == i, row(PLANES + i), table_y)
        for p in range(PLANES):
            high, low = halved(row(p) * table_y)
            window[p * 16 : (p + 1) * 16] = high
            window[PLANES * 16 + p * 16 : PLANES * 16 + (p + 1) * 16] = low
        past = row24 - row(23)
        small = jnp.zeros((24, LANES), F32)
        for j in range(6):
            small = jnp.where(past == j, row(PLANES + 6 + 5 - j), small)
        small = jnp.concatenate([small, jnp.zeros((8, LANES), F32)], axis=0)
        high, low = halved(small)
        where_block = jnp.broadcast_to(row(22), (16, LANES)).astype(BF16)
        nothing = jnp.zeros((16, LANES), BF16)
        is_here = [where_block == b for b in range(16)]
        for b in range(16):
            for source, target in ((high, x_high), (low, x_low)):
                after = jnp.where(is_here[(b - 1) % 16], source[16:32], nothing)
                target[b * 16 : (b + 1) * 16] = jnp.where(is_here[b], source[0:16], after)
        double = dot_lanes(window[...], x_high[...])
        single = dot_lanes(window[0 : PLANES * 16], x_low[...])
        out = double[0 : PLANES * 16] + double[PLANES * 16 :] + single
        out = out.reshape(PLANES, 16, K)
        grid[:, base : base + 16, :] += out

    above = around(slab, 1, SLABS)
    below = jnp.where(slab == 0, SLABS - 1, slab - 1)

    def halo_copies(piece):
        rows = pl.ds(*DONE[piece])
        up = pltpu.make_async_remote_copy(
            src_ref=planes.at[pl.ds(6, 3), rows], dst_ref=from_below.at[:, rows],
            send_sem=halo_send.at[0, piece], recv_sem=halo_recv.at[0, piece],
            device_id=(above, atom), device_id_type=MESH,
        )
        down = pltpu.make_async_remote_copy(
            src_ref=planes.at[pl.ds(0, 2), rows], dst_ref=from_above.at[:, rows],
            send_sem=halo_send.at[1, piece], recv_sem=halo_recv.at[1, piece],
            device_id=(below, atom), device_id_type=MESH,
        )
        return up, down

    def spread_piece(piece):
        for step in (1, 3, 2):
            atom_copy(piece, step).wait_recv()
        weigh(piece)

        for tile in SPREAD[piece]:
            spread(tile)
        start, size = DONE[piece]
        planes[:, start : start + size, :] = grid[:, SHIFT + start : SHIFT + start + size, :]
        for copy in halo_copies(piece):
            copy.start()
            pending.append(copy.wait_send)

    def x_copy(piece, half, step):
        rows = pl.ds(*DONE[piece])
        peer = around(atom, step, SHARDS)
        return pltpu.make_async_remote_copy(
            src_ref=x_out.at[half, peer, :, rows], dst_ref=x_in.at[half, atom, :, rows],
            send_sem=x_send.at[piece, half, step], recv_sem=x_recv.at[piece, half, SHARDS - step],
            device_id=(slab, peer), device_id_type=MESH,
        )

    def x_piece(piece):
        start, size = DONE[piece]
        rows = slice(start, start + size)
        for copy in halo_copies(piece):
            copy.wait_recv()
        real = jnp.concatenate(
            [
                planes[2, rows] + from_below[0, rows],
                planes[3, rows] + from_below[1, rows],
                planes[4, rows] + from_below[2, rows] + from_above[0, rows],
                planes[5, rows] + from_above[1, rows],
            ],
            axis=0,
        )
        high, low = halved(real)
        out = dot(high, tx[0]) + dot(low, tx[0]) + dot(high, tx[1])
        for half in range(2):
            for shard in range(SHARDS):
                block = out[2 * half * size : 2 * (half + 1) * size, shard * 128 : (shard + 1) * 128]
                x_out[half, shard, :, rows] = block.reshape(2, size, 128)
            for step in (2, 1, 3):
                x_copy(piece, half, step).start()
                pending.append(x_copy(piece, half, step).wait_send)
            x_in[half, atom, :, rows] = x_out[half, atom, :, rows]

    spread_piece(0)
    spread_piece(1)
    spread_piece(2)
    spread_piece(3)
    for load in loads[4:]:
        load.wait()
    x_piece(0)
    x_piece(1)
    x_piece(2)
    x_piece(3)

    lane = lax.broadcasted_iota(jnp.int32, (K, 128), 1)
    row8 = lax.broadcasted_iota(jnp.int32, (32, 8, 128), 1)

    def y_copy(half, mask):
        peer = across(mask)
        return pltpu.make_async_remote_copy(
            src_ref=y_out.at[half, peer],
            dst_ref=z_in.at[pl.ds(pl.multiple_of(slab * 16 + half * 8, 8), 8)],
            send_sem=y_send.at[half], recv_sem=y_recv.at[half],
            device_id=(peer, atom), device_id_type=MESH,
        )

    for half in range(2):
        for piece in range(PIECES):
            for step in (1, 3, 2):
                x_copy(piece, half, step).wait_recv()
        plain, turned = [], []
        for p in range(2):
            f = jnp.concatenate([x_in[half, shard, p] for shard in range(SHARDS)], axis=0)
            g = pltpu.roll(f, 64, 1)
            plain.append(f)
            turned.append(jnp.where(lane < 64, g, -g))
        both = jnp.concatenate([jnp.concatenate(plain, axis=1), jnp.concatenate(turned, axis=1)], axis=0)
        high, low = halved(both)
        out = dot(t[0], high) + dot(t[0], low) + dot(t[1], high)
        y0 = out[:, 0:128].reshape(32, 8, 128)
        y1 = out[:, 128:256].reshape(32, 8, 128)
        even = jnp.where(row8 < 4, y0, pltpu.roll(y1, 4, 1))
        odd = jnp.where(row8 < 4, pltpu.roll(y0, 4, 1), y1)
        y_out[half] = jnp.stack([even, odd], axis=1).reshape(SLABS, 8, 128)
        for mask in FLIPS:
            y_copy(half, mask).start()
        z_in[pl.ds(pl.multiple_of(slab * 16 + half * 8, 8), 8)] = y_out[half, slab]

    def y_all(half):
        return pltpu.make_async_remote_copy(
            src_ref=z_in.at[pl.ds(0, 8 * (SLABS - 1))], dst_ref=z_in.at[pl.ds(0, 8 * (SLABS - 1))],
            send_sem=y_send.at[half], recv_sem=y_recv.at[half],
            device_id=(above, atom), device_id_type=MESH,
        )

    pending += [y_all(half).wait_send for half in range(2)]
    span_z, span_y, span_x = box[0], box[1], box[2]
    decay = -(math.pi**2) / beta**2
    ones = jnp.ones((8, K), F32)
    m_z = lanes_const[1:2] / (ones[0:1] * span_z)
    part_z = jnp.exp(decay * m_z * m_z) * lanes_const[0:1]
    own_x = rows_const[pl.ds(pl.multiple_of(atom * QUARTER, QUARTER), QUARTER)]
    m_x = own_x[:, 1:2] / (ones[0, 0] * span_x * jnp.ones((QUARTER, 1), F32))
    scale = jnp.ones((QUARTER, 1), F32) / (math.pi * span_z * span_y * span_x * jnp.ones((QUARTER, 1), F32))
    part_x = jnp.exp(decay * m_x * m_x) * own_x[:, 0:1] * scale
    part_xz = part_x * part_z
    msq_xz = m_x * m_x + m_z * m_z
    own_y = rows_const[pl.ds(pl.multiple_of((slab // 2) * 8, 8), 8)]
    kx_at = lax.broadcasted_iota(jnp.int32, (QUARTER, K), 0) + atom * QUARTER
    kz_at = lax.broadcasted_iota(jnp.int32, (QUARTER, K), 1)
    zero_xz = kx_at + kz_at

    for half in range(2):
        y_all(half).wait_recv()

    sums = [jnp.zeros((1, K), F32) for _ in range(7)]
    for ky in range(DZ):
        f = z_in[pl.ds(ky, K, stride=4), :].T
        high, low = halved(f)
        out = dot(high, t[0]) + dot(low, t[0]) + dot(high, t[1])
        real = out[0:QUARTER, 0:K] + out[QUARTER:, K:]
        imag = out[QUARTER:, 0:K] - out[0:QUARTER, K:]
        y_row = jnp.where(lax.rem(slab, 2) == 0, own_y[ky : ky + 1], own_y[ky + 4 : ky + 5])
        m_y = y_row[:, 1:2] / (jnp.ones((1, 1), F32) * span_y)
        part_y = jnp.exp(decay * m_y * m_y) * y_row[:, 0:1]
        msq = msq_xz + m_y * m_y
        anchor = (zero_xz + (slab * DZ + ky)) == 0
        safe = jnp.where(anchor, 1.0, msq)
        theta = jnp.where(anchor, 0.0, part_xz * part_y / safe)
        result[0, ky] = theta * real
        result[1, ky] = theta * imag
        for c in range(2):
            put = pltpu.make_async_copy(result.at[c, ky], kfield.at[c, ky], out_sem.at[c, ky])
            put.start()
            pending.append(put.wait)
        half_term = 0.5 * theta * (real * real + imag * imag)
        u = half_term * (2.0 * (1.0 - decay * safe) / safe)
        u_z = u * m_z
        down_x = lambda x: jnp.sum(x, axis=0, keepdims=True)
        s_half, s_u = down_x(half_term), down_x(u)
        s_ux, s_uxx = down_x(u * m_x), down_x(u * m_x * m_x)
        s_uz = s_u * m_z
        terms = [
            s_half,
            s_half - s_uz * m_z,
            s_half - s_u * (m_y * m_y),
            s_half - s_uxx,
            -s_uz * m_y,
            -s_ux * m_z,
            -s_ux * m_y,
        ]
        sums = [a + b for a, b in zip(sums, terms)]
    lane_row = lax.broadcasted_iota(jnp.int32, (1, 128), 1)
    packed = jnp.zeros((1, 128), F32)
    for i, value in enumerate(sums):
        packed = jnp.where(lane_row == i, jnp.sum(value, axis=1, keepdims=True), packed)
    part[0] = packed

    def sum_copy(mask):
        peer = across(mask)
        return pltpu.make_async_remote_copy(
            src_ref=part.at[0], dst_ref=parts.at[slab],
            send_sem=sum_send, recv_sem=sum_recv, device_id=(peer, atom), device_id_type=MESH,
        )

    for mask in FLIPS:
        sum_copy(mask).start()
    parts[slab] = packed
    sum_all = pltpu.make_async_remote_copy(
        src_ref=parts.at[pl.ds(0, SLABS - 1)], dst_ref=parts.at[pl.ds(0, SLABS - 1)],
        send_sem=sum_send, recv_sem=sum_recv, device_id=(above, atom), device_id_type=MESH,
    )
    pending.append(sum_all.wait_send)
    sum_all.wait_recv()
    level = jnp.sum(parts[...], axis=0)
    middle[0] = level

    def mid_copy(step):
        peer = lax.rem(atom + step, SHARDS)
        return pltpu.make_async_remote_copy(
            src_ref=middle.at[0], dst_ref=middles.at[atom],
            send_sem=mid_send.at[step], recv_sem=mid_recv.at[SHARDS - step],
            device_id=(slab, peer), device_id_type=MESH,
        )

    for step in (2, 1, 3):
        mid_copy(step).start()
    middles[atom] = level

    for wait in pending:
        wait()
    for step in (1, 3, 2):
        mid_copy(step).wait_recv()
    whole = (middles[0] + middles[1]) + (middles[2] + middles[3])
    totals[...] = whole[:, 0:7] * (1.0 / (TILES * SLABS * SLOTS * SHARDS))
    for step in range(1, SHARDS):
        mid_copy(step).wait_send()


def body(cells, fractions, charges, counts, box):
    tx, t, rows_const, lanes_const = tables()
    vmem = pl.BlockSpec(memory_space=pltpu.VMEM)
    smem = pl.BlockSpec(memory_space=pltpu.SMEM)
    anywhere = pl.BlockSpec(memory_space=pl.ANY)
    hbm = pl.BlockSpec(memory_space=pltpu.HBM)
    dma = pltpu.SemaphoreType.DMA
    scratch = [
        pltpu.VMEM((3, TILES, SLOTS), jnp.int32),
        pltpu.VMEM((3, TILES, SLOTS), F32),
        pltpu.VMEM((TILES, SLOTS), F32),
        pltpu.VMEM((1, TILES), jnp.int32),
        pltpu.VMEM((K, 128), F32),
        pltpu.VMEM((8, K), F32),
        pltpu.VMEM((2, K, 2 * K), BF16),
        pltpu.VMEM((2, K, 2 * K), BF16),
        pltpu.VMEM((SHARDS, 18, 8, SLOTS), F32),
        pltpu.VMEM((SHARDS, 18, 8, SLOTS), F32),
        pltpu.VMEM((24, 8 * PIECES, LANES), F32),
        pltpu.VMEM((2, 2 * PLANES * 16, LANES), BF16),
        pltpu.VMEM((2, K, LANES), BF16),
        pltpu.VMEM((2, K, LANES), BF16),
        pltpu.VMEM((PLANES, ROWS, K), F32),
        pltpu.VMEM((PLANES, QUARTER, K), F32),
        pltpu.VMEM((3, QUARTER, K), F32),
        pltpu.VMEM((2, QUARTER, K), F32),
        pltpu.VMEM((2, SHARDS, 2, QUARTER, 128), F32),
        pltpu.VMEM((2, SHARDS, 2, QUARTER, 128), F32),
        pltpu.VMEM((2, SLABS, 8, 128), F32),
        pltpu.VMEM((SLABS * 16, 128), F32),
        pltpu.VMEM((2, DZ, QUARTER, K), F32),
        pltpu.VMEM((1, 1, 128), F32),
        pltpu.VMEM((SLABS, 1, 128), F32),
        pltpu.VMEM((1, 1, 128), F32),
        pltpu.VMEM((SHARDS, 1, 128), F32),
        dma((8,)), dma((PIECES, SHARDS)), dma((PIECES, SHARDS)), dma((2, PIECES)), dma((2, PIECES)),
        dma((PIECES, 2, SHARDS)), dma((PIECES, 2, SHARDS)),
        dma((2,)), dma((2,)), dma((2, DZ)), dma, dma, dma((SHARDS,)), dma((SHARDS,)),
    ]
    kfield, totals = pl.pallas_call(
        kernel,
        name="ewald",
        out_shape=(
            jax.ShapeDtypeStruct((2, DZ, QUARTER, K), F32),
            jax.ShapeDtypeStruct((1, 7), F32),
        ),
        in_specs=[hbm, hbm, hbm, hbm, smem, hbm, hbm, hbm, hbm],
        out_specs=(anywhere, vmem),
        scratch_shapes=scratch,
        compiler_params=pltpu.CompilerParams(collective_id=0, has_side_effects=True),
    )(cells, fractions, charges, counts.reshape(1, TILES), box, tx, t, rows_const, lanes_const)
    return kfield, totals.reshape(7)


def solution(mesh):
    placed = (P(None, "slab", "atom"), P(None, "slab", "atom"), P("slab", "atom"), P("slab", "atom"), P())
    return jax.shard_map(
        body,
        mesh=mesh,
        in_specs=placed,
        out_specs=(P(None, "slab", "atom", None), P()),
        check_vma=False,
    )
```

```python
import functools
import math

import jax
import jax.numpy as jnp
import numpy as np
from jax import lax
from jax.experimental import pallas as pl
from jax.experimental.pallas import tpu as pltpu
from jax.sharding import PartitionSpec as P

K = 256
TILES = 64
SLOTS = 128
SLABS = 64
SHARDS = 4
DZ = 4
QUARTER = 64
MAIN = 16
PLANES = 9
ROWS = 88
SHIFT = 10
LANES = SHARDS * SLOTS
PIECES = 4
BLOCKS = ((0, 5), (5, 4), (9, 4), (13, 5))
SPREAD = (range(-1, 3), range(3, 7), range(7, 11), range(11, 17))
DONE = ((0, 8), (8, 16), (24, 16), (40, 24))


def distance(mask):
    return sum((0, 1, 2, 1)[(mask >> low) & 3] for low in (2, 4)) + ((mask >> 1) & 1)


FLIPS = sorted(range(1, SLABS), key=lambda mask: -distance(mask))
beta = 1.25
F32 = jnp.float32
BF16 = jnp.bfloat16
MESH = pl.DeviceIdType.MESH


def tables():
    index = np.arange(K)
    angle = (index[:, None] * index[None, :] % K) * (2.0 * np.pi / K)
    cosine, sine = np.cos(angle), np.sin(angle)
    plain = np.concatenate([cosine, sine], axis=1)
    blocks = []
    for shard in range(SHARDS):
        cols = slice(shard * QUARTER, (shard + 1) * QUARTER)
        blocks += [cosine[:, cols], -sine[:, cols]]
    ordered = np.concatenate(blocks, axis=1)

    def halves(x):
        high = x.astype(np.float32).astype(jnp.bfloat16)
        low = (x - high.astype(np.float64)).astype(np.float32).astype(jnp.bfloat16)
        return np.stack([high, low])

    turn = 2.0 * np.pi * index / K
    modulus = (120.0 / (66.0 + 52.0 * np.cos(turn) + 2.0 * np.cos(2.0 * turn))) ** 2
    folded = np.where(index < K // 2, index, index - K)
    along_rows = np.zeros((K, 128), np.float32)
    along_rows[:, 0] = modulus
    along_rows[:, 1] = folded
    along_lanes = np.zeros((8, K), np.float32)
    along_lanes[0] = modulus
    along_lanes[1] = folded
    return halves(ordered), halves(plain), along_rows, along_lanes


def spline_weights(frac):
    prior = [jnp.ones_like(frac)]
    for order in range(2, 7):
        nxt = []
        for i in range(order):
            point = frac + i
            if i == 0:
                value = point * prior[0]
            elif i == order - 1:
                value = (order - point) * prior[i - 1]
            else:
                value = point * prior[i] + (order - point) * prior[i - 1]
            nxt.append(value * (1.0 / (order - 1)))
        prior = nxt
    return prior


def halved(x):
    high = x.astype(BF16)
    low = (x - high.astype(F32)).astype(BF16)
    return high, low


def dot(a, b):
    return jnp.dot(a, b, preferred_element_type=F32)


def dot_lanes(a, b):
    return lax.dot_general(a, b, (((1,), (1,)), ((), ())), preferred_element_type=F32)


def kernel(
    cells_hbm, fractions_hbm, charges_hbm, counts_hbm, box, tx_hbm, t_hbm, rows_hbm, lanes_hbm,
    kfield, totals,
    cells, fractions, charges, counts, rows_const, lanes_const,
    tx, t, send_atoms, atoms, splines, windows, x_highs, x_lows, grid, planes, from_below, from_above,
    x_out, x_in, y_out, z_in, thetas, factors, result, part, parts, middle, middles,
    table_sem, atom_send, atom_recv, halo_send, halo_recv, x_send, x_recv,
    y_send, y_recv, out_sem, sum_send, sum_recv, mid_send, mid_recv,
):
    slab = lax.axis_index("slab")
    atom = lax.axis_index("atom")

    def around(place, step, count):
        peer = place + step
        return jnp.where(peer >= count, peer - count, peer)

    pairs = [
        (cells_hbm, cells), (charges_hbm, charges), (counts_hbm, counts), (fractions_hbm, fractions),
        (tx_hbm, tx), (t_hbm, t), (rows_hbm, rows_const), (lanes_hbm, lanes_const),
    ]
    loads = [pltpu.make_async_copy(a, b, table_sem.at[i]) for i, (a, b) in enumerate(pairs)]
    for load in loads[:4]:
        load.start()
    barrier = pltpu.get_barrier_semaphore()
    for step in range(1, SHARDS):
        pl.semaphore_signal(barrier, inc=1, device_id=(slab, around(atom, step, SHARDS)), device_id_type=MESH)

    bits = [(1 - 2 * lax.rem(slab // (1 << b), 2)) * (1 << b) for b in range(6)]
    lower = [sum((bits[b] for b in range(3) if m >> b & 1), slab) for m in range(8)]
    upper = [sum((bits[b + 3] for b in range(3) if m >> b & 1), 0) for m in range(8)]

    def across(mask):
        return lower[mask % 8] + upper[mask // 8]

    for mask in FLIPS:
        pl.semaphore_signal(barrier, inc=1, device_id=(across(mask), atom), device_id_type=MESH)
    for load in loads[4:]:
        load.start()
    pending = []
    for load in loads[:4]:
        load.wait()

    slot = lax.broadcasted_iota(jnp.int32, (TILES, SLOTS), 1)
    tile_row = lax.broadcasted_iota(jnp.int32, (TILES, TILES), 0)
    tile_col = lax.broadcasted_iota(jnp.int32, (TILES, TILES), 1)
    diagonal = jnp.where(tile_row == tile_col, counts[...].astype(F32), 0.0)
    limit = jnp.sum(diagonal, axis=1, keepdims=True)
    weight = jnp.where(slot.astype(F32) < limit, charges[...], 0.0)
    fields = [cells[d].astype(F32) for d in range(3)] + [fractions[d] for d in range(3)] + [weight]
    spare = jnp.zeros((4, SLOTS), F32)
    for shard in range(SHARDS):
        for piece, (start, size) in enumerate(BLOCKS):
            first = shard * MAIN + 4 * piece
            cuts = [field[first : first + 4] for field in fields] + [spare]
            for pair in range(4):
                send_atoms[shard, start + pair] = jnp.concatenate(cuts[2 * pair : 2 * pair + 2], axis=0)
            if size == 5:
                at = (first - 1 if piece == 0 else first + 4) % TILES
                edge = [field[at : at + 1] for field in fields] + [spare[0:1]]
                send_atoms[shard, start + 4] = jnp.concatenate(edge, axis=0)
    pl.semaphore_wait(barrier, SHARDS - 1 + SLABS - 1)

    def atom_copy(piece, step):
        start, size = BLOCKS[piece]
        peer = around(atom, step, SHARDS)
        return pltpu.make_async_remote_copy(
            src_ref=send_atoms.at[peer, pl.ds(start, size)], dst_ref=atoms.at[atom, pl.ds(start, size)],
            send_sem=atom_send.at[piece, step], recv_sem=atom_recv.at[piece, SHARDS - step],
            device_id=(slab, peer), device_id_type=MESH,
        )

    for piece in range(PIECES):
        for step in (2, 1, 3):
            atom_copy(piece, step).start()
            pending.append(atom_copy(piece, step).wait_send)
    atoms[atom] = send_atoms[atom]
    grid[...] = jnp.zeros_like(grid)

    def weigh(piece):
        start, size = BLOCKS[piece]

        def gathered(number):
            row = 4 * (number % 2)
            main = [atoms[shard, start + number // 2, row : row + 4] for shard in range(SHARDS)]
            parts_of = [jnp.concatenate(main, axis=1)]
            if size == 5:
                edge = [atoms[shard, start + 4, number : number + 1] for shard in range(SHARDS)]
                parts_of.append(jnp.concatenate(edge, axis=1))
            parts_of.append(jnp.zeros((8 - size, LANES), F32))
            return jnp.concatenate(parts_of, axis=0)

        rows = slice(8 * piece, 8 * piece + 8)
        def within(cell):
            return cell - DZ * jnp.floor(cell * (1.0 / DZ))

        weights = gathered(6)
        along_z = [value * weights for value in spline_weights(gathered(3))]
        place = within(gathered(0))
        is_at = [place == c for c in range(DZ)]
        for p in range(PLANES):
            value = jnp.zeros((8, LANES), F32)
            for c in range(DZ):
                if 0 <= c + 5 - p <= 5:
                    value = jnp.where(is_at[c], along_z[c + 5 - p], value)
            splines[p, rows] = value
        for d in range(2):
            for i, value in enumerate(spline_weights(gathered(4 + d))):
                splines[PLANES + 6 * d + i, rows] = value
        splines[21, rows] = within(gathered(1)) + 5.0
        first = gathered(2) - 2.0
        first = jnp.where(first < 0.0, first + K, first)
        block = jnp.floor(first * (1.0 / 16.0))
        splines[22, rows] = block
        splines[23, rows] = first - 16.0 * block

    row16 = lax.broadcasted_iota(jnp.int32, (16, LANES), 0).astype(F32)
    row24 = lax.broadcasted_iota(jnp.int32, (24, LANES), 0).astype(F32)

    def spread(tile):
        at = {-1: 4, MAIN: 28}.get(tile, 8 * (tile // 4) + tile % 4)
        base = ((tile + 2) // 2) * 8
        offset = 4.0 * (tile % 2)
        window, x_high, x_low = windows.at[tile % 2], x_highs.at[tile % 2], x_lows.at[tile % 2]

        def row(number):
            return splines[number, at : at + 1, :]

        near_y = (row(21) + offset) - row16
        table_y = jnp.zeros((16, LANES), F32)
        for i in range(6):
            table_y = jnp.where(near_y == i, row(PLANES + i), table_y)
        for p in range(PLANES):
            high, low = halved(row(p) * table_y)
            window[p * 16 : (p + 1) * 16] = high
            window[PLANES * 16 + p * 16 : PLANES * 16 + (p + 1) * 16] = low
        past = row24 - row(23)
        small = jnp.zeros((24, LANES), F32)
        for j in range(6):
            small = jnp.where(past == j, row(PLANES + 6 + 5 - j), small)
        small = jnp.concatenate([small, jnp.zeros((8, LANES), F32)], axis=0)
        high, low = halved(small)
        where_block = jnp.broadcast_to(row(22), (16, LANES)).astype(BF16)
        nothing = jnp.zeros((16, LANES), BF16)
        is_here = [where_block == b for b in range(16)]
        for b in range(16):
            for source, target in ((high, x_high), (low, x_low)):
                after = jnp.where(is_here[(b - 1) % 16], source[16:32], nothing)
                target[b * 16 : (b + 1) * 16] = jnp.where(is_here[b], source[0:16], after)
        double = dot_lanes(window[...], x_high[...])
        single = dot_lanes(window[0 : PLANES * 16], x_low[...])
        out = double[0 : PLANES * 16] + double[PLANES * 16 :] + single
        out = out.reshape(PLANES, 16, K)
        grid[:, base : base + 16, :] += out

    above = around(slab, 1, SLABS)
    below = jnp.where(slab == 0, SLABS - 1, slab - 1)

    def halo_copies(piece):
        rows = pl.ds(*DONE[piece])
        up = pltpu.make_async_remote_copy(
            src_ref=planes.at[pl.ds(6, 3), rows], dst_ref=from_below.at[:, rows],
            send_sem=halo_send.at[0, piece], recv_sem=halo_recv.at[0, piece],
            device_id=(above, atom), device_id_type=MESH,
        )
        down = pltpu.make_async_remote_copy(
            src_ref=planes.at[pl.ds(0, 2), rows], dst_ref=from_above.at[:, rows],
            send_sem=halo_send.at[1, piece], recv_sem=halo_recv.at[1, piece],
            device_id=(below, atom), device_id_type=MESH,
        )
        return up, down

    def spread_piece(piece):
        for step in (1, 3, 2):
            atom_copy(piece, step).wait_recv()
        weigh(piece)

        for tile in SPREAD[piece]:
            spread(tile)
        start, size = DONE[piece]
        planes[:, start : start + size, :] = grid[:, SHIFT + start : SHIFT + start + size, :]
        for copy in halo_copies(piece):
            copy.start()
            pending.append(copy.wait_send)

    def x_copy(piece, half, step):
        rows = pl.ds(*DONE[piece])
        peer = around(atom, step, SHARDS)
        return pltpu.make_async_remote_copy(
            src_ref=x_out.at[half, peer, :, rows], dst_ref=x_in.at[half, atom, :, rows],
            send_sem=x_send.at[piece, half, step], recv_sem=x_recv.at[piece, half, SHARDS - step],
            device_id=(slab, peer), device_id_type=MESH,
        )

    def x_piece(piece):
        start, size = DONE[piece]
        rows = slice(start, start + size)
        for copy in halo_copies(piece):
            copy.wait_recv()
        real = jnp.concatenate(
            [
                planes[2, rows] + from_below[0, rows],
                planes[3, rows] + from_below[1, rows],
                planes[4, rows] + from_below[2, rows] + from_above[0, rows],
                planes[5, rows] + from_above[1, rows],
            ],
            axis=0,
        )
        high, low = halved(real)
        out = dot(high, tx[0]) + dot(low, tx[0]) + dot(high, tx[1])
        for half in range(2):
            for shard in range(SHARDS):
                block = out[2 * half * size : 2 * (half + 1) * size, shard * 128 : (shard + 1) * 128]
                x_out[half, shard, :, rows] = block.reshape(2, size, 128)

    def send_x(piece, half):
        for step in (2, 1, 3):
            x_copy(piece, half, step).start()
            pending.append(x_copy(piece, half, step).wait_send)

    spread_piece(0)
    spread_piece(1)
    spread_piece(2)
    spread_piece(3)
    for load in loads[4:]:
        load.wait()
    for piece in range(3):
        x_piece(piece)
        send_x(piece, 0)
    send_x(0, 1)
    x_piece(3)
    send_x(3, 0)
    for piece in range(1, PIECES):
        send_x(piece, 1)
    x_in[:, atom] = x_out[:, atom]

    lane = lax.broadcasted_iota(jnp.int32, (K, 128), 1)
    row8 = lax.broadcasted_iota(jnp.int32, (32, 8, 128), 1)

    def y_copy(half, mask):
        peer = across(mask)
        return pltpu.make_async_remote_copy(
            src_ref=y_out.at[half, peer],
            dst_ref=z_in.at[pl.ds(pl.multiple_of(slab * 16 + half * 8, 8), 8)],
            send_sem=y_send.at[half], recv_sem=y_recv.at[half],
            device_id=(peer, atom), device_id_type=MESH,
        )

    for half in range(2):
        for piece in range(PIECES):
            for step in (1, 3, 2):
                x_copy(piece, half, step).wait_recv()
        plain, turned = [], []
        for p in range(2):
            f = jnp.concatenate([x_in[half, shard, p] for shard in range(SHARDS)], axis=0)
            g = pltpu.roll(f, 64, 1)
            plain.append(f)
            turned.append(jnp.where(lane < 64, g, -g))
        both = jnp.concatenate([jnp.concatenate(plain, axis=1), jnp.concatenate(turned, axis=1)], axis=0)
        high, low = halved(both)
        out = dot(t[0], high) + dot(t[0], low) + dot(t[1], high)
        y0 = out[:, 0:128].reshape(32, 8, 128)
        y1 = out[:, 128:256].reshape(32, 8, 128)
        even = jnp.where(row8 < 4, y0, pltpu.roll(y1, 4, 1))
        odd = jnp.where(row8 < 4, pltpu.roll(y0, 4, 1), y1)
        y_out[half] = jnp.stack([even, odd], axis=1).reshape(SLABS, 8, 128)
        for mask in FLIPS:
            y_copy(half, mask).start()
        z_in[pl.ds(pl.multiple_of(slab * 16 + half * 8, 8), 8)] = y_out[half, slab]

    def y_all(half):
        return pltpu.make_async_remote_copy(
            src_ref=z_in.at[pl.ds(0, 8 * (SLABS - 1))], dst_ref=z_in.at[pl.ds(0, 8 * (SLABS - 1))],
            send_sem=y_send.at[half], recv_sem=y_recv.at[half],
            device_id=(above, atom), device_id_type=MESH,
        )

    pending += [y_all(half).wait_send for half in range(2)]
    span_z, span_y, span_x = box[0], box[1], box[2]
    decay = -(math.pi**2) / beta**2
    ones = jnp.ones((8, K), F32)
    m_z = lanes_const[1:2] / (ones[0:1] * span_z)
    part_z = jnp.exp(decay * m_z * m_z) * lanes_const[0:1]
    own_x = rows_const[pl.ds(pl.multiple_of(atom * QUARTER, QUARTER), QUARTER)]
    m_x = own_x[:, 1:2] / (ones[0, 0] * span_x * jnp.ones((QUARTER, 1), F32))
    scale = jnp.ones((QUARTER, 1), F32) / (math.pi * span_z * span_y * span_x * jnp.ones((QUARTER, 1), F32))
    part_x = jnp.exp(decay * m_x * m_x) * own_x[:, 0:1] * scale
    part_xz = part_x * part_z
    msq_xz = m_x * m_x + m_z * m_z
    own_y = rows_const[pl.ds(pl.multiple_of((slab // 2) * 8, 8), 8)]
    kx_at = lax.broadcasted_iota(jnp.int32, (QUARTER, K), 0) + atom * QUARTER
    kz_at = lax.broadcasted_iota(jnp.int32, (QUARTER, K), 1)
    zero_xz = kx_at + kz_at

    m_ys = []
    for ky in range(DZ):
        y_row = jnp.where(lax.rem(slab, 2) == 0, own_y[ky : ky + 1], own_y[ky + 4 : ky + 5])
        m_y = y_row[:, 1:2] / (jnp.ones((1, 1), F32) * span_y)
        part_y = jnp.exp(decay * m_y * m_y) * y_row[:, 0:1]
        msq = msq_xz + m_y * m_y
        anchor = (zero_xz + (slab * DZ + ky)) == 0
        inverse = 1.0 / jnp.where(anchor, 1.0, msq)
        thetas[ky] = jnp.where(anchor, 0.0, part_xz * part_y * inverse)
        factors[ky] = inverse - decay
        m_ys.append(m_y)
    for half in range(2):
        y_all(half).wait_recv()

    sums = [jnp.zeros((1, K), F32) for _ in range(7)]
    for ky in range(DZ):
        f = z_in[pl.ds(ky, K, stride=4), :].T
        high, low = halved(f)
        out = dot(high, t[0]) + dot(low, t[0]) + dot(high, t[1])
        real = out[0:QUARTER, 0:K] + out[QUARTER:, K:]
        imag = out[QUARTER:, 0:K] - out[0:QUARTER, K:]
        theta, m_y = thetas[ky], m_ys[ky]
        result[0, ky] = theta * real
        result[1, ky] = theta * imag
        for c in range(2):
            put = pltpu.make_async_copy(result.at[c, ky], kfield.at[c, ky], out_sem.at[c, ky])
            put.start()
            pending.append(put.wait)
        double = theta * (real * real + imag * imag)
        u = double * factors[ky]
        u_x = u * m_x
        down_x = lambda x: jnp.sum(x, axis=0, keepdims=True)
        s_half, s_u = 0.5 * down_x(double), down_x(u)
        s_ux, s_uxx = down_x(u_x), down_x(u_x * m_x)
        s_uz = s_u * m_z
        terms = [
            s_half,
            s_half - s_uz * m_z,
            s_half - s_u * (m_y * m_y),
            s_half - s_uxx,
            -s_uz * m_y,
            -s_ux * m_z,
            -s_ux * m_y,
        ]
        sums = [a + b for a, b in zip(sums, terms)]
    lane_row = lax.broadcasted_iota(jnp.int32, (1, 128), 1)
    packed = jnp.zeros((1, 128), F32)
    for i, value in enumerate(sums):
        packed = jnp.where(lane_row == i, jnp.sum(value, axis=1, keepdims=True), packed)
    part[0] = packed

    def sum_copy(mask):
        peer = across(mask)
        return pltpu.make_async_remote_copy(
            src_ref=part.at[0], dst_ref=parts.at[slab],
            send_sem=sum_send, recv_sem=sum_recv, device_id=(peer, atom), device_id_type=MESH,
        )

    for mask in FLIPS:
        sum_copy(mask).start()
    parts[slab] = packed
    sum_all = pltpu.make_async_remote_copy(
        src_ref=parts.at[pl.ds(0, SLABS - 1)], dst_ref=parts.at[pl.ds(0, SLABS - 1)],
        send_sem=sum_send, recv_sem=sum_recv, device_id=(above, atom), device_id_type=MESH,
    )
    pending.append(sum_all.wait_send)
    sum_all.wait_recv()
    level = jnp.sum(parts[...], axis=0)
    middle[0] = level

    def mid_copy(step):
        peer = lax.rem(atom + step, SHARDS)
        return pltpu.make_async_remote_copy(
            src_ref=middle.at[0], dst_ref=middles.at[atom],
            send_sem=mid_send.at[step], recv_sem=mid_recv.at[SHARDS - step],
            device_id=(slab, peer), device_id_type=MESH,
        )

    for step in (2, 1, 3):
        mid_copy(step).start()
    middles[atom] = level

    for wait in pending:
        wait()
    for step in (1, 3, 2):
        mid_copy(step).wait_recv()
    whole = (middles[0] + middles[1]) + (middles[2] + middles[3])
    totals[...] = whole[:, 0:7] * (1.0 / (TILES * SLABS * SLOTS * SHARDS))
    for step in range(1, SHARDS):
        mid_copy(step).wait_send()


def body(cells, fractions, charges, counts, box):
    tx, t, rows_const, lanes_const = tables()
    vmem = pl.BlockSpec(memory_space=pltpu.VMEM)
    smem = pl.BlockSpec(memory_space=pltpu.SMEM)
    anywhere = pl.BlockSpec(memory_space=pl.ANY)
    hbm = pl.BlockSpec(memory_space=pltpu.HBM)
    dma = pltpu.SemaphoreType.DMA
    scratch = [
        pltpu.VMEM((3, TILES, SLOTS), jnp.int32),
        pltpu.VMEM((3, TILES, SLOTS), F32),
        pltpu.VMEM((TILES, SLOTS), F32),
        pltpu.VMEM((1, TILES), jnp.int32),
        pltpu.VMEM((K, 128), F32),
        pltpu.VMEM((8, K), F32),
        pltpu.VMEM((2, K, 2 * K), BF16),
        pltpu.VMEM((2, K, 2 * K), BF16),
        pltpu.VMEM((SHARDS, 18, 8, SLOTS), F32),
        pltpu.VMEM((SHARDS, 18, 8, SLOTS), F32),
        pltpu.VMEM((24, 8 * PIECES, LANES), F32),
        pltpu.VMEM((2, 2 * PLANES * 16, LANES), BF16),
        pltpu.VMEM((2, K, LANES), BF16),
        pltpu.VMEM((2, K, LANES), BF16),
        pltpu.VMEM((PLANES, ROWS, K), F32),
        pltpu.VMEM((PLANES, QUARTER, K), F32),
        pltpu.VMEM((3, QUARTER, K), F32),
        pltpu.VMEM((2, QUARTER, K), F32),
        pltpu.VMEM((2, SHARDS, 2, QUARTER, 128), F32),
        pltpu.VMEM((2, SHARDS, 2, QUARTER, 128), F32),
        pltpu.VMEM((2, SLABS, 8, 128), F32),
        pltpu.VMEM((SLABS * 16, 128), F32),
        pltpu.VMEM((DZ, QUARTER, K), F32),
        pltpu.VMEM((DZ, QUARTER, K), F32),
        pltpu.VMEM((2, DZ, QUARTER, K), F32),
        pltpu.VMEM((1, 1, 128), F32),
        pltpu.VMEM((SLABS, 1, 128), F32),
        pltpu.VMEM((1, 1, 128), F32),
        pltpu.VMEM((SHARDS, 1, 128), F32),
        dma((8,)), dma((PIECES, SHARDS)), dma((PIECES, SHARDS)), dma((2, PIECES)), dma((2, PIECES)),
        dma((PIECES, 2, SHARDS)), dma((PIECES, 2, SHARDS)),
        dma((2,)), dma((2,)), dma((2, DZ)), dma, dma, dma((SHARDS,)), dma((SHARDS,)),
    ]
    kfield, totals = pl.pallas_call(
        kernel,
        name="ewald",
        out_shape=(
            jax.ShapeDtypeStruct((2, DZ, QUARTER, K), F32),
            jax.ShapeDtypeStruct((1, 7), F32),
        ),
        in_specs=[hbm, hbm, hbm, hbm, smem, hbm, hbm, hbm, hbm],
        out_specs=(anywhere, vmem),
        scratch_shapes=scratch,
        compiler_params=pltpu.CompilerParams(collective_id=0, has_side_effects=True),
    )(cells, fractions, charges, counts.reshape(1, TILES), box, tx, t, rows_const, lanes_const)
    return kfield, totals.reshape(7)


def solution(mesh):
    placed = (P(None, "slab", "atom"), P(None, "slab", "atom"), P("slab", "atom"), P("slab", "atom"), P())
    return jax.shard_map(
        body,
        mesh=mesh,
        in_specs=placed,
        out_specs=(P(None, "slab", "atom", None), P()),
        check_vma=False,
    )
```

```python
import functools
import math

import jax
import jax.numpy as jnp
import numpy as np
from jax import lax
from jax.experimental import pallas as pl
from jax.experimental.pallas import tpu as pltpu
from jax.sharding import PartitionSpec as P

K = 256
TILES = 64
SLOTS = 128
SLABS = 64
SHARDS = 4
DZ = 4
QUARTER = 64
MAIN = 16
PLANES = 9
ROWS = 88
SHIFT = 10
LANES = SHARDS * SLOTS
PIECES = 4
BLOCKS = ((0, 5), (5, 4), (9, 4), (13, 5))
SPREAD = (range(-1, 3), range(3, 7), range(7, 11), range(11, 17))
DONE = ((0, 8), (8, 16), (24, 16), (40, 24))


def distance(mask):
    return sum((0, 1, 2, 1)[(mask >> low) & 3] for low in (2, 4)) + ((mask >> 1) & 1)


FLIPS = sorted(range(1, SLABS), key=lambda mask: -distance(mask))
beta = 1.25
F32 = jnp.float32
BF16 = jnp.bfloat16
MESH = pl.DeviceIdType.MESH


def tables():
    index = np.arange(K)
    angle = (index[:, None] * index[None, :] % K) * (2.0 * np.pi / K)
    cosine, sine = np.cos(angle), np.sin(angle)
    plain = np.concatenate([cosine, sine], axis=1)
    blocks = []
    for shard in range(SHARDS):
        cols = slice(shard * QUARTER, (shard + 1) * QUARTER)
        blocks += [cosine[:, cols], -sine[:, cols]]
    ordered = np.concatenate(blocks, axis=1)

    def halves(x):
        high = x.astype(np.float32).astype(jnp.bfloat16)
        low = (x - high.astype(np.float64)).astype(np.float32).astype(jnp.bfloat16)
        return np.stack([high, low])

    turn = 2.0 * np.pi * index / K
    modulus = (120.0 / (66.0 + 52.0 * np.cos(turn) + 2.0 * np.cos(2.0 * turn))) ** 2
    folded = np.where(index < K // 2, index, index - K)
    along_rows = np.zeros((K, 128), np.float32)
    along_rows[:, 0] = modulus
    along_rows[:, 1] = folded
    along_lanes = np.zeros((8, K), np.float32)
    along_lanes[0] = modulus
    along_lanes[1] = folded
    return halves(ordered), halves(plain), along_rows, along_lanes


def spline_weights(frac):
    prior = [jnp.ones_like(frac)]
    for order in range(2, 7):
        nxt = []
        for i in range(order):
            point = frac + i
            if i == 0:
                value = point * prior[0]
            elif i == order - 1:
                value = (order - point) * prior[i - 1]
            else:
                value = point * prior[i] + (order - point) * prior[i - 1]
            nxt.append(value * (1.0 / (order - 1)))
        prior = nxt
    return prior


def halved(x):
    high = x.astype(BF16)
    low = (x - high.astype(F32)).astype(BF16)
    return high, low


def dot(a, b):
    return jnp.dot(a, b, preferred_element_type=F32)


def dot_lanes(a, b):
    return lax.dot_general(a, b, (((1,), (1,)), ((), ())), preferred_element_type=F32)


def kernel(
    cells_hbm, fractions_hbm, charges_hbm, counts_hbm, box, tx_hbm, t_hbm, rows_hbm, lanes_hbm,
    kfield, totals,
    cells, fractions, charges, counts, rows_const, lanes_const,
    tx, t, send_atoms, atoms, splines, windows, x_highs, x_lows, grid, planes, from_below, from_above,
    x_out, x_in, y_out, z_in, thetas, factors, result, part, parts, middle, middles,
    table_sem, atom_send, atom_recv, halo_send, halo_recv, x_send, x_recv,
    y_send, y_recv, out_sem, sum_send, sum_recv, mid_send, mid_recv,
):
    slab = lax.axis_index("slab")
    atom = lax.axis_index("atom")

    def around(place, step, count):
        peer = place + step
        return jnp.where(peer >= count, peer - count, peer)

    pairs = [
        (cells_hbm, cells), (charges_hbm, charges), (counts_hbm, counts), (fractions_hbm, fractions),
        (tx_hbm, tx), (t_hbm, t), (rows_hbm, rows_const), (lanes_hbm, lanes_const),
    ]
    loads = [pltpu.make_async_copy(a, b, table_sem.at[i]) for i, (a, b) in enumerate(pairs)]
    for load in loads[:4]:
        load.start()
    barrier = pltpu.get_barrier_semaphore()
    for step in range(1, SHARDS):
        pl.semaphore_signal(barrier, inc=1, device_id=(slab, around(atom, step, SHARDS)), device_id_type=MESH)

    bits = [(1 - 2 * lax.rem(slab // (1 << b), 2)) * (1 << b) for b in range(6)]
    lower = [sum((bits[b] for b in range(3) if m >> b & 1), slab) for m in range(8)]
    upper = [sum((bits[b + 3] for b in range(3) if m >> b & 1), 0) for m in range(8)]

    def across(mask):
        return lower[mask % 8] + upper[mask // 8]

    for mask in FLIPS:
        pl.semaphore_signal(barrier, inc=1, device_id=(across(mask), atom), device_id_type=MESH)
    pending = []
    for load in loads[:4]:
        load.wait()

    slot = lax.broadcasted_iota(jnp.int32, (TILES, SLOTS), 1)
    tile_row = lax.broadcasted_iota(jnp.int32, (TILES, TILES), 0)
    tile_col = lax.broadcasted_iota(jnp.int32, (TILES, TILES), 1)
    diagonal = jnp.where(tile_row == tile_col, counts[...].astype(F32), 0.0)
    limit = jnp.sum(diagonal, axis=1, keepdims=True)
    weight = jnp.where(slot.astype(F32) < limit, charges[...], 0.0)
    fields = [cells[d].astype(F32) for d in range(3)] + [fractions[d] for d in range(3)] + [weight]
    spare = jnp.zeros((4, SLOTS), F32)
    for shard in range(SHARDS):
        for piece, (start, size) in enumerate(BLOCKS):
            first = shard * MAIN + 4 * piece
            cuts = [field[first : first + 4] for field in fields] + [spare]
            for pair in range(4):
                send_atoms[shard, start + pair] = jnp.concatenate(cuts[2 * pair : 2 * pair + 2], axis=0)
            if size == 5:
                at = (first - 1 if piece == 0 else first + 4) % TILES
                edge = [field[at : at + 1] for field in fields] + [spare[0:1]]
                send_atoms[shard, start + 4] = jnp.concatenate(edge, axis=0)
    pl.semaphore_wait(barrier, SHARDS - 1 + SLABS - 1)

    def atom_copy(piece, step):
        start, size = BLOCKS[piece]
        peer = around(atom, step, SHARDS)
        return pltpu.make_async_remote_copy(
            src_ref=send_atoms.at[peer, pl.ds(start, size)], dst_ref=atoms.at[atom, pl.ds(start, size)],
            send_sem=atom_send.at[piece, step], recv_sem=atom_recv.at[piece, SHARDS - step],
            device_id=(slab, peer), device_id_type=MESH,
        )

    for piece in range(PIECES):
        for step in (2, 1, 3):
            atom_copy(piece, step).start()
            pending.append(atom_copy(piece, step).wait_send)
    for load in loads[4:]:
        load.start()
    atoms[atom] = send_atoms[atom]
    grid[...] = jnp.zeros_like(grid)

    def weigh(piece):
        start, size = BLOCKS[piece]

        def gathered(number):
            row = 4 * (number % 2)
            main = [atoms[shard, start + number // 2, row : row + 4] for shard in range(SHARDS)]
            parts_of = [jnp.concatenate(main, axis=1)]
            if size == 5:
                edge = [atoms[shard, start + 4, number : number + 1] for shard in range(SHARDS)]
                parts_of.append(jnp.concatenate(edge, axis=1))
            parts_of.append(jnp.zeros((8 - size, LANES), F32))
            return jnp.concatenate(parts_of, axis=0)

        rows = slice(8 * piece, 8 * piece + 8)
        def within(cell):
            return cell - DZ * jnp.floor(cell * (1.0 / DZ))

        weights = gathered(6)
        along_z = [value * weights for value in spline_weights(gathered(3))]
        place = within(gathered(0))
        is_at = [place == c for c in range(DZ)]
        for p in range(PLANES):
            value = jnp.zeros((8, LANES), F32)
            for c in range(DZ):
                if 0 <= c + 5 - p <= 5:
                    value = jnp.where(is_at[c], along_z[c + 5 - p], value)
            splines[p, rows] = value
        for d in range(2):
            for i, value in enumerate(spline_weights(gathered(4 + d))):
                splines[PLANES + 6 * d + i, rows] = value
        splines[21, rows] = within(gathered(1)) + 5.0
        first = gathered(2) - 2.0
        first = jnp.where(first < 0.0, first + K, first)
        block = jnp.floor(first * (1.0 / 16.0))
        splines[22, rows] = block
        splines[23, rows] = first - 16.0 * block

    row16 = lax.broadcasted_iota(jnp.int32, (16, LANES), 0).astype(F32)
    row24 = lax.broadcasted_iota(jnp.int32, (24, LANES), 0).astype(F32)

    def spread(tile):
        at = {-1: 4, MAIN: 28}.get(tile, 8 * (tile // 4) + tile % 4)
        base = ((tile + 2) // 2) * 8
        offset = 4.0 * (tile % 2)
        window, x_high, x_low = windows.at[tile % 2], x_highs.at[tile % 2], x_lows.at[tile % 2]

        def row(number):
            return splines[number, at : at + 1, :]

        near_y = (row(21) + offset) - row16
        table_y = jnp.zeros((16, LANES), F32)
        for i in range(6):
            table_y = jnp.where(near_y == i, row(PLANES + i), table_y)
        for p in range(PLANES):
            high, low = halved(row(p) * table_y)
            window[p * 16 : (p + 1) * 16] = high
            window[PLANES * 16 + p * 16 : PLANES * 16 + (p + 1) * 16] = low
        past = row24 - row(23)
        small = jnp.zeros((24, LANES), F32)
        for j in range(6):
            small = jnp.where(past == j, row(PLANES + 6 + 5 - j), small)
        small = jnp.concatenate([small, jnp.zeros((8, LANES), F32)], axis=0)
        high, low = halved(small)
        where_block = jnp.broadcast_to(row(22), (16, LANES)).astype(BF16)
        nothing = jnp.zeros((16, LANES), BF16)
        is_here = [where_block == b for b in range(16)]
        for b in range(16):
            for source, target in ((high, x_high), (low, x_low)):
                after = jnp.where(is_here[(b - 1) % 16], source[16:32], nothing)
                target[b * 16 : (b + 1) * 16] = jnp.where(is_here[b], source[0:16], after)
        double = dot_lanes(window[...], x_high[...])
        single = dot_lanes(window[0 : PLANES * 16], x_low[...])
        out = double[0 : PLANES * 16] + double[PLANES * 16 :] + single
        out = out.reshape(PLANES, 16, K)
        grid[:, base : base + 16, :] += out

    above = around(slab, 1, SLABS)
    below = jnp.where(slab == 0, SLABS - 1, slab - 1)

    def halo_copies(piece):
        rows = pl.ds(*DONE[piece])
        up = pltpu.make_async_remote_copy(
            src_ref=planes.at[pl.ds(6, 3), rows], dst_ref=from_below.at[:, rows],
            send_sem=halo_send.at[0, piece], recv_sem=halo_recv.at[0, piece],
            device_id=(above, atom), device_id_type=MESH,
        )
        down = pltpu.make_async_remote_copy(
            src_ref=planes.at[pl.ds(0, 2), rows], dst_ref=from_above.at[:, rows],
            send_sem=halo_send.at[1, piece], recv_sem=halo_recv.at[1, piece],
            device_id=(below, atom), device_id_type=MESH,
        )
        return up, down

    def spread_piece(piece):
        for step in (1, 3, 2):
            atom_copy(piece, step).wait_recv()
        weigh(piece)

        for tile in SPREAD[piece]:
            spread(tile)
        start, size = DONE[piece]
        planes[:, start : start + size, :] = grid[:, SHIFT + start : SHIFT + start + size, :]
        for copy in halo_copies(piece):
            copy.start()
            pending.append(copy.wait_send)

    def x_copy(piece, half, step):
        rows = pl.ds(*DONE[piece])
        peer = around(atom, step, SHARDS)
        return pltpu.make_async_remote_copy(
            src_ref=x_out.at[half, peer, :, rows], dst_ref=x_in.at[half, atom, :, rows],
            send_sem=x_send.at[piece, half, step], recv_sem=x_recv.at[piece, half, SHARDS - step],
            device_id=(slab, peer), device_id_type=MESH,
        )

    def x_piece(piece):
        start, size = DONE[piece]
        rows = slice(start, start + size)
        for copy in halo_copies(piece):
            copy.wait_recv()
        real = jnp.concatenate(
            [
                planes[2, rows] + from_below[0, rows],
                planes[3, rows] + from_below[1, rows],
                planes[4, rows] + from_below[2, rows] + from_above[0, rows],
                planes[5, rows] + from_above[1, rows],
            ],
            axis=0,
        )
        high, low = halved(real)
        out = dot(high, tx[0]) + dot(low, tx[0]) + dot(high, tx[1])
        for half in range(2):
            for shard in range(SHARDS):
                block = out[2 * half * size : 2 * (half + 1) * size, shard * 128 : (shard + 1) * 128]
                x_out[half, shard, :, rows] = block.reshape(2, size, 128)

    def send_x(piece, half):
        for step in (2, 1, 3):
            x_copy(piece, half, step).start()
            pending.append(x_copy(piece, half, step).wait_send)

    spread_piece(0)
    spread_piece(1)
    spread_piece(2)
    spread_piece(3)
    for load in loads[4:]:
        load.wait()
    for piece in range(3):
        x_piece(piece)
        send_x(piece, 0)
    send_x(0, 1)
    x_piece(3)
    send_x(3, 0)
    for piece in range(1, PIECES):
        send_x(piece, 1)
    x_in[:, atom] = x_out[:, atom]

    lane = lax.broadcasted_iota(jnp.int32, (K, 128), 1)
    row8 = lax.broadcasted_iota(jnp.int32, (32, 8, 128), 1)

    def y_copy(half, mask):
        peer = across(mask)
        return pltpu.make_async_remote_copy(
            src_ref=y_out.at[half, peer],
            dst_ref=z_in.at[pl.ds(pl.multiple_of(slab * 16 + half * 8, 8), 8)],
            send_sem=y_send.at[half], recv_sem=y_recv.at[half],
            device_id=(peer, atom), device_id_type=MESH,
        )

    for half in range(2):
        for piece in range(PIECES):
            for step in (1, 3, 2):
                x_copy(piece, half, step).wait_recv()
        plain, turned = [], []
        for p in range(2):
            f = jnp.concatenate([x_in[half, shard, p] for shard in range(SHARDS)], axis=0)
            g = pltpu.roll(f, 64, 1)
            plain.append(f)
            turned.append(jnp.where(lane < 64, g, -g))
        both = jnp.concatenate([jnp.concatenate(plain, axis=1), jnp.concatenate(turned, axis=1)], axis=0)
        high, low = halved(both)
        out = dot(t[0], high) + dot(t[0], low) + dot(t[1], high)
        y0 = out[:, 0:128].reshape(32, 8, 128)
        y1 = out[:, 128:256].reshape(32, 8, 128)
        even = jnp.where(row8 < 4, y0, pltpu.roll(y1, 4, 1))
        odd = jnp.where(row8 < 4, pltpu.roll(y0, 4, 1), y1)
        y_out[half] = jnp.stack([even, odd], axis=1).reshape(SLABS, 8, 128)
        for mask in FLIPS:
            y_copy(half, mask).start()
        z_in[pl.ds(pl.multiple_of(slab * 16 + half * 8, 8), 8)] = y_out[half, slab]

    def y_all(half):
        return pltpu.make_async_remote_copy(
            src_ref=z_in.at[pl.ds(0, 8 * (SLABS - 1))], dst_ref=z_in.at[pl.ds(0, 8 * (SLABS - 1))],
            send_sem=y_send.at[half], recv_sem=y_recv.at[half],
            device_id=(above, atom), device_id_type=MESH,
        )

    pending += [y_all(half).wait_send for half in range(2)]
    span_z, span_y, span_x = box[0], box[1], box[2]
    decay = -(math.pi**2) / beta**2
    ones = jnp.ones((8, K), F32)
    m_z = lanes_const[1:2] / (ones[0:1] * span_z)
    part_z = jnp.exp(decay * m_z * m_z) * lanes_const[0:1]
    own_x = rows_const[pl.ds(pl.multiple_of(atom * QUARTER, QUARTER), QUARTER)]
    m_x = own_x[:, 1:2] / (ones[0, 0] * span_x * jnp.ones((QUARTER, 1), F32))
    scale = jnp.ones((QUARTER, 1), F32) / (math.pi * span_z * span_y * span_x * jnp.ones((QUARTER, 1), F32))
    part_x = jnp.exp(decay * m_x * m_x) * own_x[:, 0:1] * scale
    part_xz = part_x * part_z
    msq_xz = m_x * m_x + m_z * m_z
    own_y = rows_const[pl.ds(pl.multiple_of((slab // 2) * 8, 8), 8)]
    kx_at = lax.broadcasted_iota(jnp.int32, (QUARTER, K), 0) + atom * QUARTER
    kz_at = lax.broadcasted_iota(jnp.int32, (QUARTER, K), 1)
    zero_xz = kx_at + kz_at

    m_ys = []
    for ky in range(DZ):
        y_row = jnp.where(lax.rem(slab, 2) == 0, own_y[ky : ky + 1], own_y[ky + 4 : ky + 5])
        m_y = y_row[:, 1:2] / (jnp.ones((1, 1), F32) * span_y)
        part_y = jnp.exp(decay * m_y * m_y) * y_row[:, 0:1]
        msq = msq_xz + m_y * m_y
        anchor = (zero_xz + (slab * DZ + ky)) == 0
        inverse = 1.0 / jnp.where(anchor, 1.0, msq)
        thetas[ky] = jnp.where(anchor, 0.0, part_xz * part_y * inverse)
        factors[ky] = inverse - decay
        m_ys.append(m_y)
    for half in range(2):
        y_all(half).wait_recv()

    puts = []
    sums = [jnp.zeros((1, K), F32) for _ in range(7)]
    for ky in range(DZ):
        f = z_in[pl.ds(ky, K, stride=4), :].T
        high, low = halved(f)
        out = dot(high, t[0]) + dot(low, t[0]) + dot(high, t[1])
        real = out[0:QUARTER, 0:K] + out[QUARTER:, K:]
        imag = out[QUARTER:, 0:K] - out[0:QUARTER, K:]
        theta, m_y = thetas[ky], m_ys[ky]
        result[0, ky] = theta * real
        result[1, ky] = theta * imag
        for c in range(2):
            puts.append(pltpu.make_async_copy(result.at[c, ky], kfield.at[c, ky], out_sem.at[c, ky]))
        double = theta * (real * real + imag * imag)
        u = double * factors[ky]
        u_x = u * m_x
        down_x = lambda x: jnp.sum(x, axis=0, keepdims=True)
        s_half, s_u = 0.5 * down_x(double), down_x(u)
        s_ux, s_uxx = down_x(u_x), down_x(u_x * m_x)
        s_uz = s_u * m_z
        terms = [
            s_half,
            s_half - s_uz * m_z,
            s_half - s_u * (m_y * m_y),
            s_half - s_uxx,
            -s_uz * m_y,
            -s_ux * m_z,
            -s_ux * m_y,
        ]
        sums = [a + b for a, b in zip(sums, terms)]
    lane_row = lax.broadcasted_iota(jnp.int32, (1, 128), 1)
    packed = jnp.zeros((1, 128), F32)
    for i, value in enumerate(sums):
        packed = jnp.where(lane_row == i, jnp.sum(value, axis=1, keepdims=True), packed)
    part[0] = packed

    def sum_copy(mask):
        peer = across(mask)
        return pltpu.make_async_remote_copy(
            src_ref=part.at[0], dst_ref=parts.at[slab],
            send_sem=sum_send, recv_sem=sum_recv, device_id=(peer, atom), device_id_type=MESH,
        )

    for mask in FLIPS:
        sum_copy(mask).start()
    for put in puts:
        put.start()
        pending.append(put.wait)
    parts[slab] = packed
    sum_all = pltpu.make_async_remote_copy(
        src_ref=parts.at[pl.ds(0, SLABS - 1)], dst_ref=parts.at[pl.ds(0, SLABS - 1)],
        send_sem=sum_send, recv_sem=sum_recv, device_id=(above, atom), device_id_type=MESH,
    )
    pending.append(sum_all.wait_send)
    sum_all.wait_recv()
    level = jnp.sum(parts[...], axis=0)
    middle[0] = level

    def mid_copy(step):
        peer = lax.rem(atom + step, SHARDS)
        return pltpu.make_async_remote_copy(
            src_ref=middle.at[0], dst_ref=middles.at[atom],
            send_sem=mid_send.at[step], recv_sem=mid_recv.at[SHARDS - step],
            device_id=(slab, peer), device_id_type=MESH,
        )

    for step in (2, 1, 3):
        mid_copy(step).start()
    middles[atom] = level

    for wait in pending:
        wait()
    for step in (1, 3, 2):
        mid_copy(step).wait_recv()
    whole = (middles[0] + middles[1]) + (middles[2] + middles[3])
    totals[...] = whole[:, 0:7] * (1.0 / (TILES * SLABS * SLOTS * SHARDS))
    for step in range(1, SHARDS):
        mid_copy(step).wait_send()


def body(cells, fractions, charges, counts, box):
    tx, t, rows_const, lanes_const = tables()
    vmem = pl.BlockSpec(memory_space=pltpu.VMEM)
    smem = pl.BlockSpec(memory_space=pltpu.SMEM)
    anywhere = pl.BlockSpec(memory_space=pl.ANY)
    hbm = pl.BlockSpec(memory_space=pltpu.HBM)
    dma = pltpu.SemaphoreType.DMA
    scratch = [
        pltpu.VMEM((3, TILES, SLOTS), jnp.int32),
        pltpu.VMEM((3, TILES, SLOTS), F32),
        pltpu.VMEM((TILES, SLOTS), F32),
        pltpu.VMEM((1, TILES), jnp.int32),
        pltpu.VMEM((K, 128), F32),
        pltpu.VMEM((8, K), F32),
        pltpu.VMEM((2, K, 2 * K), BF16),
        pltpu.VMEM((2, K, 2 * K), BF16),
        pltpu.VMEM((SHARDS, 18, 8, SLOTS), F32),
        pltpu.VMEM((SHARDS, 18, 8, SLOTS), F32),
        pltpu.VMEM((24, 8 * PIECES, LANES), F32),
        pltpu.VMEM((2, 2 * PLANES * 16, LANES), BF16),
        pltpu.VMEM((2, K, LANES), BF16),
        pltpu.VMEM((2, K, LANES), BF16),
        pltpu.VMEM((PLANES, ROWS, K), F32),
        pltpu.VMEM((PLANES, QUARTER, K), F32),
        pltpu.VMEM((3, QUARTER, K), F32),
        pltpu.VMEM((2, QUARTER, K), F32),
        pltpu.VMEM((2, SHARDS, 2, QUARTER, 128), F32),
        pltpu.VMEM((2, SHARDS, 2, QUARTER, 128), F32),
        pltpu.VMEM((2, SLABS, 8, 128), F32),
        pltpu.VMEM((SLABS * 16, 128), F32),
        pltpu.VMEM((DZ, QUARTER, K), F32),
        pltpu.VMEM((DZ, QUARTER, K), F32),
        pltpu.VMEM((2, DZ, QUARTER, K), F32),
        pltpu.VMEM((1, 1, 128), F32),
        pltpu.VMEM((SLABS, 1, 128), F32),
        pltpu.VMEM((1, 1, 128), F32),
        pltpu.VMEM((SHARDS, 1, 128), F32),
        dma((8,)), dma((PIECES, SHARDS)), dma((PIECES, SHARDS)), dma((2, PIECES)), dma((2, PIECES)),
        dma((PIECES, 2, SHARDS)), dma((PIECES, 2, SHARDS)),
        dma((2,)), dma((2,)), dma((2, DZ)), dma, dma, dma((SHARDS,)), dma((SHARDS,)),
    ]
    arrays = (cells, fractions, charges, counts.reshape(1, TILES), box, tx, t, rows_const, lanes_const)
    inputs = [pltpu.with_memory_space_constraint(jnp.asarray(x), pltpu.HBM) for x in arrays]
    kfield, totals = pl.pallas_call(
        kernel,
        name="ewald",
        out_shape=(
            jax.ShapeDtypeStruct((2, DZ, QUARTER, K), F32),
            jax.ShapeDtypeStruct((1, 7), F32),
        ),
        in_specs=[hbm, hbm, hbm, hbm, smem, hbm, hbm, hbm, hbm],
        out_specs=(anywhere, vmem),
        scratch_shapes=scratch,
        compiler_params=pltpu.CompilerParams(collective_id=0, has_side_effects=True, vmem_limit_bytes=48 << 20),
    )(*inputs)
    return kfield, totals.reshape(7)


def solution(mesh):
    placed = (P(None, "slab", "atom"), P(None, "slab", "atom"), P("slab", "atom"), P("slab", "atom"), P())
    return jax.shard_map(
        body,
        mesh=mesh,
        in_specs=placed,
        out_specs=(P(None, "slab", "atom", None), P()),
        check_vma=False,
    )
```

```python
import functools
import math

import jax
import jax.numpy as jnp
import numpy as np
from jax import lax
from jax.experimental import pallas as pl
from jax.experimental.pallas import tpu as pltpu
from jax.sharding import PartitionSpec as P

K = 256
TILES = 64
SLOTS = 128
SLABS = 64
SHARDS = 4
DZ = 4
QUARTER = 64
MAIN = 16
PLANES = 9
ROWS = 88
SHIFT = 10
LANES = SHARDS * SLOTS
PIECES = 4
BLOCKS = ((0, 5), (5, 4), (9, 4), (13, 5))
SPREAD = (range(-1, 3), range(3, 7), range(7, 11), range(11, 17))
DONE = ((0, 8), (8, 16), (24, 16), (40, 24))


def distance(mask):
    return sum((0, 1, 2, 1)[(mask >> low) & 3] for low in (2, 4)) + ((mask >> 1) & 1)


FLIPS = sorted(range(1, SLABS), key=lambda mask: (-(mask >> 1 & 1), -distance(mask)))
beta = 1.25
F32 = jnp.float32
BF16 = jnp.bfloat16
MESH = pl.DeviceIdType.MESH


def tables():
    index = np.arange(K)
    angle = (index[:, None] * index[None, :] % K) * (2.0 * np.pi / K)
    cosine, sine = np.cos(angle), np.sin(angle)
    plain = np.concatenate([cosine, sine], axis=1)
    blocks = []
    for shard in range(SHARDS):
        cols = slice(shard * QUARTER, (shard + 1) * QUARTER)
        blocks += [cosine[:, cols], -sine[:, cols]]
    ordered = np.concatenate(blocks, axis=1)

    def halves(x):
        high = x.astype(np.float32).astype(jnp.bfloat16)
        low = (x - high.astype(np.float64)).astype(np.float32).astype(jnp.bfloat16)
        return np.stack([high, low])

    turn = 2.0 * np.pi * index / K
    modulus = (120.0 / (66.0 + 52.0 * np.cos(turn) + 2.0 * np.cos(2.0 * turn))) ** 2
    folded = np.where(index < K // 2, index, index - K)
    along_rows = np.zeros((K, 128), np.float32)
    along_rows[:, 0] = modulus
    along_rows[:, 1] = folded
    along_lanes = np.zeros((8, K), np.float32)
    along_lanes[0] = modulus
    along_lanes[1] = folded
    return halves(ordered), halves(plain), along_rows, along_lanes


def spline_weights(frac):
    prior = [jnp.ones_like(frac)]
    for order in range(2, 7):
        nxt = []
        for i in range(order):
            point = frac + i
            if i == 0:
                value = point * prior[0]
            elif i == order - 1:
                value = (order - point) * prior[i - 1]
            else:
                value = point * prior[i] + (order - point) * prior[i - 1]
            nxt.append(value * (1.0 / (order - 1)))
        prior = nxt
    return prior


def halved(x):
    high = x.astype(BF16)
    low = (x - high.astype(F32)).astype(BF16)
    return high, low


def dot(a, b):
    return jnp.dot(a, b, preferred_element_type=F32)


def dot_lanes(a, b):
    return lax.dot_general(a, b, (((1,), (1,)), ((), ())), preferred_element_type=F32)


def kernel(
    cells_hbm, fractions_hbm, charges_hbm, counts_hbm, box, tx_hbm, t_hbm, rows_hbm, lanes_hbm,
    kfield, totals,
    cells, fractions, charges, counts, rows_const, lanes_const,
    tx, t, send_atoms, atoms, splines, windows, x_highs, x_lows, grid, planes, from_below, from_above,
    x_out, x_in, y_out, z_in, thetas, factors, result, part, parts, middle, middles,
    table_sem, atom_send, atom_recv, halo_send, halo_recv, x_send, x_recv,
    y_send, y_recv, out_sem, sum_send, sum_recv, mid_send, mid_recv,
):
    slab = lax.axis_index("slab")
    atom = lax.axis_index("atom")

    def around(place, step, count):
        peer = place + step
        return jnp.where(peer >= count, peer - count, peer)

    pairs = [
        (cells_hbm, cells), (charges_hbm, charges), (counts_hbm, counts), (fractions_hbm, fractions),
        (tx_hbm, tx), (t_hbm, t), (rows_hbm, rows_const), (lanes_hbm, lanes_const),
    ]
    loads = [pltpu.make_async_copy(a, b, table_sem.at[i]) for i, (a, b) in enumerate(pairs)]
    for load in loads[:4]:
        load.start()
    barrier = pltpu.get_barrier_semaphore()
    for step in range(1, SHARDS):
        pl.semaphore_signal(barrier, inc=1, device_id=(slab, around(atom, step, SHARDS)), device_id_type=MESH)

    bits = [(1 - 2 * lax.rem(slab // (1 << b), 2)) * (1 << b) for b in range(6)]
    lower = [sum((bits[b] for b in range(3) if m >> b & 1), slab) for m in range(8)]
    upper = [sum((bits[b + 3] for b in range(3) if m >> b & 1), 0) for m in range(8)]

    def across(mask):
        return lower[mask % 8] + upper[mask // 8]

    for mask in FLIPS:
        pl.semaphore_signal(barrier, inc=1, device_id=(across(mask), atom), device_id_type=MESH)
    pending = []
    for load in loads[:4]:
        load.wait()

    slot = lax.broadcasted_iota(jnp.int32, (TILES, SLOTS), 1)
    tile_row = lax.broadcasted_iota(jnp.int32, (TILES, TILES), 0)
    tile_col = lax.broadcasted_iota(jnp.int32, (TILES, TILES), 1)
    diagonal = jnp.where(tile_row == tile_col, counts[...].astype(F32), 0.0)
    limit = jnp.sum(diagonal, axis=1, keepdims=True)
    weight = jnp.where(slot.astype(F32) < limit, charges[...], 0.0)
    fields = [cells[d].astype(F32) for d in range(3)] + [fractions[d] for d in range(3)] + [weight]
    spare = jnp.zeros((4, SLOTS), F32)
    for shard in range(SHARDS):
        for piece, (start, size) in enumerate(BLOCKS):
            first = shard * MAIN + 4 * piece
            cuts = [field[first : first + 4] for field in fields] + [spare]
            for pair in range(4):
                send_atoms[shard, start + pair] = jnp.concatenate(cuts[2 * pair : 2 * pair + 2], axis=0)
            if size == 5:
                at = (first - 1 if piece == 0 else first + 4) % TILES
                edge = [field[at : at + 1] for field in fields] + [spare[0:1]]
                send_atoms[shard, start + 4] = jnp.concatenate(edge, axis=0)
    pl.semaphore_wait(barrier, SHARDS - 1 + SLABS - 1)

    def atom_copy(piece, step):
        start, size = BLOCKS[piece]
        peer = around(atom, step, SHARDS)
        return pltpu.make_async_remote_copy(
            src_ref=send_atoms.at[peer, pl.ds(start, size)], dst_ref=atoms.at[atom, pl.ds(start, size)],
            send_sem=atom_send.at[piece, step], recv_sem=atom_recv.at[piece, SHARDS - step],
            device_id=(slab, peer), device_id_type=MESH,
        )

    for piece in range(PIECES):
        for step in (2, 1, 3):
            atom_copy(piece, step).start()
            pending.append(atom_copy(piece, step).wait_send)
    for load in loads[4:]:
        load.start()
    atoms[atom] = send_atoms[atom]
    grid[...] = jnp.zeros_like(grid)

    def weigh(piece):
        start, size = BLOCKS[piece]

        def gathered(number):
            row = 4 * (number % 2)
            main = [atoms[shard, start + number // 2, row : row + 4] for shard in range(SHARDS)]
            parts_of = [jnp.concatenate(main, axis=1)]
            if size == 5:
                edge = [atoms[shard, start + 4, number : number + 1] for shard in range(SHARDS)]
                parts_of.append(jnp.concatenate(edge, axis=1))
            parts_of.append(jnp.zeros((8 - size, LANES), F32))
            return jnp.concatenate(parts_of, axis=0)

        rows = slice(8 * piece, 8 * piece + 8)
        def within(cell):
            return cell - DZ * jnp.floor(cell * (1.0 / DZ))

        weights = gathered(6)
        along_z = [value * weights for value in spline_weights(gathered(3))]
        place = within(gathered(0))
        is_at = [place == c for c in range(DZ)]
        for p in range(PLANES):
            value = jnp.zeros((8, LANES), F32)
            for c in range(DZ):
                if 0 <= c + 5 - p <= 5:
                    value = jnp.where(is_at[c], along_z[c + 5 - p], value)
            splines[p, rows] = value
        for d in range(2):
            for i, value in enumerate(spline_weights(gathered(4 + d))):
                splines[PLANES + 6 * d + i, rows] = value
        splines[21, rows] = within(gathered(1)) + 5.0
        first = gathered(2) - 2.0
        first = jnp.where(first < 0.0, first + K, first)
        block = jnp.floor(first * (1.0 / 16.0))
        splines[22, rows] = block
        splines[23, rows] = first - 16.0 * block

    row16 = lax.broadcasted_iota(jnp.int32, (16, LANES), 0).astype(F32)
    row24 = lax.broadcasted_iota(jnp.int32, (24, LANES), 0).astype(F32)

    def spread(tile):
        at = {-1: 4, MAIN: 28}.get(tile, 8 * (tile // 4) + tile % 4)
        base = ((tile + 2) // 2) * 8
        offset = 4.0 * (tile % 2)
        window, x_high, x_low = windows.at[tile % 2], x_highs.at[tile % 2], x_lows.at[tile % 2]

        def row(number):
            return splines[number, at : at + 1, :]

        near_y = (row(21) + offset) - row16
        table_y = jnp.zeros((16, LANES), F32)
        for i in range(6):
            table_y = jnp.where(near_y == i, row(PLANES + i), table_y)
        for p in range(PLANES):
            high, low = halved(row(p) * table_y)
            window[p * 16 : (p + 1) * 16] = high
            window[PLANES * 16 + p * 16 : PLANES * 16 + (p + 1) * 16] = low
        past = row24 - row(23)
        small = jnp.zeros((24, LANES), F32)
        for j in range(6):
            small = jnp.where(past == j, row(PLANES + 6 + 5 - j), small)
        small = jnp.concatenate([small, jnp.zeros((8, LANES), F32)], axis=0)
        high, low = halved(small)
        where_block = jnp.broadcast_to(row(22), (16, LANES)).astype(BF16)
        nothing = jnp.zeros((16, LANES), BF16)
        is_here = [where_block == b for b in range(16)]
        for b in range(16):
            for source, target in ((high, x_high), (low, x_low)):
                after = jnp.where(is_here[(b - 1) % 16], source[16:32], nothing)
                target[b * 16 : (b + 1) * 16] = jnp.where(is_here[b], source[0:16], after)
        double = dot_lanes(window[...], x_high[...])
        single = dot_lanes(window[0 : PLANES * 16], x_low[...])
        out = double[0 : PLANES * 16] + double[PLANES * 16 :] + single
        out = out.reshape(PLANES, 16, K)
        grid[:, base : base + 16, :] += out

    above = around(slab, 1, SLABS)
    below = jnp.where(slab == 0, SLABS - 1, slab - 1)

    def halo_copies(piece):
        rows = pl.ds(*DONE[piece])
        up = pltpu.make_async_remote_copy(
            src_ref=planes.at[pl.ds(6, 3), rows], dst_ref=from_below.at[:, rows],
            send_sem=halo_send.at[0, piece], recv_sem=halo_recv.at[0, piece],
            device_id=(above, atom), device_id_type=MESH,
        )
        down = pltpu.make_async_remote_copy(
            src_ref=planes.at[pl.ds(0, 2), rows], dst_ref=from_above.at[:, rows],
            send_sem=halo_send.at[1, piece], recv_sem=halo_recv.at[1, piece],
            device_id=(below, atom), device_id_type=MESH,
        )
        return up, down

    def spread_piece(piece):
        for step in (1, 3, 2):
            atom_copy(piece, step).wait_recv()
        weigh(piece)

        for tile in SPREAD[piece]:
            spread(tile)
        start, size = DONE[piece]
        planes[:, start : start + size, :] = grid[:, SHIFT + start : SHIFT + start + size, :]
        for copy in halo_copies(piece):
            copy.start()
            pending.append(copy.wait_send)

    def x_copy(piece, half, step):
        rows = pl.ds(*DONE[piece])
        peer = around(atom, step, SHARDS)
        return pltpu.make_async_remote_copy(
            src_ref=x_out.at[half, peer, :, rows], dst_ref=x_in.at[half, atom, :, rows],
            send_sem=x_send.at[piece, half, step], recv_sem=x_recv.at[piece, half, SHARDS - step],
            device_id=(slab, peer), device_id_type=MESH,
        )

    def x_piece(piece):
        start, size = DONE[piece]
        rows = slice(start, start + size)
        for copy in halo_copies(piece):
            copy.wait_recv()
        real = jnp.concatenate(
            [
                planes[2, rows] + from_below[0, rows],
                planes[3, rows] + from_below[1, rows],
                planes[4, rows] + from_below[2, rows] + from_above[0, rows],
                planes[5, rows] + from_above[1, rows],
            ],
            axis=0,
        )
        high, low = halved(real)
        double = dot(jnp.concatenate([high, low], axis=0), tx[0])
        out = double[0 : 4 * size] + double[4 * size :] + dot(high, tx[1])
        for half in range(2):
            for shard in range(SHARDS):
                block = out[2 * half * size : 2 * (half + 1) * size, shard * 128 : (shard + 1) * 128]
                x_out[half, shard, :, rows] = block.reshape(2, size, 128)

    def send_x(piece, half):
        for step in (2, 1, 3):
            x_copy(piece, half, step).start()
            pending.append(x_copy(piece, half, step).wait_send)

    spread_piece(0)
    spread_piece(1)
    spread_piece(2)
    spread_piece(3)
    for load in loads[4:]:
        load.wait()
    for piece in range(3):
        x_piece(piece)
        send_x(piece, 0)
    send_x(0, 1)
    x_piece(3)
    send_x(3, 0)
    for piece in range(1, PIECES):
        send_x(piece, 1)
    x_in[:, atom] = x_out[:, atom]

    lane = lax.broadcasted_iota(jnp.int32, (K, 128), 1)
    row8 = lax.broadcasted_iota(jnp.int32, (16, 8, 128), 1)

    def y_copy(half, mask):
        peer = across(mask)
        return pltpu.make_async_remote_copy(
            src_ref=y_out.at[half, peer],
            dst_ref=z_in.at[pl.ds(pl.multiple_of(slab * 16 + half * 8, 8), 8)],
            send_sem=y_send.at[half], recv_sem=y_recv.at[half],
            device_id=(peer, atom), device_id_type=MESH,
        )

    for half in range(2):
        for piece in range(PIECES):
            for step in (1, 3, 2):
                x_copy(piece, half, step).wait_recv()
        plain, turned = [], []
        for p in range(2):
            f = jnp.concatenate([x_in[half, shard, p] for shard in range(SHARDS)], axis=0)
            g = pltpu.roll(f, 64, 1)
            plain.append(f)
            turned.append(jnp.where(lane < 64, g, -g))
        both = jnp.concatenate([jnp.concatenate(plain, axis=1), jnp.concatenate(turned, axis=1)], axis=0)
        high, low = halved(both)
        for other in (1, 0):
            side = slab // 32
            side = 1 - side if other else side
            rows = pl.ds(pl.multiple_of(side * 128, 128), 128)
            t_high, t_low = t[0, rows], t[1, rows]
            out = dot(t_high, high) + dot(t_high, low) + dot(t_low, high)
            y0 = out[:, 0:128].reshape(16, 8, 128)
            y1 = out[:, 128:256].reshape(16, 8, 128)
            even = jnp.where(row8 < 4, y0, pltpu.roll(y1, 4, 1))
            odd = jnp.where(row8 < 4, pltpu.roll(y0, 4, 1), y1)
            y_out[half, pl.ds(side * 32, 32)] = jnp.stack([even, odd], axis=1).reshape(32, 8, 128)
            for mask in FLIPS:
                if mask // 32 == other:
                    y_copy(half, mask).start()
        z_in[pl.ds(pl.multiple_of(slab * 16 + half * 8, 8), 8)] = y_out[half, slab]

    def y_all(half):
        return pltpu.make_async_remote_copy(
            src_ref=z_in.at[pl.ds(0, 8 * (SLABS - 1))], dst_ref=z_in.at[pl.ds(0, 8 * (SLABS - 1))],
            send_sem=y_send.at[half], recv_sem=y_recv.at[half],
            device_id=(above, atom), device_id_type=MESH,
        )

    pending += [y_all(half).wait_send for half in range(2)]
    span_z, span_y, span_x = box[0], box[1], box[2]
    decay = -(math.pi**2) / beta**2
    ones = jnp.ones((8, K), F32)
    m_z = lanes_const[1:2] / (ones[0:1] * span_z)
    part_z = jnp.exp(decay * m_z * m_z) * lanes_const[0:1]
    own_x = rows_const[pl.ds(pl.multiple_of(atom * QUARTER, QUARTER), QUARTER)]
    m_x = own_x[:, 1:2] / (ones[0, 0] * span_x * jnp.ones((QUARTER, 1), F32))
    scale = jnp.ones((QUARTER, 1), F32) / (math.pi * span_z * span_y * span_x * jnp.ones((QUARTER, 1), F32))
    part_x = jnp.exp(decay * m_x * m_x) * own_x[:, 0:1] * scale
    part_xz = part_x * part_z
    msq_xz = m_x * m_x + m_z * m_z
    own_y = rows_const[pl.ds(pl.multiple_of((slab // 2) * 8, 8), 8)]
    kx_at = lax.broadcasted_iota(jnp.int32, (QUARTER, K), 0) + atom * QUARTER
    kz_at = lax.broadcasted_iota(jnp.int32, (QUARTER, K), 1)
    zero_xz = kx_at + kz_at

    m_ys = []
    for ky in range(DZ):
        y_row = jnp.where(lax.rem(slab, 2) == 0, own_y[ky : ky + 1], own_y[ky + 4 : ky + 5])
        m_y = y_row[:, 1:2] / (jnp.ones((1, 1), F32) * span_y)
        part_y = jnp.exp(decay * m_y * m_y) * y_row[:, 0:1]
        msq = msq_xz + m_y * m_y
        anchor = (zero_xz + (slab * DZ + ky)) == 0
        inverse = 1.0 / jnp.where(anchor, 1.0, msq)
        thetas[ky] = jnp.where(anchor, 0.0, part_xz * part_y * inverse)
        factors[ky] = inverse - decay
        m_ys.append(m_y)
    for half in range(2):
        y_all(half).wait_recv()

    puts = []
    sums = [jnp.zeros((1, K), F32) for _ in range(7)]
    for ky in range(DZ):
        f = z_in[pl.ds(ky, K, stride=4), :].T
        high, low = halved(f)
        both = dot(jnp.concatenate([high, low], axis=0), t[0])
        out = both[0:128] + both[128:] + dot(high, t[1])
        real = out[0:QUARTER, 0:K] + out[QUARTER:, K:]
        imag = out[QUARTER:, 0:K] - out[0:QUARTER, K:]
        theta, m_y = thetas[ky], m_ys[ky]
        result[0, ky] = theta * real
        result[1, ky] = theta * imag
        for c in range(2):
            puts.append(pltpu.make_async_copy(result.at[c, ky], kfield.at[c, ky], out_sem.at[c, ky]))
        double = theta * (real * real + imag * imag)
        u = double * factors[ky]
        u_x = u * m_x
        down_x = lambda x: jnp.sum(x, axis=0, keepdims=True)
        s_half, s_u = 0.5 * down_x(double), down_x(u)
        s_ux, s_uxx = down_x(u_x), down_x(u_x * m_x)
        s_uz = s_u * m_z
        terms = [
            s_half,
            s_half - s_uz * m_z,
            s_half - s_u * (m_y * m_y),
            s_half - s_uxx,
            -s_uz * m_y,
            -s_ux * m_z,
            -s_ux * m_y,
        ]
        sums = [a + b for a, b in zip(sums, terms)]
    lane_row = lax.broadcasted_iota(jnp.int32, (1, 128), 1)
    packed = jnp.zeros((1, 128), F32)
    for i, value in enumerate(sums):
        packed = jnp.where(lane_row == i, jnp.sum(value, axis=1, keepdims=True), packed)
    part[0] = packed

    def sum_copy(mask):
        peer = across(mask)
        return pltpu.make_async_remote_copy(
            src_ref=part.at[0], dst_ref=parts.at[slab],
            send_sem=sum_send, recv_sem=sum_recv, device_id=(peer, atom), device_id_type=MESH,
        )

    for mask in FLIPS:
        sum_copy(mask).start()
    for put in puts:
        put.start()
        pending.append(put.wait)
    parts[slab] = packed
    sum_all = pltpu.make_async_remote_copy(
        src_ref=parts.at[pl.ds(0, SLABS - 1)], dst_ref=parts.at[pl.ds(0, SLABS - 1)],
        send_sem=sum_send, recv_sem=sum_recv, device_id=(above, atom), device_id_type=MESH,
    )
    pending.append(sum_all.wait_send)
    sum_all.wait_recv()
    level = jnp.sum(parts[...], axis=0)
    middle[0] = level

    def mid_copy(step):
        peer = lax.rem(atom + step, SHARDS)
        return pltpu.make_async_remote_copy(
            src_ref=middle.at[0], dst_ref=middles.at[atom],
            send_sem=mid_send.at[step], recv_sem=mid_recv.at[SHARDS - step],
            device_id=(slab, peer), device_id_type=MESH,
        )

    for step in (2, 1, 3):
        mid_copy(step).start()
    middles[atom] = level

    for wait in pending:
        wait()
    for step in (1, 3, 2):
        mid_copy(step).wait_recv()
    whole = (middles[0] + middles[1]) + (middles[2] + middles[3])
    totals[...] = whole[:, 0:7] * (1.0 / (TILES * SLABS * SLOTS * SHARDS))
    for step in range(1, SHARDS):
        mid_copy(step).wait_send()


def body(cells, fractions, charges, counts, box):
    tx, t, rows_const, lanes_const = tables()
    vmem = pl.BlockSpec(memory_space=pltpu.VMEM)
    smem = pl.BlockSpec(memory_space=pltpu.SMEM)
    anywhere = pl.BlockSpec(memory_space=pl.ANY)
    hbm = pl.BlockSpec(memory_space=pltpu.HBM)
    dma = pltpu.SemaphoreType.DMA
    scratch = [
        pltpu.VMEM((3, TILES, SLOTS), jnp.int32),
        pltpu.VMEM((3, TILES, SLOTS), F32),
        pltpu.VMEM((TILES, SLOTS), F32),
        pltpu.VMEM((1, TILES), jnp.int32),
        pltpu.VMEM((K, 128), F32),
        pltpu.VMEM((8, K), F32),
        pltpu.VMEM((2, K, 2 * K), BF16),
        pltpu.VMEM((2, K, 2 * K), BF16),
        pltpu.VMEM((SHARDS, 18, 8, SLOTS), F32),
        pltpu.VMEM((SHARDS, 18, 8, SLOTS), F32),
        pltpu.VMEM((24, 8 * PIECES, LANES), F32),
        pltpu.VMEM((2, 2 * PLANES * 16, LANES), BF16),
        pltpu.VMEM((2, K, LANES), BF16),
        pltpu.VMEM((2, K, LANES), BF16),
        pltpu.VMEM((PLANES, ROWS, K), F32),
        pltpu.VMEM((PLANES, QUARTER, K), F32),
        pltpu.VMEM((3, QUARTER, K), F32),
        pltpu.VMEM((2, QUARTER, K), F32),
        pltpu.VMEM((2, SHARDS, 2, QUARTER, 128), F32),
        pltpu.VMEM((2, SHARDS, 2, QUARTER, 128), F32),
        pltpu.VMEM((2, SLABS, 8, 128), F32),
        pltpu.VMEM((SLABS * 16, 128), F32),
        pltpu.VMEM((DZ, QUARTER, K), F32),
        pltpu.VMEM((DZ, QUARTER, K), F32),
        pltpu.VMEM((2, DZ, QUARTER, K), F32),
        pltpu.VMEM((1, 1, 128), F32),
        pltpu.VMEM((SLABS, 1, 128), F32),
        pltpu.VMEM((1, 1, 128), F32),
        pltpu.VMEM((SHARDS, 1, 128), F32),
        dma((8,)), dma((PIECES, SHARDS)), dma((PIECES, SHARDS)), dma((2, PIECES)), dma((2, PIECES)),
        dma((PIECES, 2, SHARDS)), dma((PIECES, 2, SHARDS)),
        dma((2,)), dma((2,)), dma((2, DZ)), dma, dma, dma((SHARDS,)), dma((SHARDS,)),
    ]
    arrays = (cells, fractions, charges, counts.reshape(1, TILES), box, tx, t, rows_const, lanes_const)
    inputs = [pltpu.with_memory_space_constraint(jnp.asarray(x), pltpu.HBM) for x in arrays]
    kfield, totals = pl.pallas_call(
        kernel,
        name="ewald",
        out_shape=(
            jax.ShapeDtypeStruct((2, DZ, QUARTER, K), F32),
            jax.ShapeDtypeStruct((1, 7), F32),
        ),
        in_specs=[hbm, hbm, hbm, hbm, smem, hbm, hbm, hbm, hbm],
        out_specs=(anywhere, vmem),
        scratch_shapes=scratch,
        compiler_params=pltpu.CompilerParams(collective_id=0, has_side_effects=True, vmem_limit_bytes=48 << 20),
    )(*inputs)
    return kfield, totals.reshape(7)


def solution(mesh):
    placed = (P(None, "slab", "atom"), P(None, "slab", "atom"), P("slab", "atom"), P("slab", "atom"), P())
    return jax.shard_map(
        body,
        mesh=mesh,
        in_specs=placed,
        out_specs=(P(None, "slab", "atom", None), P()),
        check_vma=False,
    )
```

```python
import functools
import math

import jax
import jax.numpy as jnp
import numpy as np
from jax import lax
from jax.experimental import pallas as pl
from jax.experimental.pallas import tpu as pltpu
from jax.sharding import PartitionSpec as P

K = 256
TILES = 64
SLOTS = 128
SLABS = 64
SHARDS = 4
DZ = 4
QUARTER = 64
MAIN = 16
PLANES = 9
ROWS = 88
SHIFT = 10
LANES = SHARDS * SLOTS
PIECES = 4
BLOCKS = ((0, 5), (5, 4), (9, 4), (13, 5))
SPREAD = (range(-1, 3), range(3, 7), range(7, 11), range(11, 17))
DONE = ((0, 8), (8, 16), (24, 16), (40, 24))


def distance(mask):
    return sum((0, 1, 2, 1)[(mask >> low) & 3] for low in (2, 4)) + ((mask >> 1) & 1)


FLIPS = sorted(range(1, SLABS), key=lambda mask: (-(mask >> 1 & 1), -distance(mask)))
beta = 1.25
F32 = jnp.float32
BF16 = jnp.bfloat16
MESH = pl.DeviceIdType.MESH


def tables():
    index = np.arange(K)
    angle = (index[:, None] * index[None, :] % K) * (2.0 * np.pi / K)
    cosine, sine = np.cos(angle), np.sin(angle)
    plain = np.concatenate([cosine, sine], axis=1)
    blocks = []
    for shard in range(SHARDS):
        cols = slice(shard * QUARTER, (shard + 1) * QUARTER)
        blocks += [cosine[:, cols], -sine[:, cols]]
    ordered = np.concatenate(blocks, axis=1)

    def halves(x):
        high = x.astype(np.float32).astype(jnp.bfloat16)
        low = (x - high.astype(np.float64)).astype(np.float32).astype(jnp.bfloat16)
        return np.stack([high, low])

    turn = 2.0 * np.pi * index / K
    modulus = (120.0 / (66.0 + 52.0 * np.cos(turn) + 2.0 * np.cos(2.0 * turn))) ** 2
    folded = np.where(index < K // 2, index, index - K)
    along_rows = np.zeros((K, 128), np.float32)
    along_rows[:, 0] = modulus
    along_rows[:, 1] = folded
    along_lanes = np.zeros((8, K), np.float32)
    along_lanes[0] = modulus
    along_lanes[1] = folded
    return halves(ordered), halves(plain), along_rows, along_lanes


def spline_weights(frac):
    prior = [jnp.ones_like(frac)]
    for order in range(2, 7):
        nxt = []
        for i in range(order):
            point = frac + i
            if i == 0:
                value = point * prior[0]
            elif i == order - 1:
                value = (order - point) * prior[i - 1]
            else:
                value = point * prior[i] + (order - point) * prior[i - 1]
            nxt.append(value * (1.0 / (order - 1)))
        prior = nxt
    return prior


def halved(x):
    high = x.astype(BF16)
    low = (x - high.astype(F32)).astype(BF16)
    return high, low


def dot(a, b):
    return jnp.dot(a, b, preferred_element_type=F32)


def dot_lanes(a, b):
    return lax.dot_general(a, b, (((1,), (1,)), ((), ())), preferred_element_type=F32)


def kernel(
    cells_hbm, fractions_hbm, charges_hbm, counts_hbm, box, tx_hbm, t_hbm, rows_hbm, lanes_hbm,
    kfield, totals,
    cells, fractions, charges, counts, rows_const, lanes_const,
    tx, t, send_atoms, atoms, splines, windows, x_highs, x_lows, grid, planes, from_below, from_above,
    x_out, x_in, y_out, z_in, thetas, factors, result, part, parts, middle, middles,
    table_sem, atom_send, atom_recv, halo_send, halo_recv, x_send, x_recv,
    y_send, y_recv, out_sem, sum_send, sum_recv, mid_send, mid_recv,
):
    slab = lax.axis_index("slab")
    atom = lax.axis_index("atom")

    def around(place, step, count):
        peer = place + step
        return jnp.where(peer >= count, peer - count, peer)

    pairs = [
        (cells_hbm, cells), (charges_hbm, charges), (counts_hbm, counts), (fractions_hbm, fractions),
        (tx_hbm, tx), (t_hbm, t), (rows_hbm, rows_const), (lanes_hbm, lanes_const),
    ]
    loads = [pltpu.make_async_copy(a, b, table_sem.at[i]) for i, (a, b) in enumerate(pairs)]
    for load in loads[:4]:
        load.start()
    barrier = pltpu.get_barrier_semaphore()
    for step in range(1, SHARDS):
        pl.semaphore_signal(barrier, inc=1, device_id=(slab, around(atom, step, SHARDS)), device_id_type=MESH)

    bits = [(1 - 2 * lax.rem(slab // (1 << b), 2)) * (1 << b) for b in range(6)]
    lower = [sum((bits[b] for b in range(3) if m >> b & 1), slab) for m in range(8)]
    upper = [sum((bits[b + 3] for b in range(3) if m >> b & 1), 0) for m in range(8)]

    def across(mask):
        return lower[mask % 8] + upper[mask // 8]

    for mask in FLIPS:
        pl.semaphore_signal(barrier, inc=1, device_id=(across(mask), atom), device_id_type=MESH)
    pending = []
    for load in loads[:4]:
        load.wait()

    slot = lax.broadcasted_iota(jnp.int32, (TILES, SLOTS), 1)
    tile_row = lax.broadcasted_iota(jnp.int32, (TILES, TILES), 0)
    tile_col = lax.broadcasted_iota(jnp.int32, (TILES, TILES), 1)
    diagonal = jnp.where(tile_row == tile_col, counts[...].astype(F32), 0.0)
    limit = jnp.sum(diagonal, axis=1, keepdims=True)
    weight = jnp.where(slot.astype(F32) < limit, charges[...], 0.0)
    fields = [cells[d].astype(F32) for d in range(3)] + [fractions[d] for d in range(3)] + [weight]
    spare = jnp.zeros((4, SLOTS), F32)
    for shard in range(SHARDS):
        for piece, (start, size) in enumerate(BLOCKS):
            first = shard * MAIN + 4 * piece
            cuts = [field[first : first + 4] for field in fields] + [spare]
            for pair in range(4):
                send_atoms[shard, start + pair] = jnp.concatenate(cuts[2 * pair : 2 * pair + 2], axis=0)
            if size == 5:
                at = (first - 1 if piece == 0 else first + 4) % TILES
                edge = [field[at : at + 1] for field in fields] + [spare[0:1]]
                send_atoms[shard, start + 4] = jnp.concatenate(edge, axis=0)
    pl.semaphore_wait(barrier, SHARDS - 1 + SLABS - 1)

    def atom_copy(piece, step):
        start, size = BLOCKS[piece]
        peer = around(atom, step, SHARDS)
        return pltpu.make_async_remote_copy(
            src_ref=send_atoms.at[peer, pl.ds(start, size)], dst_ref=atoms.at[atom, pl.ds(start, size)],
            send_sem=atom_send.at[piece, step], recv_sem=atom_recv.at[piece, SHARDS - step],
            device_id=(slab, peer), device_id_type=MESH,
        )

    for piece in range(PIECES):
        for step in (2, 1, 3):
            atom_copy(piece, step).start()
            pending.append(atom_copy(piece, step).wait_send)
    for load in loads[4:]:
        load.start()
    atoms[atom] = send_atoms[atom]
    grid[...] = jnp.zeros_like(grid)

    def weigh(piece):
        start, size = BLOCKS[piece]

        def gathered(number):
            row = 4 * (number % 2)
            main = [atoms[shard, start + number // 2, row : row + 4] for shard in range(SHARDS)]
            parts_of = [jnp.concatenate(main, axis=1)]
            if size == 5:
                edge = [atoms[shard, start + 4, number : number + 1] for shard in range(SHARDS)]
                parts_of.append(jnp.concatenate(edge, axis=1))
            parts_of.append(jnp.zeros((8 - size, LANES), F32))
            return jnp.concatenate(parts_of, axis=0)

        rows = slice(8 * piece, 8 * piece + 8)
        def within(cell):
            return cell - DZ * jnp.floor(cell * (1.0 / DZ))

        weights = gathered(6)
        along_z = [value * weights for value in spline_weights(gathered(3))]
        place = within(gathered(0))
        is_at = [place == c for c in range(DZ)]
        for p in range(PLANES):
            value = jnp.zeros((8, LANES), F32)
            for c in range(DZ):
                if 0 <= c + 5 - p <= 5:
                    value = jnp.where(is_at[c], along_z[c + 5 - p], value)
            splines[p, rows] = value
        for d in range(2):
            for i, value in enumerate(spline_weights(gathered(4 + d))):
                splines[PLANES + 6 * d + i, rows] = value
        splines[21, rows] = within(gathered(1)) + 5.0
        first = gathered(2) - 2.0
        first = jnp.where(first < 0.0, first + K, first)
        block = jnp.floor(first * (1.0 / 16.0))
        splines[22, rows] = block
        splines[23, rows] = first - 16.0 * block

    row16 = lax.broadcasted_iota(jnp.int32, (16, LANES), 0).astype(F32)
    row24 = lax.broadcasted_iota(jnp.int32, (24, LANES), 0).astype(F32)

    def spread(tile):
        at = {-1: 4, MAIN: 28}.get(tile, 8 * (tile // 4) + tile % 4)
        base = ((tile + 2) // 2) * 8
        offset = 4.0 * (tile % 2)
        window, x_high, x_low = windows.at[tile % 2], x_highs.at[tile % 2], x_lows.at[tile % 2]

        def row(number):
            return splines[number, at : at + 1, :]

        near_y = (row(21) + offset) - row16
        table_y = jnp.zeros((16, LANES), F32)
        for i in range(6):
            table_y = jnp.where(near_y == i, row(PLANES + i), table_y)
        for p in range(PLANES):
            high, low = halved(row(p) * table_y)
            window[p * 16 : (p + 1) * 16] = high
            window[PLANES * 16 + p * 16 : PLANES * 16 + (p + 1) * 16] = low
        past = row24 - row(23)
        small = jnp.zeros((24, LANES), F32)
        for j in range(6):
            small = jnp.where(past == j, row(PLANES + 6 + 5 - j), small)
        small = jnp.concatenate([small, jnp.zeros((8, LANES), F32)], axis=0)
        high, low = halved(small)
        where_block = jnp.broadcast_to(row(22), (16, LANES)).astype(BF16)
        nothing = jnp.zeros((16, LANES), BF16)
        is_here = [where_block == b for b in range(16)]
        for b in range(16):
            for source, target in ((high, x_high), (low, x_low)):
                after = jnp.where(is_here[(b - 1) % 16], source[16:32], nothing)
                target[b * 16 : (b + 1) * 16] = jnp.where(is_here[b], source[0:16], after)
        double = dot_lanes(window[...], x_high[...])
        single = dot_lanes(window[0 : PLANES * 16], x_low[...])
        out = double[0 : PLANES * 16] + double[PLANES * 16 :] + single
        out = out.reshape(PLANES, 16, K)
        grid[:, base : base + 16, :] += out

    above = around(slab, 1, SLABS)
    below = jnp.where(slab == 0, SLABS - 1, slab - 1)

    def halo_copies(piece):
        rows = pl.ds(*DONE[piece])
        up = pltpu.make_async_remote_copy(
            src_ref=planes.at[pl.ds(6, 3), rows], dst_ref=from_below.at[:, rows],
            send_sem=halo_send.at[0, piece], recv_sem=halo_recv.at[0, piece],
            device_id=(above, atom), device_id_type=MESH,
        )
        down = pltpu.make_async_remote_copy(
            src_ref=planes.at[pl.ds(0, 2), rows], dst_ref=from_above.at[:, rows],
            send_sem=halo_send.at[1, piece], recv_sem=halo_recv.at[1, piece],
            device_id=(below, atom), device_id_type=MESH,
        )
        return up, down

    def spread_piece(piece):
        for step in (1, 3, 2):
            atom_copy(piece, step).wait_recv()
        weigh(piece)

        for tile in SPREAD[piece]:
            spread(tile)
        start, size = DONE[piece]
        planes[:, start : start + size, :] = grid[:, SHIFT + start : SHIFT + start + size, :]
        for copy in halo_copies(piece):
            copy.start()
            pending.append(copy.wait_send)

    def x_copy(piece, half, step):
        rows = pl.ds(*DONE[piece])
        peer = around(atom, step, SHARDS)
        return pltpu.make_async_remote_copy(
            src_ref=x_out.at[half, peer, :, rows], dst_ref=x_in.at[half, atom, :, rows],
            send_sem=x_send.at[piece, half, step], recv_sem=x_recv.at[piece, half, SHARDS - step],
            device_id=(slab, peer), device_id_type=MESH,
        )

    def x_piece(piece):
        start, size = DONE[piece]
        rows = slice(start, start + size)
        for copy in halo_copies(piece):
            copy.wait_recv()
        real = jnp.concatenate(
            [
                planes[2, rows] + from_below[0, rows],
                planes[3, rows] + from_below[1, rows],
                planes[4, rows] + from_below[2, rows] + from_above[0, rows],
                planes[5, rows] + from_above[1, rows],
            ],
            axis=0,
        )
        high, low = halved(real)
        double = dot(jnp.concatenate([high, low], axis=0), tx[0])
        out = double[0 : 4 * size] + double[4 * size :] + dot(high, tx[1])
        for half in range(2):
            for shard in range(SHARDS):
                block = out[2 * half * size : 2 * (half + 1) * size, shard * 128 : (shard + 1) * 128]
                x_out[half, shard, :, rows] = block.reshape(2, size, 128)

    def send_x(piece, half):
        for step in (2, 1, 3):
            x_copy(piece, half, step).start()
            pending.append(x_copy(piece, half, step).wait_send)

    spread_piece(0)
    spread_piece(1)
    spread_piece(2)
    spread_piece(3)
    for load in loads[4:]:
        load.wait()
    for piece in range(3):
        x_piece(piece)
        send_x(piece, 0)
    send_x(0, 1)
    x_piece(3)
    send_x(3, 0)
    for piece in range(1, PIECES):
        send_x(piece, 1)
    x_in[:, atom] = x_out[:, atom]

    lane = lax.broadcasted_iota(jnp.int32, (K, 128), 1)
    row8 = lax.broadcasted_iota(jnp.int32, (16, 8, 128), 1)

    def y_copy(half, mask):
        peer = across(mask)
        return pltpu.make_async_remote_copy(
            src_ref=y_out.at[half, peer],
            dst_ref=z_in.at[pl.ds(pl.multiple_of(slab * 16 + half * 8, 8), 8)],
            send_sem=y_send.at[half], recv_sem=y_recv.at[half],
            device_id=(peer, atom), device_id_type=MESH,
        )

    for half in range(2):
        for piece in range(PIECES):
            for step in (1, 3, 2):
                x_copy(piece, half, step).wait_recv()
        plain, turned = [], []
        for p in range(2):
            f = jnp.concatenate([x_in[half, shard, p] for shard in range(SHARDS)], axis=0)
            g = pltpu.roll(f, 64, 1)
            plain.append(f)
            turned.append(jnp.where(lane < 64, g, -g))
        both = jnp.concatenate([jnp.concatenate(plain, axis=1), jnp.concatenate(turned, axis=1)], axis=0)
        high, low = halved(both)
        for other in (1, 0):
            side = slab // 32
            side = 1 - side if other else side
            rows = pl.ds(pl.multiple_of(side * 128, 128), 128)
            t_high, t_low = t[0, rows], t[1, rows]
            out = dot(t_high, high) + dot(t_high, low) + dot(t_low, high)
            y0 = out[:, 0:128].reshape(16, 8, 128)
            y1 = out[:, 128:256].reshape(16, 8, 128)
            even = jnp.where(row8 < 4, y0, pltpu.roll(y1, 4, 1))
            odd = jnp.where(row8 < 4, pltpu.roll(y0, 4, 1), y1)
            y_out[half, pl.ds(side * 32, 32)] = jnp.stack([even, odd], axis=1).reshape(32, 8, 128)
            for mask in FLIPS:
                if mask // 32 == other:
                    y_copy(half, mask).start()
        z_in[pl.ds(pl.multiple_of(slab * 16 + half * 8, 8), 8)] = y_out[half, slab]

    def y_all(half):
        return pltpu.make_async_remote_copy(
            src_ref=z_in.at[pl.ds(0, 8 * (SLABS - 1))], dst_ref=z_in.at[pl.ds(0, 8 * (SLABS - 1))],
            send_sem=y_send.at[half], recv_sem=y_recv.at[half],
            device_id=(above, atom), device_id_type=MESH,
        )

    pending += [y_all(half).wait_send for half in range(2)]
    span_z, span_y, span_x = box[0], box[1], box[2]
    decay = -(math.pi**2) / beta**2
    ones = jnp.ones((8, K), F32)
    m_z = lanes_const[1:2] / (ones[0:1] * span_z)
    part_z = jnp.exp(decay * m_z * m_z) * lanes_const[0:1]
    own_x = rows_const[pl.ds(pl.multiple_of(atom * QUARTER, QUARTER), QUARTER)]
    m_x = own_x[:, 1:2] / (ones[0, 0] * span_x * jnp.ones((QUARTER, 1), F32))
    scale = jnp.ones((QUARTER, 1), F32) / (math.pi * span_z * span_y * span_x * jnp.ones((QUARTER, 1), F32))
    part_x = jnp.exp(decay * m_x * m_x) * own_x[:, 0:1] * scale
    part_xz = part_x * part_z
    msq_xz = m_x * m_x + m_z * m_z
    own_y = rows_const[pl.ds(pl.multiple_of((slab // 2) * 8, 8), 8)]
    kx_at = lax.broadcasted_iota(jnp.int32, (QUARTER, K), 0) + atom * QUARTER
    kz_at = lax.broadcasted_iota(jnp.int32, (QUARTER, K), 1)
    zero_xz = kx_at + kz_at

    m_ys = []
    for ky in range(DZ):
        y_row = jnp.where(lax.rem(slab, 2) == 0, own_y[ky : ky + 1], own_y[ky + 4 : ky + 5])
        m_y = y_row[:, 1:2] / (jnp.ones((1, 1), F32) * span_y)
        part_y = jnp.exp(decay * m_y * m_y) * y_row[:, 0:1]
        msq = msq_xz + m_y * m_y
        anchor = (zero_xz + (slab * DZ + ky)) == 0
        inverse = 1.0 / jnp.where(anchor, 1.0, msq)
        thetas[ky] = jnp.where(anchor, 0.0, part_xz * part_y * inverse)
        factors[ky] = inverse - decay
        m_ys.append(m_y)
    for half in range(2):
        y_all(half).wait_recv()

    puts = []
    sums = [jnp.zeros((1, K), F32) for _ in range(7)]
    for ky in range(DZ):
        f = z_in[pl.ds(ky, K, stride=4), :].T
        high, low = halved(f)
        both = dot(jnp.concatenate([high, low], axis=0), t[0])
        out = both[0:128] + both[128:] + dot(high, t[1])
        real = out[0:QUARTER, 0:K] + out[QUARTER:, K:]
        imag = out[QUARTER:, 0:K] - out[0:QUARTER, K:]
        theta, m_y = thetas[ky], m_ys[ky]
        result[0, ky] = theta * real
        result[1, ky] = theta * imag
        for c in range(2):
            puts.append(pltpu.make_async_copy(result.at[c, ky], kfield.at[c, ky], out_sem.at[c, ky]))
        double = theta * (real * real + imag * imag)
        u = double * factors[ky]
        u_x = u * m_x
        down_x = lambda x: jnp.sum(x, axis=0, keepdims=True)
        s_half, s_u = 0.5 * down_x(double), down_x(u)
        s_ux, s_uxx = down_x(u_x), down_x(u_x * m_x)
        s_uz = s_u * m_z
        terms = [
            s_half,
            s_half - s_uz * m_z,
            s_half - s_u * (m_y * m_y),
            s_half - s_uxx,
            -s_uz * m_y,
            -s_ux * m_z,
            -s_ux * m_y,
        ]
        sums = [a + b for a, b in zip(sums, terms)]
    lane_row = lax.broadcasted_iota(jnp.int32, (1, 128), 1)
    packed = jnp.zeros((1, 128), F32)
    for i, value in enumerate(sums):
        packed = jnp.where(lane_row == i, jnp.sum(value, axis=1, keepdims=True), packed)
    part[0] = packed

    def sum_copy(mask):
        peer = across(mask)
        return pltpu.make_async_remote_copy(
            src_ref=part.at[0], dst_ref=parts.at[slab],
            send_sem=sum_send, recv_sem=sum_recv, device_id=(peer, atom), device_id_type=MESH,
        )

    for mask in FLIPS:
        sum_copy(mask).start()
    for put in puts:
        put.start()
        pending.append(put.wait)
    parts[slab] = packed
    sum_all = pltpu.make_async_remote_copy(
        src_ref=parts.at[pl.ds(0, SLABS - 1)], dst_ref=parts.at[pl.ds(0, SLABS - 1)],
        send_sem=sum_send, recv_sem=sum_recv, device_id=(above, atom), device_id_type=MESH,
    )
    pending.append(sum_all.wait_send)
    sum_all.wait_recv()
    level = jnp.sum(parts[...], axis=0)
    middle[0] = level

    def mid_copy(step):
        peer = lax.rem(atom + step, SHARDS)
        return pltpu.make_async_remote_copy(
            src_ref=middle.at[0], dst_ref=middles.at[atom],
            send_sem=mid_send.at[step], recv_sem=mid_recv.at[SHARDS - step],
            device_id=(slab, peer), device_id_type=MESH,
        )

    for step in (2, 1, 3):
        mid_copy(step).start()
    middles[atom] = level

    for wait in pending:
        wait()
    for step in (1, 3, 2):
        mid_copy(step).wait_recv()
    whole = (middles[0] + middles[1]) + (middles[2] + middles[3])
    totals[...] = whole[:, 0:7] * (1.0 / (TILES * SLABS * SLOTS * SHARDS))
    for step in range(1, SHARDS):
        mid_copy(step).wait_send()


def put_out(kfield, totals, kfield_out, totals_out, sem):
    copies = [
        pltpu.make_async_copy(kfield, kfield_out, sem.at[0]),
        pltpu.make_async_copy(totals, totals_out, sem.at[1]),
    ]
    for copy in copies:
        copy.start()
    for copy in copies:
        copy.wait()


def body(cells, fractions, charges, counts, box):
    tx, t, rows_const, lanes_const = tables()
    vmem = pl.BlockSpec(memory_space=pltpu.VMEM)
    smem = pl.BlockSpec(memory_space=pltpu.SMEM)
    anywhere = pl.BlockSpec(memory_space=pl.ANY)
    hbm = pl.BlockSpec(memory_space=pltpu.HBM)
    dma = pltpu.SemaphoreType.DMA
    scratch = [
        pltpu.VMEM((3, TILES, SLOTS), jnp.int32),
        pltpu.VMEM((3, TILES, SLOTS), F32),
        pltpu.VMEM((TILES, SLOTS), F32),
        pltpu.VMEM((1, TILES), jnp.int32),
        pltpu.VMEM((K, 128), F32),
        pltpu.VMEM((8, K), F32),
        pltpu.VMEM((2, K, 2 * K), BF16),
        pltpu.VMEM((2, K, 2 * K), BF16),
        pltpu.VMEM((SHARDS, 18, 8, SLOTS), F32),
        pltpu.VMEM((SHARDS, 18, 8, SLOTS), F32),
        pltpu.VMEM((24, 8 * PIECES, LANES), F32),
        pltpu.VMEM((2, 2 * PLANES * 16, LANES), BF16),
        pltpu.VMEM((2, K, LANES), BF16),
        pltpu.VMEM((2, K, LANES), BF16),
        pltpu.VMEM((PLANES, ROWS, K), F32),
        pltpu.VMEM((PLANES, QUARTER, K), F32),
        pltpu.VMEM((3, QUARTER, K), F32),
        pltpu.VMEM((2, QUARTER, K), F32),
        pltpu.VMEM((2, SHARDS, 2, QUARTER, 128), F32),
        pltpu.VMEM((2, SHARDS, 2, QUARTER, 128), F32),
        pltpu.VMEM((2, SLABS, 8, 128), F32),
        pltpu.VMEM((SLABS * 16, 128), F32),
        pltpu.VMEM((DZ, QUARTER, K), F32),
        pltpu.VMEM((DZ, QUARTER, K), F32),
        pltpu.VMEM((2, DZ, QUARTER, K), F32),
        pltpu.VMEM((1, 1, 128), F32),
        pltpu.VMEM((SLABS, 1, 128), F32),
        pltpu.VMEM((1, 1, 128), F32),
        pltpu.VMEM((SHARDS, 1, 128), F32),
        dma((8,)), dma((PIECES, SHARDS)), dma((PIECES, SHARDS)), dma((2, PIECES)), dma((2, PIECES)),
        dma((PIECES, 2, SHARDS)), dma((PIECES, 2, SHARDS)),
        dma((2,)), dma((2,)), dma((2, DZ)), dma, dma, dma((SHARDS,)), dma((SHARDS,)),
    ]
    arrays = (cells, fractions, charges, counts.reshape(1, TILES), box, tx, t, rows_const, lanes_const)
    inputs = [pltpu.with_memory_space_constraint(jnp.asarray(x), pltpu.HBM) for x in arrays]
    kfield, totals = pl.pallas_call(
        kernel,
        name="ewald",
        out_shape=(
            jax.ShapeDtypeStruct((2, DZ, QUARTER, K), F32),
            jax.ShapeDtypeStruct((1, 7), F32),
        ),
        in_specs=[hbm, hbm, hbm, hbm, smem, hbm, hbm, hbm, hbm],
        out_specs=(anywhere, vmem),
        scratch_shapes=scratch,
        compiler_params=pltpu.CompilerParams(collective_id=0, has_side_effects=True, vmem_limit_bytes=48 << 20),
    )(*inputs)
    kfield, totals = pl.pallas_call(
        put_out,
        name="put_out",
        out_shape=(
            jax.ShapeDtypeStruct((2, DZ, QUARTER, K), F32),
            jax.ShapeDtypeStruct((1, 7), F32),
        ),
        in_specs=[anywhere, anywhere],
        out_specs=(hbm, hbm),
        scratch_shapes=[dma((2,))],
        compiler_params=pltpu.CompilerParams(vmem_limit_bytes=1 << 20),
    )(kfield, totals)
    return kfield, totals.reshape(7)


def solution(mesh):
    placed = (P(None, "slab", "atom"), P(None, "slab", "atom"), P("slab", "atom"), P("slab", "atom"), P())
    return jax.shard_map(
        body,
        mesh=mesh,
        in_specs=placed,
        out_specs=(P(None, "slab", "atom", None), P()),
        check_vma=False,
    )
```

```python
import functools
import math

import jax
import jax.numpy as jnp
import numpy as np
from jax import lax
from jax.experimental import pallas as pl
from jax.experimental.pallas import tpu as pltpu
from jax.sharding import PartitionSpec as P

K = 256
TILES = 64
SLOTS = 128
SLABS = 64
SHARDS = 4
DZ = 4
QUARTER = 64
MAIN = 16
PLANES = 9
ROWS = 88
SHIFT = 10
LANES = SHARDS * SLOTS
PIECES = 4
BLOCKS = ((0, 5), (5, 4), (9, 4), (13, 5))
SPREAD = (range(-1, 3), range(3, 7), range(7, 11), range(11, 17))
DONE = ((0, 8), (8, 16), (24, 16), (40, 24))


def distance(mask):
    return sum((0, 1, 2, 1)[(mask >> low) & 3] for low in (2, 4)) + ((mask >> 1) & 1)


FLIPS = sorted(range(1, SLABS), key=lambda mask: (-(mask >> 1 & 1), -distance(mask)))
beta = 1.25
F32 = jnp.float32
BF16 = jnp.bfloat16
MESH = pl.DeviceIdType.MESH


def tables():
    index = np.arange(K)
    angle = (index[:, None] * index[None, :] % K) * (2.0 * np.pi / K)
    cosine, sine = np.cos(angle), np.sin(angle)
    plain = np.concatenate([cosine, sine], axis=1)
    blocks = []
    for shard in range(SHARDS):
        cols = slice(shard * QUARTER, (shard + 1) * QUARTER)
        blocks += [cosine[:, cols], -sine[:, cols]]
    ordered = np.concatenate(blocks, axis=1)

    def halves(x):
        high = x.astype(np.float32).astype(jnp.bfloat16)
        low = (x - high.astype(np.float64)).astype(np.float32).astype(jnp.bfloat16)
        return np.stack([high, low])

    turn = 2.0 * np.pi * index / K
    modulus = (120.0 / (66.0 + 52.0 * np.cos(turn) + 2.0 * np.cos(2.0 * turn))) ** 2
    folded = np.where(index < K // 2, index, index - K)
    along_rows = np.zeros((K, 128), np.float32)
    along_rows[:, 0] = modulus
    along_rows[:, 1] = folded
    along_lanes = np.zeros((8, K), np.float32)
    along_lanes[0] = modulus
    along_lanes[1] = folded
    return halves(ordered), halves(plain), along_rows, along_lanes


def spline_weights(frac):
    prior = [jnp.ones_like(frac)]
    for order in range(2, 7):
        nxt = []
        for i in range(order):
            point = frac + i
            if i == 0:
                value = point * prior[0]
            elif i == order - 1:
                value = (order - point) * prior[i - 1]
            else:
                value = point * prior[i] + (order - point) * prior[i - 1]
            nxt.append(value * (1.0 / (order - 1)))
        prior = nxt
    return prior


def halved(x):
    high = x.astype(BF16)
    low = (x - high.astype(F32)).astype(BF16)
    return high, low


def dot(a, b):
    return jnp.dot(a, b, preferred_element_type=F32)


def dot_lanes(a, b):
    return lax.dot_general(a, b, (((1,), (1,)), ((), ())), preferred_element_type=F32)


def kernel(
    cells_hbm, fractions_hbm, charges_hbm, counts_hbm, box, tx_hbm, t_hbm, rows_hbm, lanes_hbm,
    kfield, totals,
    cells, fractions, charges, counts, rows_const, lanes_const,
    tx, t, send_atoms, atoms, splines, windows, x_highs, x_lows, grid, planes, from_below, from_above,
    x_out, x_in, y_out, z_in, thetas, factors, result, part, parts, middle, middles,
    table_sem, atom_send, atom_recv, halo_send, halo_recv, x_send, x_recv,
    y_send, y_recv, out_sem, sum_send, sum_recv, mid_send, mid_recv,
):
    slab = lax.axis_index("slab")
    atom = lax.axis_index("atom")

    def around(place, step, count):
        peer = place + step
        return jnp.where(peer >= count, peer - count, peer)

    pairs = [
        (cells_hbm, cells), (charges_hbm, charges), (counts_hbm, counts), (fractions_hbm, fractions),
        (tx_hbm, tx), (t_hbm, t), (rows_hbm, rows_const), (lanes_hbm, lanes_const),
    ]
    loads = [pltpu.make_async_copy(a, b, table_sem.at[i]) for i, (a, b) in enumerate(pairs)]
    for load in loads[:4]:
        load.start()
    barrier = pltpu.get_barrier_semaphore()
    for step in range(1, SHARDS):
        pl.semaphore_signal(barrier, inc=1, device_id=(slab, around(atom, step, SHARDS)), device_id_type=MESH)

    bits = [(1 - 2 * lax.rem(slab // (1 << b), 2)) * (1 << b) for b in range(6)]
    lower = [sum((bits[b] for b in range(3) if m >> b & 1), slab) for m in range(8)]
    upper = [sum((bits[b + 3] for b in range(3) if m >> b & 1), 0) for m in range(8)]

    def across(mask):
        return lower[mask % 8] + upper[mask // 8]

    for mask in FLIPS:
        pl.semaphore_signal(barrier, inc=1, device_id=(across(mask), atom), device_id_type=MESH)
    pending = []
    for load in loads[:4]:
        load.wait()

    slot = lax.broadcasted_iota(jnp.int32, (TILES, SLOTS), 1)
    tile_row = lax.broadcasted_iota(jnp.int32, (TILES, TILES), 0)
    tile_col = lax.broadcasted_iota(jnp.int32, (TILES, TILES), 1)
    diagonal = jnp.where(tile_row == tile_col, counts[...].astype(F32), 0.0)
    limit = jnp.sum(diagonal, axis=1, keepdims=True)
    weight = jnp.where(slot.astype(F32) < limit, charges[...], 0.0)
    fields = [cells[d].astype(F32) for d in range(3)] + [fractions[d] for d in range(3)] + [weight]
    spare = jnp.zeros((4, SLOTS), F32)
    for shard in range(SHARDS):
        for piece, (start, size) in enumerate(BLOCKS):
            first = shard * MAIN + 4 * piece
            cuts = [field[first : first + 4] for field in fields] + [spare]
            for pair in range(4):
                send_atoms[shard, start + pair] = jnp.concatenate(cuts[2 * pair : 2 * pair + 2], axis=0)
            if size == 5:
                at = (first - 1 if piece == 0 else first + 4) % TILES
                edge = [field[at : at + 1] for field in fields] + [spare[0:1]]
                send_atoms[shard, start + 4] = jnp.concatenate(edge, axis=0)
    pl.semaphore_wait(barrier, SHARDS - 1 + SLABS - 1)

    def atom_copy(piece, step):
        start, size = BLOCKS[piece]
        peer = around(atom, step, SHARDS)
        return pltpu.make_async_remote_copy(
            src_ref=send_atoms.at[peer, pl.ds(start, size)], dst_ref=atoms.at[atom, pl.ds(start, size)],
            send_sem=atom_send.at[piece, step], recv_sem=atom_recv.at[piece, SHARDS - step],
            device_id=(slab, peer), device_id_type=MESH,
        )

    for piece in range(PIECES):
        for step in (2, 1, 3):
            atom_copy(piece, step).start()
            pending.append(atom_copy(piece, step).wait_send)
    atoms[atom] = send_atoms[atom]
    grid[...] = jnp.zeros_like(grid)

    def weigh(piece):
        start, size = BLOCKS[piece]

        def gathered(number):
            row = 4 * (number % 2)
            main = [atoms[shard, start + number // 2, row : row + 4] for shard in range(SHARDS)]
            parts_of = [jnp.concatenate(main, axis=1)]
            if size == 5:
                edge = [atoms[shard, start + 4, number : number + 1] for shard in range(SHARDS)]
                parts_of.append(jnp.concatenate(edge, axis=1))
            parts_of.append(jnp.zeros((8 - size, LANES), F32))
            return jnp.concatenate(parts_of, axis=0)

        rows = slice(8 * piece, 8 * piece + 8)
        def within(cell):
            return cell - DZ * jnp.floor(cell * (1.0 / DZ))

        weights = gathered(6)
        along_z = [value * weights for value in spline_weights(gathered(3))]
        place = within(gathered(0))
        is_at = [place == c for c in range(DZ)]
        for p in range(PLANES):
            value = jnp.zeros((8, LANES), F32)
            for c in range(DZ):
                if 0 <= c + 5 - p <= 5:
                    value = jnp.where(is_at[c], along_z[c + 5 - p], value)
            splines[p, rows] = value
        for d in range(2):
            for i, value in enumerate(spline_weights(gathered(4 + d))):
                splines[PLANES + 6 * d + i, rows] = value
        splines[21, rows] = within(gathered(1)) + 5.0
        first = gathered(2) - 2.0
        first = jnp.where(first < 0.0, first + K, first)
        block = jnp.floor(first * (1.0 / 16.0))
        splines[22, rows] = block
        splines[23, rows] = first - 16.0 * block

    row16 = lax.broadcasted_iota(jnp.int32, (16, LANES), 0).astype(F32)
    row24 = lax.broadcasted_iota(jnp.int32, (24, LANES), 0).astype(F32)

    def spread(tile):
        at = {-1: 4, MAIN: 28}.get(tile, 8 * (tile // 4) + tile % 4)
        base = ((tile + 2) // 2) * 8
        offset = 4.0 * (tile % 2)
        window, x_high, x_low = windows.at[tile % 2], x_highs.at[tile % 2], x_lows.at[tile % 2]

        def row(number):
            return splines[number, at : at + 1, :]

        near_y = (row(21) + offset) - row16
        table_y = jnp.zeros((16, LANES), F32)
        for i in range(6):
            table_y = jnp.where(near_y == i, row(PLANES + i), table_y)
        for p in range(PLANES):
            high, low = halved(row(p) * table_y)
            window[p * 16 : (p + 1) * 16] = high
            window[PLANES * 16 + p * 16 : PLANES * 16 + (p + 1) * 16] = low
        past = row24 - row(23)
        small = jnp.zeros((24, LANES), F32)
        for j in range(6):
            small = jnp.where(past == j, row(PLANES + 6 + 5 - j), small)
        small = jnp.concatenate([small, jnp.zeros((8, LANES), F32)], axis=0)
        high, low = halved(small)
        where_block = jnp.broadcast_to(row(22), (16, LANES)).astype(BF16)
        nothing = jnp.zeros((16, LANES), BF16)
        is_here = [where_block == b for b in range(16)]
        for b in range(16):
            for source, target in ((high, x_high), (low, x_low)):
                after = jnp.where(is_here[(b - 1) % 16], source[16:32], nothing)
                target[b * 16 : (b + 1) * 16] = jnp.where(is_here[b], source[0:16], after)
        double = dot_lanes(window[...], x_high[...])
        single = dot_lanes(window[0 : PLANES * 16], x_low[...])
        out = double[0 : PLANES * 16] + double[PLANES * 16 :] + single
        out = out.reshape(PLANES, 16, K)
        grid[:, base : base + 16, :] += out

    above = around(slab, 1, SLABS)
    below = jnp.where(slab == 0, SLABS - 1, slab - 1)

    def halo_copies(piece):
        rows = pl.ds(*DONE[piece])
        up = pltpu.make_async_remote_copy(
            src_ref=planes.at[pl.ds(6, 3), rows], dst_ref=from_below.at[:, rows],
            send_sem=halo_send.at[0, piece], recv_sem=halo_recv.at[0, piece],
            device_id=(above, atom), device_id_type=MESH,
        )
        down = pltpu.make_async_remote_copy(
            src_ref=planes.at[pl.ds(0, 2), rows], dst_ref=from_above.at[:, rows],
            send_sem=halo_send.at[1, piece], recv_sem=halo_recv.at[1, piece],
            device_id=(below, atom), device_id_type=MESH,
        )
        return up, down

    def spread_piece(piece):
        for step in (1, 3, 2):
            atom_copy(piece, step).wait_recv()
        weigh(piece)

        for tile in SPREAD[piece]:
            spread(tile)
        start, size = DONE[piece]
        ranges = (slice(6, 9), slice(0, 2))
        for copy, part_of in zip(halo_copies(piece), ranges):
            planes[part_of, start : start + size, :] = grid[part_of, SHIFT + start : SHIFT + start + size, :]
            copy.start()
            pending.append(copy.wait_send)
        planes[2:6, start : start + size, :] = grid[2:6, SHIFT + start : SHIFT + start + size, :]

    def x_copy(piece, half, step):
        rows = pl.ds(*DONE[piece])
        peer = around(atom, step, SHARDS)
        return pltpu.make_async_remote_copy(
            src_ref=x_out.at[half, peer, :, rows], dst_ref=x_in.at[half, atom, :, rows],
            send_sem=x_send.at[piece, half, step], recv_sem=x_recv.at[piece, half, SHARDS - step],
            device_id=(slab, peer), device_id_type=MESH,
        )

    def x_piece(piece):
        start, size = DONE[piece]
        rows = slice(start, start + size)
        for copy in halo_copies(piece):
            copy.wait_recv()
        real = jnp.concatenate(
            [
                planes[2, rows] + from_below[0, rows],
                planes[3, rows] + from_below[1, rows],
                planes[4, rows] + from_below[2, rows] + from_above[0, rows],
                planes[5, rows] + from_above[1, rows],
            ],
            axis=0,
        )
        high, low = halved(real)
        double = dot(jnp.concatenate([high, low], axis=0), tx[0])
        out = double[0 : 4 * size] + double[4 * size :] + dot(high, tx[1])
        for half in range(2):
            for shard in range(SHARDS):
                block = out[2 * half * size : 2 * (half + 1) * size, shard * 128 : (shard + 1) * 128]
                x_out[half, shard, :, rows] = block.reshape(2, size, 128)

    def send_x(piece, half):
        for step in (2, 1, 3):
            x_copy(piece, half, step).start()
            pending.append(x_copy(piece, half, step).wait_send)

    spread_piece(0)
    for load in loads[4:]:
        load.start()
    spread_piece(1)
    spread_piece(2)
    spread_piece(3)
    for load in loads[4:]:
        load.wait()
    for piece in range(3):
        x_piece(piece)
        send_x(piece, 0)
    send_x(0, 1)
    x_piece(3)
    send_x(3, 0)
    for piece in range(1, PIECES):
        send_x(piece, 1)
    x_in[:, atom] = x_out[:, atom]

    lane = lax.broadcasted_iota(jnp.int32, (K, 128), 1)
    row8 = lax.broadcasted_iota(jnp.int32, (16, 8, 128), 1)

    def y_copy(half, mask):
        peer = across(mask)
        return pltpu.make_async_remote_copy(
            src_ref=y_out.at[half, peer],
            dst_ref=z_in.at[pl.ds(pl.multiple_of(slab * 16 + half * 8, 8), 8)],
            send_sem=y_send.at[half], recv_sem=y_recv.at[half],
            device_id=(peer, atom), device_id_type=MESH,
        )

    for half in range(2):
        for piece in range(PIECES):
            for step in (1, 3, 2):
                x_copy(piece, half, step).wait_recv()
        plain, turned = [], []
        for p in range(2):
            f = jnp.concatenate([x_in[half, shard, p] for shard in range(SHARDS)], axis=0)
            g = pltpu.roll(f, 64, 1)
            plain.append(f)
            turned.append(jnp.where(lane < 64, g, -g))
        both = jnp.concatenate([jnp.concatenate(plain, axis=1), jnp.concatenate(turned, axis=1)], axis=0)
        high, low = halved(both)
        for other in (1, 0):
            side = slab // 32
            side = 1 - side if other else side
            rows = pl.ds(pl.multiple_of(side * 128, 128), 128)
            t_high, t_low = t[0, rows], t[1, rows]
            out = dot(t_high, high) + dot(t_high, low) + dot(t_low, high)
            y0 = out[:, 0:128].reshape(16, 8, 128)
            y1 = out[:, 128:256].reshape(16, 8, 128)
            even = jnp.where(row8 < 4, y0, pltpu.roll(y1, 4, 1))
            odd = jnp.where(row8 < 4, pltpu.roll(y0, 4, 1), y1)
            y_out[half, pl.ds(side * 32, 32)] = jnp.stack([even, odd], axis=1).reshape(32, 8, 128)
            for mask in FLIPS:
                if mask // 32 == other:
                    y_copy(half, mask).start()
        z_in[pl.ds(pl.multiple_of(slab * 16 + half * 8, 8), 8)] = y_out[half, slab]

    def y_all(half):
        return pltpu.make_async_remote_copy(
            src_ref=z_in.at[pl.ds(0, 8 * (SLABS - 1))], dst_ref=z_in.at[pl.ds(0, 8 * (SLABS - 1))],
            send_sem=y_send.at[half], recv_sem=y_recv.at[half],
            device_id=(above, atom), device_id_type=MESH,
        )

    pending += [y_all(half).wait_send for half in range(2)]
    span_z, span_y, span_x = box[0], box[1], box[2]
    decay = -(math.pi**2) / beta**2
    ones = jnp.ones((8, K), F32)
    m_z = lanes_const[1:2] / (ones[0:1] * span_z)
    part_z = jnp.exp(decay * m_z * m_z) * lanes_const[0:1]
    own_x = rows_const[pl.ds(pl.multiple_of(atom * QUARTER, QUARTER), QUARTER)]
    m_x = own_x[:, 1:2] / (ones[0, 0] * span_x * jnp.ones((QUARTER, 1), F32))
    scale = jnp.ones((QUARTER, 1), F32) / (math.pi * span_z * span_y * span_x * jnp.ones((QUARTER, 1), F32))
    part_x = jnp.exp(decay * m_x * m_x) * own_x[:, 0:1] * scale
    part_xz = part_x * part_z
    msq_xz = m_x * m_x + m_z * m_z
    own_y = rows_const[pl.ds(pl.multiple_of((slab // 2) * 8, 8), 8)]
    kx_at = lax.broadcasted_iota(jnp.int32, (QUARTER, K), 0) + atom * QUARTER
    kz_at = lax.broadcasted_iota(jnp.int32, (QUARTER, K), 1)
    zero_xz = kx_at + kz_at

    m_ys = []
    for ky in range(DZ):
        y_row = jnp.where(lax.rem(slab, 2) == 0, own_y[ky : ky + 1], own_y[ky + 4 : ky + 5])
        m_y = y_row[:, 1:2] / (jnp.ones((1, 1), F32) * span_y)
        part_y = jnp.exp(decay * m_y * m_y) * y_row[:, 0:1]
        msq = msq_xz + m_y * m_y
        anchor = (zero_xz + (slab * DZ + ky)) == 0
        inverse = 1.0 / jnp.where(anchor, 1.0, msq)
        thetas[ky] = jnp.where(anchor, 0.0, part_xz * part_y * inverse)
        factors[ky] = inverse - decay
        m_ys.append(m_y)
    for half in range(2):
        y_all(half).wait_recv()

    puts = []
    sums = [jnp.zeros((1, K), F32) for _ in range(7)]
    for ky in range(DZ):
        f = z_in[pl.ds(ky, K, stride=4), :].T
        high, low = halved(f)
        both = dot(jnp.concatenate([high, low], axis=0), t[0])
        out = both[0:128] + both[128:] + dot(high, t[1])
        real = out[0:QUARTER, 0:K] + out[QUARTER:, K:]
        imag = out[QUARTER:, 0:K] - out[0:QUARTER, K:]
        theta, m_y = thetas[ky], m_ys[ky]
        result[0, ky] = theta * real
        result[1, ky] = theta * imag
        for c in range(2):
            puts.append(pltpu.make_async_copy(result.at[c, ky], kfield.at[c, ky], out_sem.at[c, ky]))
        double = theta * (real * real + imag * imag)
        u = double * factors[ky]
        u_x = u * m_x
        down_x = lambda x: jnp.sum(x, axis=0, keepdims=True)
        s_half, s_u = 0.5 * down_x(double), down_x(u)
        s_ux, s_uxx = down_x(u_x), down_x(u_x * m_x)
        s_uz = s_u * m_z
        terms = [
            s_half,
            s_half - s_uz * m_z,
            s_half - s_u * (m_y * m_y),
            s_half - s_uxx,
            -s_uz * m_y,
            -s_ux * m_z,
            -s_ux * m_y,
        ]
        sums = [a + b for a, b in zip(sums, terms)]
    lane_row = lax.broadcasted_iota(jnp.int32, (1, 128), 1)
    packed = jnp.zeros((1, 128), F32)
    for i, value in enumerate(sums):
        packed = jnp.where(lane_row == i, jnp.sum(value, axis=1, keepdims=True), packed)
    part[0] = packed

    def sum_copy(mask):
        peer = across(mask)
        return pltpu.make_async_remote_copy(
            src_ref=part.at[0], dst_ref=parts.at[slab],
            send_sem=sum_send, recv_sem=sum_recv, device_id=(peer, atom), device_id_type=MESH,
        )

    for mask in FLIPS:
        sum_copy(mask).start()
    for put in puts:
        put.start()
        pending.append(put.wait)
    parts[slab] = packed
    sum_all = pltpu.make_async_remote_copy(
        src_ref=parts.at[pl.ds(0, SLABS - 1)], dst_ref=parts.at[pl.ds(0, SLABS - 1)],
        send_sem=sum_send, recv_sem=sum_recv, device_id=(above, atom), device_id_type=MESH,
    )
    pending.append(sum_all.wait_send)
    sum_all.wait_recv()
    level = jnp.sum(parts[...], axis=0)
    middle[0] = level

    def mid_copy(step):
        peer = lax.rem(atom + step, SHARDS)
        return pltpu.make_async_remote_copy(
            src_ref=middle.at[0], dst_ref=middles.at[atom],
            send_sem=mid_send.at[step], recv_sem=mid_recv.at[SHARDS - step],
            device_id=(slab, peer), device_id_type=MESH,
        )

    for step in (2, 1, 3):
        mid_copy(step).start()
    middles[atom] = level

    for wait in pending:
        wait()
    for step in (1, 3, 2):
        mid_copy(step).wait_recv()
    whole = (middles[0] + middles[1]) + (middles[2] + middles[3])
    totals[...] = whole[:, 0:7] * (1.0 / (TILES * SLABS * SLOTS * SHARDS))
    for step in range(1, SHARDS):
        mid_copy(step).wait_send()


def put_out(kfield, totals, kfield_out, totals_out, sem):
    copies = [
        pltpu.make_async_copy(kfield, kfield_out, sem.at[0]),
        pltpu.make_async_copy(totals, totals_out, sem.at[1]),
    ]
    for copy in copies:
        copy.start()
    for copy in copies:
        copy.wait()


def body(cells, fractions, charges, counts, box):
    tx, t, rows_const, lanes_const = tables()
    vmem = pl.BlockSpec(memory_space=pltpu.VMEM)
    smem = pl.BlockSpec(memory_space=pltpu.SMEM)
    anywhere = pl.BlockSpec(memory_space=pl.ANY)
    hbm = pl.BlockSpec(memory_space=pltpu.HBM)
    dma = pltpu.SemaphoreType.DMA
    scratch = [
        pltpu.VMEM((3, TILES, SLOTS), jnp.int32),
        pltpu.VMEM((3, TILES, SLOTS), F32),
        pltpu.VMEM((TILES, SLOTS), F32),
        pltpu.VMEM((1, TILES), jnp.int32),
        pltpu.VMEM((K, 128), F32),
        pltpu.VMEM((8, K), F32),
        pltpu.VMEM((2, K, 2 * K), BF16),
        pltpu.VMEM((2, K, 2 * K), BF16),
        pltpu.VMEM((SHARDS, 18, 8, SLOTS), F32),
        pltpu.VMEM((SHARDS, 18, 8, SLOTS), F32),
        pltpu.VMEM((24, 8 * PIECES, LANES), F32),
        pltpu.VMEM((2, 2 * PLANES * 16, LANES), BF16),
        pltpu.VMEM((2, K, LANES), BF16),
        pltpu.VMEM((2, K, LANES), BF16),
        pltpu.VMEM((PLANES, ROWS, K), F32),
        pltpu.VMEM((PLANES, QUARTER, K), F32),
        pltpu.VMEM((3, QUARTER, K), F32),
        pltpu.VMEM((2, QUARTER, K), F32),
        pltpu.VMEM((2, SHARDS, 2, QUARTER, 128), F32),
        pltpu.VMEM((2, SHARDS, 2, QUARTER, 128), F32),
        pltpu.VMEM((2, SLABS, 8, 128), F32),
        pltpu.VMEM((SLABS * 16, 128), F32),
        pltpu.VMEM((DZ, QUARTER, K), F32),
        pltpu.VMEM((DZ, QUARTER, K), F32),
        pltpu.VMEM((2, DZ, QUARTER, K), F32),
        pltpu.VMEM((1, 1, 128), F32),
        pltpu.VMEM((SLABS, 1, 128), F32),
        pltpu.VMEM((1, 1, 128), F32),
        pltpu.VMEM((SHARDS, 1, 128), F32),
        dma((8,)), dma((PIECES, SHARDS)), dma((PIECES, SHARDS)), dma((2, PIECES)), dma((2, PIECES)),
        dma((PIECES, 2, SHARDS)), dma((PIECES, 2, SHARDS)),
        dma((2,)), dma((2,)), dma((2, DZ)), dma, dma, dma((SHARDS,)), dma((SHARDS,)),
    ]
    arrays = (cells, fractions, charges, counts.reshape(1, TILES), box, tx, t, rows_const, lanes_const)
    inputs = [pltpu.with_memory_space_constraint(jnp.asarray(x), pltpu.HBM) for x in arrays]
    kfield, totals = pl.pallas_call(
        kernel,
        name="ewald",
        out_shape=(
            jax.ShapeDtypeStruct((2, DZ, QUARTER, K), F32),
            jax.ShapeDtypeStruct((1, 7), F32),
        ),
        in_specs=[hbm, hbm, hbm, hbm, smem, hbm, hbm, hbm, hbm],
        out_specs=(anywhere, vmem),
        scratch_shapes=scratch,
        compiler_params=pltpu.CompilerParams(collective_id=0, has_side_effects=True, vmem_limit_bytes=48 << 20),
    )(*inputs)
    kfield, totals = pl.pallas_call(
        put_out,
        name="put_out",
        out_shape=(
            jax.ShapeDtypeStruct((2, DZ, QUARTER, K), F32),
            jax.ShapeDtypeStruct((1, 7), F32),
        ),
        in_specs=[anywhere, anywhere],
        out_specs=(hbm, hbm),
        scratch_shapes=[dma((2,))],
        compiler_params=pltpu.CompilerParams(vmem_limit_bytes=1 << 20),
    )(kfield, totals)
    return kfield, totals.reshape(7)


def solution(mesh):
    placed = (P(None, "slab", "atom"), P(None, "slab", "atom"), P("slab", "atom"), P("slab", "atom"), P())
    return jax.shard_map(
        body,
        mesh=mesh,
        in_specs=placed,
        out_specs=(P(None, "slab", "atom", None), P()),
        check_vma=False,
    )
```
